32 devices in a mesh: groups: 2 (over y), chol: 4 (over z), walk: 2 (over x), orb: 2 (over core).
Axes of the slice: x: 2, y: 2, z: 4, core: 2. Of those that a mesh axis runs over, the one named last changes fastest.
Arguments:
- walkers: float32 [32, 2, 36864], P(('groups', 'walk'), None, ('chol', 'orb')), parts along dimension 0, may hold values from -6 to 6
- correlation_inverse: float32 [32, 2, 96, 96], P(('groups', 'walk')), parts along dimension 0, may hold values from -0.625 to 0.625
- half_vectors: bfloat16 [4096, 36864], P(('groups', 'walk'), ('chol', 'orb')), parts along dimension 0, may hold values from -0.01953125 to 0.01953125
- field_vectors: bfloat16 [4096, 384, 384], P(('groups', 'walk'), ('chol', 'orb')), parts along dimension 0, may hold values from -0.0048828125 to 0.0048828125
- samples: float32 [32, 2048], P('groups', 'walk'), parts along dimension 0, may hold values from -6 to 6
- source: int32 [32], P(('groups', 'walk')), parts along dimension 0, may hold values from 0 to 15
Outputs:
- walkers_next: float32 [32, 2, 36864], P(('groups', 'walk'), None, ('chol', 'orb')), parts along dimension 0
The draws below stay inside these ranges and needn't reach their ends.
There are 2 independent parts, one for each index of `groups`. The reference program is written for one: setup_inputs(seed, part) draws one part's arguments, and reference() takes and returns one part's arrays. A program takes and returns all parts, laid end to end along the dimension named above; each array names one. Nothing has to cross between parts.
All inputs are finite; a program needn't handle non-finite values.
Results may differ from the reference program's by a relative error of at most 0.02.
Values may be sent and summed in bfloat16 or wider, within the bound.
No kernel may reach another device: no remote copies, remote signals or barrier semaphores. Data moves between devices by JAX's collectives and lax.ppermute only.
A program may use at most 128 MiB of HBM per device.

```python
import math
import jax
import jax.numpy as jnp
import numpy as np
from jax import lax

M = 384
N = 96
G = 2048
TERMS = 4
NS_STEPS = 2
W = 16


def touch_ends(array, key, least, largest):
    index_at = [jax.random.randint(jax.random.fold_in(key, axis), (), 0, length) for axis, length in enumerate(array.shape)]
    main_axis = array.shape.index(max(array.shape))
    beside = index_at[:main_axis] + [(index_at[main_axis] + 1) % array.shape[main_axis]] + index_at[main_axis + 1:]
    return array.at[tuple(index_at)].set(least).at[tuple(beside)].set(largest)


def shard_levels(key, shape, shards, smallest, top_value):
    def one(dim, parts):
        draws = jax.random.uniform(jax.random.fold_in(jax.random.fold_in(key, 6), dim), (parts,), jnp.float32, smallest / len(shards), top_value / len(shards))
        return jnp.repeat(jnp.exp(draws), shape[dim] // parts).reshape((-1,) + (1,) * (len(shape) - dim - 1))

    factor_of = one(*shards[0])
    for cut in shards[1:]:
        factor_of = factor_of * one(*cut)
    return factor_of


def rank_table(amount, skew):
    loads = [(1 << 20) // math.isqrt(rank ** skew) + 1 for rank in range(1, amount + 1)]
    spread = 1 + sum(loads) // (1 << 30)
    return np.cumsum(np.array([max(1, weight // spread) for weight in loads]))


def ranked(key, dims, amount, skew):
    table = rank_table(amount, skew)
    pick = jax.random.randint(jax.random.fold_in(key, 1), dims, 0, int(table[amount - 1]))
    rank = jnp.searchsorted(jnp.asarray(table, jnp.int32), pick, side="right")
    return jax.random.permutation(jax.random.fold_in(key, 2), amount)[rank].astype(jnp.int32)


def bell_draw(stream_key, shape, scale, limit, shards=(), kind=jnp.bfloat16):
    drawn = jax.random.normal(stream_key, shape, jnp.float32) * scale
    if len(shards) > 0:
        drawn = shard_levels(stream_key, shape, shards, -0.22, 0.18) * drawn
    return jnp.clip(drawn, min=-limit, max=limit).astype(kind)


def setup_inputs(seed: int = 0, part: int = 0) -> dict:
    key_of = jax.random.split(jax.random.key(seed), 7)
    part_keys = jax.random.split(jax.random.fold_in(key_of[6], part), 7)
    walkers = bell_draw(part_keys[0], (W, 2, M * N), 1.0, 6.0, ((0, 2), (2, 8)), jnp.float32)
    correlation_inverse = bell_draw(part_keys[1], (W, 2, N, N), N ** -0.5, 0.625, ((0, 2),), jnp.float32)
    half_vectors = bell_draw(part_keys[2], (G, M * N), (3 * M * N) ** -0.5, 0.01953125, ((0, 2), (1, 8)))
    field_vectors = bell_draw(part_keys[3], (G, M, M), (2 * G * M) ** -0.5, 0.0048828125, ((0, 2), (1, 8)))
    samples = bell_draw(part_keys[4], (W, G), 1.0, 6.0, ((1, 2),), jnp.float32)
    source = touch_ends(ranked(part_keys[5], (W,), W, 2), jax.random.fold_in(part_keys[5], 3), 0, W - 1).astype(jnp.int32)
    return dict(walkers=walkers, correlation_inverse=correlation_inverse, half_vectors=half_vectors, field_vectors=field_vectors, samples=samples, source=source)


def to_half(value):
    return lax.optimization_barrier(value.astype(jnp.bfloat16)).astype(jnp.float32)

def complex_product(left_real, left_imag, right_real, right_imag, formula):
    first = jnp.einsum(formula, left_real, right_real, precision=lax.Precision.HIGHEST)
    second = jnp.einsum(formula, left_imag, right_imag, precision=lax.Precision.HIGHEST)
    third = jnp.einsum(formula, left_real, right_imag, precision=lax.Precision.HIGHEST)
    fourth = jnp.einsum(formula, left_imag, right_real, precision=lax.Precision.HIGHEST)
    return (first - second, third + fourth)

def normalizer(gram_real, gram_imag):
    electrons = gram_real.shape[-1]
    identity = jnp.eye(electrons, dtype=jnp.float32)
    scale_factor = jnp.trace(gram_real, axis1=1, axis2=2) / electrons
    iter_real = gram_real / scale_factor[:, None, None]
    iter_imag = gram_imag / scale_factor[:, None, None]
    root_real = jnp.broadcast_to(identity, gram_real.shape)
    root_imag = jnp.zeros_like(gram_real)
    for sweep_index in range(NS_STEPS):
        prod_real, prod_imag = complex_product(root_real, root_imag, iter_real, iter_imag, 'wij,wjk->wik')
        step_real = 1.5 * identity - 0.5 * prod_real
        step_imag = -0.5 * prod_imag
        iter_real, iter_imag = complex_product(iter_real, iter_imag, step_real, step_imag, 'wij,wjk->wik')
        root_real, root_imag = complex_product(step_real, step_imag, root_real, root_imag, 'wij,wjk->wik')
    inverse_root = lax.rsqrt(scale_factor)[:, None, None]
    return (root_real * inverse_root, root_imag * inverse_root)

def reference(walkers, correlation_inverse, half_vectors, field_vectors, samples, source):
    population = walkers.shape[0]
    grid = walkers.reshape(population, 2, M, N)
    theta_real, theta_imag = complex_product(grid[:, 0], grid[:, 1], correlation_inverse[:, 0], correlation_inverse[:, 1], 'wmk,wkn->wmn')
    theta = to_half(jnp.stack([theta_real, theta_imag], 1).reshape(population, 2, M * N))
    bias = jnp.einsum('wcj,gj->wcg', theta, half_vectors.astype(jnp.float32), precision=lax.Precision.HIGHEST)
    coefficient = to_half(jnp.stack([bias[:, 1], samples - bias[:, 0]], 1))
    field = jnp.einsum('wcg,gab->wcab', coefficient, field_vectors.astype(jnp.float32), precision=lax.Precision.HIGHEST)
    field = to_half(field)
    field_real = field[:, 0]
    field_imag = field[:, 1]
    current = grid
    summed = grid
    for order_index in range(1, TERMS + 1):
        rounded = to_half(current)
        next_real, next_imag = complex_product(field_real, field_imag, rounded[:, 0], rounded[:, 1], 'wab,wbn->wan')
        current = jnp.stack([next_real, next_imag], 1) / order_index
        summed = summed + current
    total_real = summed[:, 0]
    total_imag = summed[:, 1]
    gram_real, gram_imag = complex_product(total_real, -total_imag, total_real, total_imag, 'wmi,wmj->wij')
    gram_real = gram_real / M
    gram_imag = gram_imag / M
    root_real, root_imag = normalizer(gram_real, gram_imag)
    norm_real, norm_imag = complex_product(total_real, total_imag, root_real, root_imag, 'wmk,wkn->wmn')
    normalized = jnp.stack([norm_real, norm_imag], 1).reshape(population, 2, M * N)
    return jnp.take(normalized, source.astype(jnp.int32), axis=0)
```

```python
import jax
import jax.numpy as jnp
from jax import lax
from jax.sharding import PartitionSpec as P

TERMS = 4
NS_STEPS = 2
ROWS = ("chol", "orb")
HALF = jnp.bfloat16


def complex_product(left_real, left_imag, right_real, right_imag, formula):
    first = jnp.einsum(formula, left_real, right_real, precision=lax.Precision.HIGHEST)
    second = jnp.einsum(formula, left_imag, right_imag, precision=lax.Precision.HIGHEST)
    third = jnp.einsum(formula, left_real, right_imag, precision=lax.Precision.HIGHEST)
    fourth = jnp.einsum(formula, left_imag, right_real, precision=lax.Precision.HIGHEST)
    return (first - second, third + fourth)


def normalizer(gram_real, gram_imag):
    electrons = gram_real.shape[-1]
    identity = jnp.eye(electrons, dtype=jnp.float32)
    scale_factor = jnp.trace(gram_real, axis1=1, axis2=2) / electrons
    iter_real = gram_real / scale_factor[:, None, None]
    iter_imag = gram_imag / scale_factor[:, None, None]
    root_real = jnp.broadcast_to(identity, gram_real.shape)
    root_imag = jnp.zeros_like(gram_real)
    for sweep_index in range(NS_STEPS):
        if sweep_index == 0:
            prod_real, prod_imag = iter_real, iter_imag
        else:
            prod_real, prod_imag = complex_product(
                root_real, root_imag, iter_real, iter_imag, "wij,wjk->wik"
            )
        step_real = 1.5 * identity - 0.5 * prod_real
        step_imag = -0.5 * prod_imag
        if sweep_index + 1 < NS_STEPS:
            iter_real, iter_imag = complex_product(
                iter_real, iter_imag, step_real, step_imag, "wij,wjk->wik"
            )
        if sweep_index == 0:
            root_real, root_imag = step_real, step_imag
        else:
            root_real, root_imag = complex_product(
                step_real, step_imag, root_real, root_imag, "wij,wjk->wik"
            )
    inverse_root = lax.rsqrt(scale_factor)[:, None, None]
    return (root_real * inverse_root, root_imag * inverse_root)


def field_apply(field_block, values):
    next_real = jnp.einsum(
        "wab,wbn->wan", field_block[:, 0], values[:, 0], preferred_element_type=jnp.float32
    )
    next_real = next_real - jnp.einsum(
        "wab,wbn->wan", field_block[:, 1], values[:, 1], preferred_element_type=jnp.float32
    )
    next_imag = jnp.einsum(
        "wab,wbn->wan", field_block[:, 0], values[:, 1], preferred_element_type=jnp.float32
    )
    next_imag = next_imag + jnp.einsum(
        "wab,wbn->wan", field_block[:, 1], values[:, 0], preferred_element_type=jnp.float32
    )
    return jnp.stack([next_real, next_imag], 1)


def shift(value, axis, step):
    size = lax.axis_size(axis)
    return lax.ppermute(value, axis, [(i, (i + step) % size) for i in range(size)])


def gather_relative(value, axis):
    size = lax.axis_size(axis)
    return jnp.concatenate([value] + [shift(value, axis, -s) for s in range(1, size)], 0)


def scatter_sum(value, axis, dim):
    size = lax.axis_size(axis)
    here = lax.axis_index(axis)
    width = value.shape[dim] // size
    total = lax.dynamic_slice_in_dim(value, here * width, width, dim)
    for s in range(1, size):
        block = lax.dynamic_slice_in_dim(value, ((here + s) % size) * width, width, dim)
        total = total + shift(block, axis, s)
    return total


def gather_ordered(value, axis, dim):
    size = lax.axis_size(axis)
    here = lax.axis_index(axis)
    width = value.shape[dim]
    shape = list(value.shape)
    shape[dim] = width * size
    whole = jnp.zeros(shape, value.dtype)
    for s in range(size):
        block = value if s == 0 else shift(value, axis, s)
        whole = lax.dynamic_update_slice_in_dim(whole, block, ((here - s) % size) * width, dim)
    return whole


def exchange_sum(value, axis):
    size = lax.axis_size(axis)
    if size & (size - 1):
        return sum([shift(value, axis, s) for s in range(1, size)], value)
    step = 1
    while step < size:
        value = value + lax.ppermute(value, axis, [(i, i ^ step) for i in range(size)])
        step *= 2
    return value


def body(walkers, correlation_inverse, half_vectors, field_vectors, samples, source):
    local_walkers = walkers.shape[0]
    row_block = field_vectors.shape[1]
    orbitals = field_vectors.shape[2]
    electrons = correlation_inverse.shape[2]
    planes = lax.axis_size("walk")
    population = local_walkers * planes
    plane = lax.axis_index("walk")
    devices_rows = lax.axis_size(ROWS)
    sharers = devices_rows // local_walkers
    col_width = electrons // sharers

    wanted = gather_relative(source, "walk")
    wanted = (wanted - plane * local_walkers) % population
    grid = walkers.reshape(local_walkers, 2, row_block, electrons)
    all_grid = gather_relative(grid.astype(HALF), "walk")
    picked = jnp.take(all_grid, wanted[:local_walkers], axis=0)
    theta_real, theta_imag = complex_product(
        grid[:, 0], grid[:, 1], correlation_inverse[:, 0], correlation_inverse[:, 1], "wmk,wkn->wmn"
    )
    theta = (
        jnp.stack([theta_real, theta_imag], 1)
        .reshape(local_walkers, 2, row_block * electrons)
        .astype(HALF)
    )
    all_theta = gather_relative(theta, "walk")
    bias = jnp.einsum("wcj,gj->wcg", all_theta, half_vectors, preferred_element_type=jnp.float32)
    bias = exchange_sum(scatter_sum(bias, "orb", 2), "chol")
    width = bias.shape[2]
    drawn = lax.dynamic_slice_in_dim(samples, lax.axis_index("orb") * width, width, 1)
    drawn = jnp.roll(drawn, -plane * local_walkers, axis=0)
    coefficient = jnp.stack([bias[:, 1], drawn - bias[:, 0]], 1).astype(HALF)
    coefficient = jnp.take(coefficient, wanted, axis=0)
    coefficient = gather_ordered(coefficient, "orb", 2)

    def to_owners(value):
        value = jnp.broadcast_to(value[:, None], (local_walkers, sharers) + value.shape[1:])
        value = value.reshape((devices_rows,) + value.shape[2:])
        return lax.all_to_all(value, ROWS, split_axis=0, concat_axis=0, tiled=True)

    columns = to_owners(picked).transpose(1, 0, 2, 3)
    columns = columns.reshape(1, 2, orbitals, electrons).astype(jnp.float32)

    parts = max(1, row_block // 16) if row_block % 16 == 0 else 1
    rows = row_block // parts
    pieces = []
    for part in range(parts):
        vectors = lax.slice_in_dim(field_vectors, part * rows, (part + 1) * rows, axis=1)
        field = jnp.einsum(
            "wcg,gab->wcab", coefficient, vectors, preferred_element_type=jnp.float32
        )
        total = field[:local_walkers]
        for s in range(1, planes):
            sent = field[s * local_walkers : (s + 1) * local_walkers].astype(HALF)
            total = total + shift(sent, "walk", s)
        pieces.append(to_owners(total.astype(HALF)))
    whole_field = jnp.stack(pieces, 1)
    whole_field = whole_field.transpose(2, 0, 1, 3, 4).reshape(1, 2, orbitals, orbitals)

    current = columns
    summed = columns
    for order_index in range(1, TERMS + 1):
        current = field_apply(whole_field, current.astype(HALF)) / order_index
        summed = summed + current
    gram_real, gram_imag = complex_product(
        summed[:, 0], -summed[:, 1], summed[:, 0], summed[:, 1], "wmi,wmj->wij"
    )
    root_real, root_imag = normalizer(gram_real / orbitals, gram_imag / orbitals)
    norm_real, norm_imag = complex_product(
        summed[:, 0], summed[:, 1], root_real, root_imag, "wmk,wkn->wmn"
    )
    normalized = jnp.concatenate([norm_real, norm_imag], 0).astype(HALF)
    share = lax.axis_index(ROWS) % sharers
    normalized = lax.dynamic_slice_in_dim(normalized, share * col_width, col_width, 2)
    normalized = normalized.reshape(2, devices_rows, row_block, col_width).transpose(1, 0, 2, 3)
    returned = lax.all_to_all(normalized, ROWS, split_axis=0, concat_axis=0, tiled=True)
    returned = returned.reshape(local_walkers, sharers, 2, row_block, col_width)
    returned = returned.transpose(0, 2, 3, 1, 4)
    return returned.reshape(local_walkers, 2, row_block * electrons).astype(jnp.float32)


def solution(mesh):
    placed = (
        P(("groups", "walk"), None, ("chol", "orb")),
        P(("groups", "walk"), None, None, None),
        P(("groups", "walk"), ("chol", "orb")),
        P(("groups", "walk"), ("chol", "orb"), None),
        P("groups", "walk"),
        P(("groups", "walk")),
    )
    return jax.shard_map(
        body,
        mesh=mesh,
        in_specs=placed,
        out_specs=P(("groups", "walk"), None, ("chol", "orb")),
        check_vma=False,
    )
```

```python
import functools

import jax
import jax.numpy as jnp
from jax import lax
from jax.experimental import pallas as pl
from jax.experimental.pallas import tpu as pltpu
from jax.sharding import PartitionSpec as P

TERMS = 4
NS_STEPS = 2
ROWS = ("chol", "orb")
HALF = jnp.bfloat16
FULL = jnp.float32
LANES = 128
TILE = 8
VMEM = pltpu.VMEM


def split_half(value):
    high = value.astype(HALF)
    return high, (value - high.astype(FULL)).astype(HALF)


def dot(left, right, contract=((1,), (0,))):
    return lax.dot_general(left, right, (contract, ((), ())), preferred_element_type=FULL)


def fine_dot(left, right):
    left_high, left_low = split_half(left)
    right_high, right_low = split_half(right)
    height = left.shape[0]
    both = dot(jnp.concatenate([left_high, left_low], 0), right_high)
    return both[:height] + both[height:] + dot(left_high, right_low)


def theta_kernel(grid_ref, inverse_ref, theta_ref):
    rows = grid_ref.shape[2]
    for w in range(grid_ref.shape[0]):
        stacked = jnp.concatenate([grid_ref[w, 0], grid_ref[w, 1]], 0)
        by_real = fine_dot(stacked, inverse_ref[w, 0])
        by_imag = fine_dot(stacked, inverse_ref[w, 1])
        theta_ref[w, 0] = (by_real[:rows] - by_imag[rows:]).astype(HALF)
        theta_ref[w, 1] = (by_imag[:rows] + by_real[rows:]).astype(HALF)


def spread_kernel(repeated_ref, spread_ref):
    height, vectors = repeated_ref.shape
    wide = LANES * TILE
    row = lax.broadcasted_iota(jnp.int32, (LANES, wide), 0)
    column = lax.broadcasted_iota(jnp.int32, (LANES, wide), 1)
    copies = (column // TILE == row).astype(FULL).astype(HALF)
    a = lax.broadcasted_iota(jnp.int32, (height, wide), 0) % TILE
    b = lax.broadcasted_iota(jnp.int32, (height, wide), 1) % TILE
    keep = a == b
    for block in range(vectors // LANES):
        values = dot(repeated_ref[:, block * LANES : (block + 1) * LANES], copies)
        spread_ref[:, block * wide : (block + 1) * wide] = jnp.where(keep, values, 0.0).astype(HALF)


def spread_coefficient(coefficient):
    count, vectors = coefficient.shape
    repeated = jnp.repeat(coefficient, TILE, axis=0)
    return pl.pallas_call(
        spread_kernel,
        out_shape=jax.ShapeDtypeStruct((count * TILE, vectors * TILE), HALF),
        in_specs=[pl.BlockSpec(memory_space=VMEM)],
        out_specs=pl.BlockSpec(memory_space=VMEM),
        compiler_params=pltpu.CompilerParams(vmem_limit_bytes=24 << 20),
        name="spread",
    )(repeated)


def field_kernel(steps, mine, spread_ref, vectors_ref, own_ref, sent_ref, total_ref):
    step = pl.program_id(0)
    group, tiles, _, orbitals = vectors_ref.shape
    depth = group * TILE
    count = spread_ref.shape[0] // TILE
    left = spread_ref[:, pl.ds(pl.multiple_of(step * depth, LANES), depth)]
    right = jnp.concatenate(
        [vectors_ref[:, t].reshape(depth, orbitals) for t in range(tiles)], 1
    )
    product = dot(left, right)

    @pl.when(step == 0)
    def _():
        total_ref[...] = product

    @pl.when(step > 0)
    def _():
        total_ref[...] += product

    @pl.when(step == steps - 1)
    def _():
        for t in range(tiles):
            block = total_ref[:, t * orbitals : (t + 1) * orbitals]
            block = block.reshape(count, TILE, orbitals)
            own_ref[:, t * TILE : (t + 1) * TILE] = block[:mine]
            sent_ref[:, t * TILE : (t + 1) * TILE] = block[mine:].astype(HALF)


def field_rows(spread, tiled_vectors, part, tiles, mine):
    vectors, _, _, orbitals = tiled_vectors.shape
    count = spread.shape[0] // TILE
    group = min(vectors, 512)
    steps = vectors // group
    rows = tiles * TILE
    return pl.pallas_call(
        functools.partial(field_kernel, steps, mine),
        grid=(steps,),
        in_specs=[
            pl.BlockSpec(memory_space=VMEM),
            pl.BlockSpec((group, tiles, TILE, orbitals), lambda k: (k, part, 0, 0)),
        ],
        out_specs=[
            pl.BlockSpec((mine, rows, orbitals), lambda k: (0, 0, 0)),
            pl.BlockSpec((count - mine, rows, orbitals), lambda k: (0, 0, 0)),
        ],
        out_shape=[
            jax.ShapeDtypeStruct((mine, rows, orbitals), FULL),
            jax.ShapeDtypeStruct((count - mine, rows, orbitals), HALF),
        ],
        scratch_shapes=[VMEM((count * TILE, tiles * orbitals), FULL)],
        compiler_params=pltpu.CompilerParams(vmem_limit_bytes=32 << 20),
        cost_estimate=pl.CostEstimate(
            flops=2 * count * TILE * vectors * rows * orbitals,
            bytes_accessed=2 * vectors * rows * orbitals,
            transcendentals=0,
        ),
        name="field",
    )(spread, tiled_vectors)


def walker_kernel(count, orbitals, electrons, *refs):
    piece_refs = refs[:count]
    start_ref, out_ref, field_ref, start_wide_ref = refs[count:]
    blocks, _, rows, _ = start_ref.shape
    wide = start_wide_ref.shape[1] // 2
    start_wide_ref[...] = jnp.zeros_like(start_wide_ref)
    for r in range(blocks):
        for c in range(2):
            at = r * rows
            start_wide_ref[pl.ds(at, rows), pl.ds(c * wide, electrons)] = start_ref[r, c]
            at = c * orbitals + r * rows
            for piece_ref in piece_refs:
                height = piece_ref.shape[2]
                field_ref[pl.ds(at, height)] = piece_ref[r, c]
                at += height
    current = start_wide_ref[...]
    summed = current.astype(FULL)
    for order in range(1, TERMS + 1):
        product = dot(field_ref[...], current)
        top, low = product[:orbitals], product[orbitals:]
        following = jnp.concatenate(
            [top[:, :wide] - low[:, wide:], top[:, wide:] + low[:, :wide]], 1
        )
        following = following * (1.0 / order)
        summed = summed + following
        current = following.astype(HALF)

    high, low = split_half(summed)
    rows_first = ((0,), (0,))
    gram = dot(high, high, rows_first) + dot(high, low, rows_first) + dot(low, high, rows_first)
    gram_real = (gram[:wide, :wide] + gram[wide:, wide:]) * (1.0 / orbitals)
    gram_imag = (gram[:wide, wide:] - gram[wide:, :wide]) * (1.0 / orbitals)
    row = lax.broadcasted_iota(jnp.int32, (wide, wide), 0)
    column = lax.broadcasted_iota(jnp.int32, (wide, wide), 1)
    identity = jnp.where((row == column) & (row < electrons), 1.0, 0.0)
    scale = jnp.sum(gram_real * identity, axis=0, keepdims=True)
    scale = jnp.sum(scale, axis=1, keepdims=True) * (1.0 / electrons)

    def times(left, right):
        product = fine_dot(jnp.concatenate(left, 0), jnp.concatenate(right, 1))
        real = product[:wide, :wide] - product[wide:, wide:]
        return real, product[:wide, wide:] + product[wide:, :wide]

    iterate = (gram_real / scale, gram_imag / scale)
    root = None
    for sweep in range(NS_STEPS):
        real, imag = iterate if root is None else times(root, iterate)
        step = (1.5 * identity - 0.5 * real, -0.5 * imag)
        if sweep + 1 < NS_STEPS:
            iterate = times(iterate, step)
        root = step if root is None else times(step, root)
    inverse = lax.rsqrt(scale)
    root = jnp.concatenate([root[0] * inverse, root[1] * inverse], 1)
    product = fine_dot(jnp.concatenate([summed[:, :wide], summed[:, wide:]], 0), root)
    top, low = product[:orbitals], product[orbitals:]
    real = (top[:, :wide] - low[:, wide:]).astype(HALF)
    imag = (top[:, wide:] + low[:, :wide]).astype(HALF)
    for r in range(blocks):
        out_ref[r, 0] = real[r * rows : (r + 1) * rows, :electrons]
        out_ref[r, 1] = imag[r * rows : (r + 1) * rows, :electrons]


def walker_step(pieces, start):
    orbitals = pieces[0].shape[3]
    electrons = start.shape[3]
    wide = -(-electrons // LANES) * LANES
    return pl.pallas_call(
        functools.partial(walker_kernel, len(pieces), orbitals, electrons),
        out_shape=jax.ShapeDtypeStruct(start.shape, HALF),
        in_specs=[pl.BlockSpec(memory_space=VMEM)] * (len(pieces) + 1),
        out_specs=pl.BlockSpec(memory_space=VMEM),
        scratch_shapes=[VMEM((2 * orbitals, orbitals), HALF), VMEM((orbitals, 2 * wide), HALF)],
        compiler_params=pltpu.CompilerParams(vmem_limit_bytes=24 << 20),
        name="walker",
    )(*pieces, start)


def shift(value, axis, step):
    size = lax.axis_size(axis)
    return lax.ppermute(value, axis, [(i, (i + step) % size) for i in range(size)])


def gather_relative(value, axis):
    size = lax.axis_size(axis)
    return jnp.concatenate([value] + [shift(value, axis, -s) for s in range(1, size)], 0)


def scatter_sum(value, axis, dim):
    size = lax.axis_size(axis)
    here = lax.axis_index(axis)
    width = value.shape[dim] // size
    total = lax.dynamic_slice_in_dim(value, here * width, width, dim)
    for s in range(1, size):
        block = lax.dynamic_slice_in_dim(value, ((here + s) % size) * width, width, dim)
        total = total + shift(block, axis, s)
    return total


def gather_ordered(value, axis, dim):
    size = lax.axis_size(axis)
    here = lax.axis_index(axis)
    width = value.shape[dim]
    shape = list(value.shape)
    shape[dim] = width * size
    whole = jnp.zeros(shape, value.dtype)
    for s in range(size):
        block = value if s == 0 else shift(value, axis, s)
        whole = lax.dynamic_update_slice_in_dim(whole, block, ((here - s) % size) * width, dim)
    return whole


def exchange_sum(value, axis):
    size = lax.axis_size(axis)
    if size & (size - 1):
        return sum([shift(value, axis, s) for s in range(1, size)], value)
    step = 1
    while step < size:
        value = value + lax.ppermute(value, axis, [(i, i ^ step) for i in range(size)])
        step *= 2
    return value


def body(walkers, correlation_inverse, half_vectors, field_vectors, samples, source):
    local_walkers = walkers.shape[0]
    vectors, row_block, orbitals = field_vectors.shape
    electrons = correlation_inverse.shape[2]
    planes = lax.axis_size("walk")
    population = local_walkers * planes
    plane = lax.axis_index("walk")
    devices_rows = lax.axis_size(ROWS)
    sharers = devices_rows // local_walkers
    col_width = electrons // sharers
    tiled = row_block % (2 * TILE) == 0 and vectors % LANES == 0

    wanted = gather_relative(source, "walk")
    wanted = (wanted - plane * local_walkers) % population
    grid = walkers.reshape(local_walkers, 2, row_block, electrons)
    all_grid = gather_relative(grid.astype(HALF), "walk")
    picked = jnp.take(all_grid, wanted[:local_walkers], axis=0)
    theta = pl.pallas_call(
        theta_kernel,
        out_shape=jax.ShapeDtypeStruct(grid.shape, HALF),
        in_specs=[pl.BlockSpec(memory_space=VMEM)] * 2,
        out_specs=pl.BlockSpec(memory_space=VMEM),
        compiler_params=pltpu.CompilerParams(vmem_limit_bytes=24 << 20),
        name="theta",
    )(grid, correlation_inverse)
    theta = theta.reshape(local_walkers, 2, row_block * electrons)
    all_theta = gather_relative(theta, "walk")
    bias = jnp.einsum("wcj,gj->wcg", all_theta, half_vectors, preferred_element_type=FULL)
    bias = exchange_sum(scatter_sum(bias, "orb", 2), "chol")
    width = bias.shape[2]
    drawn = lax.dynamic_slice_in_dim(samples, lax.axis_index("orb") * width, width, 1)
    drawn = jnp.roll(drawn, -plane * local_walkers, axis=0)
    coefficient = jnp.stack([bias[:, 1], drawn - bias[:, 0]], 1).astype(HALF)
    coefficient = jnp.take(coefficient, wanted, axis=0)
    coefficient = gather_ordered(coefficient, "orb", 2)

    def to_owners(value):
        value = jnp.broadcast_to(value[:, None], (local_walkers, sharers) + value.shape[1:])
        value = value.reshape((devices_rows,) + value.shape[2:])
        return lax.all_to_all(value, ROWS, split_axis=0, concat_axis=0, tiled=True)

    columns = to_owners(picked)

    def add_planes(own, sent):
        total = own
        for s in range(1, planes):
            block = sent[(s - 1) * local_walkers : s * local_walkers]
            total = total + shift(block, "walk", s)
        return total.astype(HALF)

    pieces = []
    if tiled:
        spread = spread_coefficient(coefficient.reshape(population * 2, vectors))
        tiled_vectors = field_vectors.reshape(vectors, row_block // TILE, TILE, orbitals)
        rows = 2 * TILE
        for part in range(row_block // rows):
            own, sent = field_rows(spread, tiled_vectors, part, 2, local_walkers * 2)
            own = own.reshape(local_walkers, 2, rows, orbitals)
            sent = sent.reshape(population - local_walkers, 2, rows, orbitals)
            pieces.append(to_owners(add_planes(own, sent)))
    else:
        field = jnp.einsum(
            "wcg,gab->wcab", coefficient, field_vectors, preferred_element_type=FULL
        )
        own, sent = field[:local_walkers], field[local_walkers:].astype(HALF)
        whole = to_owners(add_planes(own, sent)).transpose(1, 0, 2, 3)
        pieces.append(whole.reshape(1, 2, orbitals, orbitals))
        columns = columns.transpose(1, 0, 2, 3).reshape(1, 2, orbitals, electrons)

    normalized = walker_step(pieces, columns)
    if not tiled:
        normalized = normalized.reshape(2, devices_rows, row_block, electrons)
        normalized = normalized.transpose(1, 0, 2, 3)
    if sharers > 1:
        share = lax.axis_index(ROWS) % sharers
        normalized = lax.dynamic_slice_in_dim(normalized, share * col_width, col_width, 3)
    returned = lax.all_to_all(normalized, ROWS, split_axis=0, concat_axis=0, tiled=True)
    if sharers > 1:
        returned = returned.reshape(local_walkers, sharers, 2, row_block, col_width)
        returned = returned.transpose(0, 2, 3, 1, 4)
    return returned.reshape(local_walkers, 2, row_block * electrons).astype(FULL)


def solution(mesh):
    placed = (
        P(("groups", "walk"), None, ("chol", "orb")),
        P(("groups", "walk"), None, None, None),
        P(("groups", "walk"), ("chol", "orb")),
        P(("groups", "walk"), ("chol", "orb"), None),
        P("groups", "walk"),
        P(("groups", "walk")),
    )
    return jax.shard_map(
        body,
        mesh=mesh,
        in_specs=placed,
        out_specs=P(("groups", "walk"), None, ("chol", "orb")),
        check_vma=False,
    )
```

```python
import functools

import jax
import jax.numpy as jnp
from jax import lax
from jax.experimental import pallas as pl
from jax.experimental.pallas import tpu as pltpu
from jax.sharding import PartitionSpec as P


TERMS = 4
NS_STEPS = 2
ROWS = ("chol", "orb")
HALF = jnp.bfloat16
FULL = jnp.float32
LANES = 128
TILE = 8
SMALL = 8 << 20
VMEM = pltpu.VMEM


def split_half(value):
    high = value.astype(HALF)
    return high, (value - high.astype(FULL)).astype(HALF)


def dot(left, right, contract=((1,), (0,))):
    return lax.dot_general(left, right, (contract, ((), ())), preferred_element_type=FULL)


def fine_dot(left, right):
    left_high, left_low = split_half(left)
    right_high, right_low = split_half(right)
    height = left.shape[0]
    both = dot(jnp.concatenate([left_high, left_low], 0), right_high)
    return both[:height] + both[height:] + dot(left_high, right_low)


def theta_kernel(grid_ref, inverse_ref, theta_ref):
    rows = grid_ref.shape[2]
    for w in range(grid_ref.shape[0]):
        stacked = jnp.concatenate([grid_ref[w, 0], grid_ref[w, 1]], 0)
        by_real = fine_dot(stacked, inverse_ref[w, 0])
        by_imag = fine_dot(stacked, inverse_ref[w, 1])
        theta_ref[w, 0] = (by_real[:rows] - by_imag[rows:]).astype(HALF)
        theta_ref[w, 1] = (by_imag[:rows] + by_real[rows:]).astype(HALF)


def fill_spread(place_ref, own_ref, received_ref, spread_ref):
    count, half = own_ref.shape
    height = count * TILE
    wide = LANES * TILE
    row = lax.broadcasted_iota(jnp.int32, (LANES, wide), 0)
    column = lax.broadcasted_iota(jnp.int32, (LANES, wide), 1)
    copies = (column // TILE == row).astype(FULL).astype(HALF)
    a = lax.broadcasted_iota(jnp.int32, (height, wide), 0) % TILE
    b = lax.broadcasted_iota(jnp.int32, (height, wide), 1) % TILE
    keep = a == b
    row = lax.broadcasted_iota(jnp.int32, (height, count), 0)
    column = lax.broadcasted_iota(jnp.int32, (height, count), 1)
    repeats = (row // TILE == column).astype(FULL).astype(HALF)
    low = place_ref[1] == 0
    own, received = own_ref[...].astype(FULL), received_ref[...].astype(FULL)
    for part, values in enumerate((jnp.where(low, own, received), jnp.where(low, received, own))):
        values = dot(repeats, values.astype(HALF)).astype(HALF)
        for block in range(half // LANES):
            at = (part * half + block * LANES) * TILE
            wider = dot(values[:, block * LANES : (block + 1) * LANES], copies)
            spread_ref[:, at : at + wide] = jnp.where(keep, wider, 0.0).astype(HALF)


SCALARS = pl.BlockSpec(memory_space=pltpu.SMEM)
ARRAY = pl.BlockSpec(memory_space=VMEM)


def local_kernel(kernel, in_specs, out_shape, scratch_shapes=()):
    return pl.pallas_call(
        kernel,
        in_specs=in_specs,
        out_specs=jax.tree.map(lambda _: ARRAY, out_shape),
        out_shape=out_shape,
        scratch_shapes=list(scratch_shapes),
        compiler_params=pltpu.CompilerParams(vmem_limit_bytes=SMALL),
    )


def wanted_walker(place_ref, source_ref, others_ref, i, population):
    local = source_ref.shape[0]
    walker = source_ref[i] if i < local else others_ref[i - local]
    relative = walker - place_ref[0]
    return walker, jnp.where(relative < 0, relative + population, relative)


def pick_kernel(place_ref, source_ref, own_ref, received_ref, keep_ref, send_ref, all_ref):
    local = own_ref.shape[0]
    population = all_ref.shape[0]
    all_ref[:local] = own_ref[...]
    all_ref[local:] = received_ref[...]
    for t in range(local // 2):
        for target_ref, core in ((keep_ref, place_ref[1]), (send_ref, 1 - place_ref[1])):
            relative = source_ref[2 * t + core] - place_ref[0]
            relative = jnp.where(relative < 0, relative + population, relative)
            target_ref[t, 0] = all_ref[relative]


def split_kernel(step, place_ref, own_ref, received_ref, keep_ref, send_ref):
    senders = own_ref.shape[1]
    bit = (place_ref[2] // step) % 2
    for t in range(own_ref.shape[0] // 2):
        for target_ref, side in ((keep_ref, bit), (send_ref, 1 - bit)):
            target_ref[t, :senders] = own_ref[2 * t + side]
            target_ref[t, senders:] = received_ref[2 * t + side]


def bias_kernel(place_ref, own_ref, received_ref, vectors_ref, keep_ref, send_ref):
    angles = jnp.concatenate([own_ref[...], received_ref[...]], 0)
    bias = dot(vectors_ref[...], angles, ((1,), (1,))).T
    half = bias.shape[1] // 2
    first, second = bias[:, :half], bias[:, half:]
    low = place_ref[1] == 0
    keep_ref[...] = jnp.where(low, first, second)
    send_ref[...] = jnp.where(low, second, first)


def add_kernel(left_ref, right_ref, out_ref):
    out_ref[...] = left_ref[...] + right_ref[...]


def coefficient_kernel(
    place_ref, source_ref, others_ref, left_ref, right_ref, samples_ref, out_ref, bias_ref, row_ref
):
    bias_ref[...] = left_ref[...] + right_ref[...]
    count, half = bias_ref.shape
    lanes = pl.ds(pl.multiple_of(place_ref[1] * half, LANES), half)
    for i in range(count // 2):
        walker, relative = wanted_walker(place_ref, source_ref, others_ref, i, count // 2)
        row_ref[2 * i : 2 * i + 1] = bias_ref[pl.ds(2 * relative + 1, 1)]
        drawn = samples_ref[pl.ds(walker, 1), lanes]
        row_ref[2 * i + 1 : 2 * i + 2] = drawn - bias_ref[pl.ds(2 * relative, 1)]
    out_ref[...] = row_ref[...].astype(HALF)


def read_kernel(half_hbm, field_hbm, half_ref, chunk_ref, semaphores):
    tiles = chunk_ref.shape[1]
    copies = []
    for source_ref, target_ref in (
        (half_hbm, half_ref),
        (field_hbm.at[:, pl.ds(0, tiles)], chunk_ref),
    ):
        vectors = target_ref.shape[0]
        for block in range(vectors // LANES):
            group = pl.ds(block * LANES, LANES)
            semaphore = semaphores.at[len(copies)]
            copy = pltpu.make_async_copy(source_ref.at[group], target_ref.at[group], semaphore)
            copy.start()
            copies.append(copy)
    for copy in copies:
        copy.wait()


def read_early(half_vectors, tiled_vectors, tiles):
    vectors, _, _, orbitals = tiled_vectors.shape
    chunk = jax.ShapeDtypeStruct((vectors, tiles, TILE, orbitals), HALF)
    size = half_vectors.size + chunk.size
    return pl.pallas_call(
        read_kernel,
        in_specs=[pl.BlockSpec(memory_space=pltpu.HBM)] * 2,
        out_specs=[pl.BlockSpec(memory_space=VMEM)] * 2,
        out_shape=[VMEM(half_vectors.shape, HALF), VMEM(chunk.shape, HALF)],
        scratch_shapes=[pltpu.SemaphoreType.DMA((2 * (vectors // LANES),))],
        compiler_params=pltpu.CompilerParams(vmem_limit_bytes=36 << 20),
        cost_estimate=pl.CostEstimate(flops=0, bytes_accessed=2 * size, transcendentals=0),
        name="read",
    )(half_vectors, tiled_vectors)


def field_kernel(part, parts, mine, *refs):
    refs = list(refs)
    left_refs = [refs.pop(0) for _ in range(3 if part == 0 else 1)]
    chunk_ref, vectors_ref, own_ref, sent_ref = refs[:4]
    refs = refs[4:]
    spread_ref = refs.pop(0) if part == 0 else left_refs[0]
    vectors, tiles, _, orbitals = chunk_ref.shape
    count = spread_ref.shape[0] // TILE
    copies = []
    if part + 1 < parts:
        next_ref, semaphores = refs
        for block in range(vectors // LANES):
            group = pl.ds(block * LANES, LANES)
            copy = pltpu.make_async_copy(
                vectors_ref.at[group, pl.ds((part + 1) * tiles, tiles)],
                next_ref.at[group],
                semaphores.at[block],
            )
            copy.start()
            copies.append(copy)
    if part == 0:
        fill_spread(*left_refs, spread_ref)
    group = min(vectors, 4 * LANES)
    depth = group * TILE
    total = None
    for block in range(vectors // group):
        right = jnp.concatenate(
            [
                chunk_ref[block * group : (block + 1) * group, t].reshape(depth, orbitals)
                for t in range(tiles)
            ],
            1,
        )
        product = dot(spread_ref[:, block * depth : (block + 1) * depth], right)
        total = product if total is None else total + product
    for t in range(tiles):
        slab = total[:, t * orbitals : (t + 1) * orbitals].reshape(count, TILE, orbitals)
        own_ref[:, t * TILE : (t + 1) * TILE] = slab[:mine]
        sent_ref[:, t * TILE : (t + 1) * TILE] = slab[mine:].astype(HALF)
    for copy in copies:
        copy.wait()


def field_rows(left, chunk, tiled_vectors, part, parts, count, mine):
    vectors, tiles, _, orbitals = chunk.shape
    rows = tiles * TILE
    out_shape = [
        jax.ShapeDtypeStruct((mine, rows, orbitals), FULL),
        jax.ShapeDtypeStruct((count - mine, rows, orbitals), HALF),
    ]
    if part == 0:
        out_shape.append(jax.ShapeDtypeStruct((count * TILE, vectors * TILE), HALF))
    scratch = []
    if part + 1 < parts:
        out_shape.append(jax.ShapeDtypeStruct(chunk.shape, HALF))
        scratch.append(pltpu.SemaphoreType.DMA((vectors // LANES,)))
    left_specs = [SCALARS, ARRAY, ARRAY] if part == 0 else [ARRAY]
    own, sent, *rest = pl.pallas_call(
        functools.partial(field_kernel, part, parts, mine),
        in_specs=left_specs + [ARRAY, pl.BlockSpec(memory_space=pltpu.HBM)],
        out_specs=[ARRAY] * len(out_shape),
        out_shape=out_shape,
        scratch_shapes=scratch,
        compiler_params=pltpu.CompilerParams(vmem_limit_bytes=SMALL),
        cost_estimate=pl.CostEstimate(
            flops=2 * count * TILE * vectors * rows * orbitals,
            bytes_accessed=2 * vectors * rows * orbitals,
            transcendentals=0,
        ),
        name="field",
    )(*left, chunk, tiled_vectors)
    left = [rest.pop(0)] if part == 0 else left
    return own, sent, left, rest[0] if rest else None


def combine_kernel(chunks, *refs):
    own_refs, received_refs, out_ref = refs[:chunks], refs[chunks:-1], refs[-1]
    others = len(received_refs) // chunks
    rows = own_refs[0].shape[2]
    for c in range(chunks):
        total = own_refs[c][...]
        for received_ref in received_refs[c * others : (c + 1) * others]:
            total = total + received_ref[...].astype(FULL)
        out_ref[:, :, c * rows : (c + 1) * rows] = total.astype(HALF)


def combine(owns, received):
    chunks = len(owns)
    slots, parts, rows, orbitals = owns[0].shape
    return pl.pallas_call(
        functools.partial(combine_kernel, chunks),
        out_shape=jax.ShapeDtypeStruct((slots, parts, rows * chunks, orbitals), HALF),
        in_specs=[pl.BlockSpec(memory_space=VMEM)] * (chunks + len(received)),
        out_specs=pl.BlockSpec(memory_space=VMEM),
        compiler_params=pltpu.CompilerParams(vmem_limit_bytes=SMALL),
        name="combine",
    )(*owns, *received)


def walker_kernel(count, orbitals, electrons, rank_ref, field_piece_ref, *refs):
    start_refs = refs[:count]
    out_ref, field_ref, start_wide_ref = refs[count:]
    blocks, _, rows, _ = field_piece_ref.shape
    wide = start_wide_ref.shape[1] // 2
    start_wide_ref[...] = jnp.zeros_like(start_wide_ref)
    for r in range(blocks):
        for c in range(2):
            field_ref[pl.ds(c * orbitals + r * rows, rows)] = field_piece_ref[r, c]
    block = 0
    for start_ref in start_refs:
        for d in range(start_ref.shape[0]):
            at = pl.multiple_of((rank_ref[0] ^ block) * rows, 2 * TILE)
            for c in range(2):
                start_wide_ref[pl.ds(at, rows), pl.ds(c * wide, electrons)] = start_ref[d, c]
            block += 1
    current = start_wide_ref[...]
    summed = current.astype(FULL)
    for order in range(1, TERMS + 1):
        product = dot(field_ref[...], current)
        top, low = product[:orbitals], product[orbitals:]
        following = jnp.concatenate(
            [top[:, :wide] - low[:, wide:], top[:, wide:] + low[:, :wide]], 1
        )
        following = following * (1.0 / order)
        summed = summed + following
        current = following.astype(HALF)

    high, low = split_half(summed)
    rows_first = ((0,), (0,))
    gram = dot(high, high, rows_first) + dot(high, low, rows_first) + dot(low, high, rows_first)
    gram_real = (gram[:wide, :wide] + gram[wide:, wide:]) * (1.0 / orbitals)
    gram_imag = (gram[:wide, wide:] - gram[wide:, :wide]) * (1.0 / orbitals)
    row = lax.broadcasted_iota(jnp.int32, (wide, wide), 0)
    column = lax.broadcasted_iota(jnp.int32, (wide, wide), 1)
    identity = jnp.where((row == column) & (row < electrons), 1.0, 0.0)
    scale = jnp.sum(gram_real * identity, axis=0, keepdims=True)
    scale = jnp.sum(scale, axis=1, keepdims=True) * (1.0 / electrons)

    def times(left, right):
        product = fine_dot(jnp.concatenate(left, 0), jnp.concatenate(right, 1))
        real = product[:wide, :wide] - product[wide:, wide:]
        return real, product[:wide, wide:] + product[wide:, :wide]

    iterate = (gram_real / scale, gram_imag / scale)
    root = None
    for sweep in range(NS_STEPS):
        real, imag = iterate if root is None else times(root, iterate)
        step = (1.5 * identity - 0.5 * real, -0.5 * imag)
        if sweep + 1 < NS_STEPS:
            iterate = times(iterate, step)
        root = step if root is None else times(step, root)
    inverse = lax.rsqrt(scale)
    root = jnp.concatenate([root[0] * inverse, root[1] * inverse], 1)
    product = fine_dot(jnp.concatenate([summed[:, :wide], summed[:, wide:]], 0), root)
    top, low = product[:orbitals], product[orbitals:]
    real = (top[:, :wide] - low[:, wide:]).astype(HALF)
    imag = (top[:, wide:] + low[:, :wide]).astype(HALF)
    for r in range(blocks):
        out_ref[r, 0] = real[r * rows : (r + 1) * rows, :electrons]
        out_ref[r, 1] = imag[r * rows : (r + 1) * rows, :electrons]


def walker_step(rank, field, starts):
    blocks, parts, rows, orbitals = field.shape
    electrons = starts[0].shape[3]
    wide = -(-electrons // LANES) * LANES
    return local_kernel(
        functools.partial(walker_kernel, len(starts), orbitals, electrons),
        [SCALARS] + [ARRAY] * (1 + len(starts)),
        jax.ShapeDtypeStruct((blocks, parts, rows, electrons), HALF),
        [VMEM((2 * orbitals, orbitals), HALF), VMEM((orbitals, 2 * wide), HALF)],
    )(rank, field, *starts)


def shift(value, axis, step):
    size = lax.axis_size(axis)
    return lax.ppermute(value, axis, [(i, (i + step) % size) for i in range(size)])


def scatter_sum(value, axis, dim):
    size = lax.axis_size(axis)
    here = lax.axis_index(axis)
    width = value.shape[dim] // size
    total = lax.dynamic_slice_in_dim(value, here * width, width, dim)
    for s in range(1, size):
        block = lax.dynamic_slice_in_dim(value, ((here + s) % size) * width, width, dim)
        total = total + shift(block, axis, s)
    return total


def gather_ordered(value, axis, dim):
    size = lax.axis_size(axis)
    here = lax.axis_index(axis)
    width = value.shape[dim]
    shape = list(value.shape)
    shape[dim] = width * size
    whole = jnp.zeros(shape, value.dtype)
    for s in range(size):
        block = value if s == 0 else shift(value, axis, s)
        whole = lax.dynamic_update_slice_in_dim(whole, block, ((here - s) % size) * width, dim)
    return whole


def exchange_sum(value, axis):
    size = lax.axis_size(axis)
    if size & (size - 1):
        return sum([shift(value, axis, s) for s in range(1, size)], value)
    step = 1
    while step < size:
        value = value + lax.ppermute(value, axis, [(i, i ^ step) for i in range(size)])
        step *= 2
    return value


def whole_step(walkers, correlation_inverse, half_vectors, field_vectors, samples, source):
    local = walkers.shape[0]
    vectors, row_block, orbitals = field_vectors.shape
    electrons = correlation_inverse.shape[2]
    planes = lax.axis_size("walk")
    population = local * planes
    count = population * 2
    devices_rows = lax.axis_size(ROWS)
    sharers = devices_rows // local
    first = lax.axis_index("walk") * local
    core = lax.axis_index("orb")
    chol = lax.axis_size("chol")
    half = vectors // 2
    fast = (
        row_block % (2 * TILE) == 0
        and vectors % (2 * LANES) == 0
        and lax.axis_size("orb") == 2
        and planes > 1
        and sharers == 1
        and chol & (chol - 1) == 0
    )

    def to_owners(value):
        value = jnp.broadcast_to(value[:, None], (local, sharers) + value.shape[1:])
        value = value.reshape((devices_rows,) + value.shape[2:])
        return lax.all_to_all(value, ROWS, split_axis=0, concat_axis=0, tiled=True)

    def others(value):
        return jnp.concatenate([shift(value, "walk", -s) for s in range(1, planes)], 0)

    def from_planes(sent):
        blocks = [sent[s * local : (s + 1) * local] for s in range(planes - 1)]
        return [shift(block, "walk", s + 1) for s, block in enumerate(blocks)]

    other_source = others(source)
    place = jnp.stack([first, core, lax.axis_index("chol")]).astype(jnp.int32)
    rank = lax.axis_index(ROWS).astype(jnp.int32).reshape(1)
    grid = walkers.reshape(local, 2, row_block, electrons)
    theta = local_kernel(
        theta_kernel, [ARRAY] * 2, jax.ShapeDtypeStruct(grid.shape, HALF)
    )(grid, correlation_inverse)
    theta = theta.reshape(local * 2, row_block * electrons)
    other_theta = others(theta)
    start = grid.astype(HALF)
    other_start = others(start)

    if fast:
        tiled_vectors = field_vectors.reshape(vectors, row_block // TILE, TILE, orbitals)
        half_vectors, chunk = read_early(half_vectors, tiled_vectors, 2)
        part_shape = jax.ShapeDtypeStruct((count, half), FULL)
        bias, sent = local_kernel(
            bias_kernel, [SCALARS] + [ARRAY] * 3, [part_shape] * 2
        )(place, theta, other_theta, half_vectors)
        received = shift(sent, "orb", 1)
        add = local_kernel(add_kernel, [ARRAY] * 2, part_shape)
        block = (2, row_block, electrons)
        slots = jax.ShapeDtypeStruct((local // 2, 1) + block, HALF)
        keep, sent = local_kernel(
            pick_kernel,
            [SCALARS] * 2 + [ARRAY] * 2,
            [slots] * 2,
            [VMEM((population,) + block, HALF)],
        )(place, source, start, other_start)
        passed = shift(sent, "orb", 1)
        step = 1
        while step < chol:
            pairs = [(i, i ^ step) for i in range(chol)]
            bias = add(bias, received)
            received = lax.ppermute(bias, "chol", pairs)
            slots = jax.ShapeDtypeStruct((keep.shape[0] // 2, keep.shape[1] * 2) + block, HALF)
            keep, sent = local_kernel(
                functools.partial(split_kernel, step), [SCALARS] + [ARRAY] * 2, [slots] * 2
            )(place, keep, passed)
            passed = lax.ppermute(sent, "chol", pairs)
            step *= 2
        coefficient = local_kernel(
            coefficient_kernel,
            [SCALARS] * 3 + [ARRAY] * 3,
            jax.ShapeDtypeStruct((count, half), HALF),
            [VMEM((count, half), FULL)] * 2,
        )(place, source, other_source, bias, received, samples)
        other_half = shift(coefficient, "orb", 1)
        rows = 2 * TILE
        parts = row_block // rows
        owns, received = [], []
        left = [place, coefficient, other_half]
        for part in range(parts):
            own, sent, left, chunk = field_rows(
                left, chunk, tiled_vectors, part, parts, count, local * 2
            )
            owns.append(own.reshape(local, 2, rows, orbitals))
            sent = sent.reshape(population - local, 2, rows, orbitals)
            received += from_planes(sent)
        field = to_owners(combine(owns, received))
        starts = [keep[0], passed[0]]
    else:
        wanted = jnp.concatenate([source, other_source], 0)
        relative = jnp.where(wanted < first, wanted - first + population, wanted - first)
        all_start = jnp.concatenate([start, other_start], 0)
        picked = all_start.at[relative[:local]].get(mode="promise_in_bounds")
        columns = to_owners(picked)
        angles = jnp.concatenate([theta, other_theta], 0)
        bias = jnp.einsum("ij,gj->ig", angles, half_vectors, preferred_element_type=FULL)
        bias = bias.reshape(population, 2, vectors)
        bias = exchange_sum(scatter_sum(bias, "orb", 2), "chol")
        bias = bias.at[relative].get(mode="promise_in_bounds")
        width = bias.shape[2]
        drawn = lax.dynamic_slice_in_dim(samples, core * width, width, 1)
        drawn = drawn.at[wanted].get(mode="promise_in_bounds")
        coefficient = jnp.stack([bias[:, 1], drawn - bias[:, 0]], 1).astype(HALF)
        coefficient = gather_ordered(coefficient, "orb", 2)
        field = jnp.einsum(
            "wcg,gab->wcab", coefficient, field_vectors, preferred_element_type=FULL
        )
        total = field[:local]
        for block in from_planes(field[local:].astype(HALF)):
            total = total + block
        field = to_owners(total.astype(HALF)).transpose(1, 0, 2, 3)
        field = field.reshape(1, 2, orbitals, orbitals)
        starts = [columns.transpose(1, 0, 2, 3).reshape(1, 2, orbitals, electrons)]
        rank = jnp.zeros((1,), jnp.int32)

    normalized = walker_step(rank, field, starts)
    if not fast:
        normalized = normalized.reshape(2, devices_rows, row_block, electrons)
        normalized = normalized.transpose(1, 0, 2, 3)
    if sharers > 1:
        share = lax.axis_index(ROWS) % sharers
        width = electrons // sharers
        normalized = lax.dynamic_slice_in_dim(normalized, share * width, width, 3)
    returned = lax.all_to_all(normalized, ROWS, split_axis=0, concat_axis=0, tiled=True)
    if sharers > 1:
        returned = returned.reshape(local, sharers, 2, row_block, width)
        returned = returned.transpose(0, 2, 3, 1, 4)
    return returned.reshape(local, 2, row_block * electrons).astype(FULL)


def solution(mesh):
    placed = (
        P(("groups", "walk"), None, ("chol", "orb")),
        P(("groups", "walk"), None, None, None),
        P(("groups", "walk"), ("chol", "orb")),
        P(("groups", "walk"), ("chol", "orb"), None),
        P("groups", "walk"),
        P(("groups", "walk")),
    )
    return jax.shard_map(
        whole_step,
        mesh=mesh,
        in_specs=placed,
        out_specs=P(("groups", "walk"), None, ("chol", "orb")),
        check_vma=False,
    )
```

```python
import functools

import jax
import jax.numpy as jnp
from jax import lax
from jax.experimental import pallas as pl
from jax.experimental.pallas import tpu as pltpu
from jax.sharding import PartitionSpec as P


TERMS = 4
NS_STEPS = 2
ROWS = ("chol", "orb")
HALF = jnp.bfloat16
FULL = jnp.float32
LANES = 128
TILE = 8
SMALL = 8 << 20
TINY = 2 << 20
READ_LIMIT = 36 << 20
VMEM = pltpu.VMEM


def split_half(value):
    high = value.astype(HALF)
    return high, (value - high.astype(FULL)).astype(HALF)


def dot(left, right, contract=((1,), (0,))):
    return lax.dot_general(left, right, (contract, ((), ())), preferred_element_type=FULL)


def fine_dot(left, right):
    left_high, left_low = split_half(left)
    right_high, right_low = split_half(right)
    height = left.shape[0]
    both = dot(jnp.concatenate([left_high, left_low], 0), right_high)
    return both[:height] + both[height:] + dot(left_high, right_low)


def theta_kernel(grid_ref, inverse_ref, theta_ref):
    rows = grid_ref.shape[2]
    for w in range(grid_ref.shape[0]):
        stacked = jnp.concatenate([grid_ref[w, 0], grid_ref[w, 1]], 0)
        by_real = fine_dot(stacked, inverse_ref[w, 0])
        by_imag = fine_dot(stacked, inverse_ref[w, 1])
        theta_ref[w, 0] = (by_real[:rows] - by_imag[rows:]).astype(HALF)
        theta_ref[w, 1] = (by_imag[:rows] + by_real[rows:]).astype(HALF)


def fill_spread(place_ref, own_ref, received_ref, spread_ref, values_ref):
    count, half = own_ref.shape
    height = count * TILE
    wide = LANES * TILE
    row = lax.broadcasted_iota(jnp.int32, (height, count), 0)
    column = lax.broadcasted_iota(jnp.int32, (height, count), 1)
    repeats = (row // TILE == column).astype(FULL).astype(HALF)
    low = place_ref[1] == 0
    own, received = own_ref[...].astype(FULL), received_ref[...].astype(FULL)
    values_ref[:, :half] = dot(repeats, jnp.where(low, own, received).astype(HALF)).astype(HALF)
    values_ref[:, half:] = dot(repeats, jnp.where(low, received, own).astype(HALF)).astype(HALF)
    row = lax.broadcasted_iota(jnp.int32, (LANES, wide), 0)
    column = lax.broadcasted_iota(jnp.int32, (LANES, wide), 1)
    copies = (column // TILE == row).astype(FULL).astype(HALF)
    a = lax.broadcasted_iota(jnp.int32, (height, wide), 0) % TILE
    b = lax.broadcasted_iota(jnp.int32, (height, wide), 1) % TILE

    @pl.loop(0, 2 * half // LANES)
    def _(block):
        values = values_ref[:, pl.ds(pl.multiple_of(block * LANES, LANES), LANES)]
        wider = jnp.where(a == b, dot(values, copies), 0.0).astype(HALF)
        spread_ref[:, pl.ds(pl.multiple_of(block * wide, wide), wide)] = wider


SCALARS = pl.BlockSpec(memory_space=pltpu.SMEM)
ARRAY = pl.BlockSpec(memory_space=VMEM)


def local_kernel(kernel, in_specs, out_shape, scratch_shapes=(), limit=TINY):
    return pl.pallas_call(
        kernel,
        in_specs=in_specs,
        out_specs=jax.tree.map(lambda _: ARRAY, out_shape),
        out_shape=out_shape,
        scratch_shapes=list(scratch_shapes),
        compiler_params=pltpu.CompilerParams(vmem_limit_bytes=limit),
    )


def wanted_walker(place_ref, source_ref, others_ref, i, population):
    local = source_ref.shape[0]
    walker = source_ref[i] if i < local else others_ref[i - local]
    relative = walker - place_ref[0]
    return walker, jnp.where(relative < 0, relative + population, relative)


def pick_kernel(place_ref, source_ref, own_ref, received_ref, keep_ref, send_ref, all_ref):
    local = own_ref.shape[0]
    population = all_ref.shape[0]
    all_ref[:local] = own_ref[...]
    all_ref[local:] = received_ref[...]
    for t in range(local // 2):
        for target_ref, core in ((keep_ref, place_ref[1]), (send_ref, 1 - place_ref[1])):
            relative = source_ref[2 * t + core] - place_ref[0]
            relative = jnp.where(relative < 0, relative + population, relative)
            target_ref[t, 0] = all_ref[relative]


def split_kernel(step, place_ref, own_ref, received_ref, keep_ref, send_ref):
    senders = own_ref.shape[1]
    bit = (place_ref[2] // step) % 2
    for t in range(own_ref.shape[0] // 2):
        for target_ref, side in ((keep_ref, bit), (send_ref, 1 - bit)):
            target_ref[t, :senders] = own_ref[2 * t + side]
            target_ref[t, senders:] = received_ref[2 * t + side]


def start_reading(pairs, semaphores):
    copies = []
    for source_ref, target_ref in pairs:
        for block in range(target_ref.shape[0] // LANES):
            group = pl.ds(block * LANES, LANES)
            semaphore = semaphores.at[len(copies)]
            copy = pltpu.make_async_copy(source_ref.at[group], target_ref.at[group], semaphore)
            copy.start()
            copies.append(copy)
    return copies


def unit_of(field_hbm, target_ref, unit):
    height, tiles = target_ref.shape[:2]
    rows = pl.ds(unit % 2 * height, height)
    return field_hbm.at[rows, pl.ds(unit // 2 * tiles, tiles)], target_ref


def bias_kernel(
    place_ref, own_ref, received_ref, vectors_ref, field_hbm, keep_ref, send_ref, unit_ref, semaphores
):
    copies = start_reading([unit_of(field_hbm, unit_ref, 1)], semaphores)
    angles = jnp.concatenate([own_ref[...], received_ref[...]], 0)
    bias = dot(vectors_ref[...], angles, ((1,), (1,))).T
    half = bias.shape[1] // 2
    first, second = bias[:, :half], bias[:, half:]
    low = place_ref[1] == 0
    keep_ref[...] = jnp.where(low, first, second)
    send_ref[...] = jnp.where(low, second, first)
    for copy in copies:
        copy.wait()


def add_kernel(left_ref, right_ref, out_ref, rounded_ref):
    total = left_ref[...] + right_ref[...].astype(FULL)
    out_ref[...] = total
    rounded_ref[...] = total.astype(HALF)


def coefficient_kernel(
    place_ref, source_ref, others_ref, left_ref, right_ref, samples_ref, out_ref, bias_ref, row_ref
):
    bias_ref[...] = left_ref[...] + right_ref[...].astype(FULL)
    count, half = bias_ref.shape
    lanes = pl.ds(pl.multiple_of(place_ref[1] * half, LANES), half)
    for i in range(count // 2):
        walker, relative = wanted_walker(place_ref, source_ref, others_ref, i, count // 2)
        row_ref[2 * i : 2 * i + 1] = bias_ref[pl.ds(2 * relative + 1, 1)]
        drawn = samples_ref[pl.ds(walker, 1), lanes]
        row_ref[2 * i + 1 : 2 * i + 2] = drawn - bias_ref[pl.ds(2 * relative, 1)]
    out_ref[...] = row_ref[...].astype(HALF)


def read_kernel(half_hbm, field_hbm, half_ref, unit_ref, semaphores):
    pairs = [(half_hbm, half_ref), unit_of(field_hbm, unit_ref, 0)]
    for copy in start_reading(pairs, semaphores):
        copy.wait()


def read_early(half_vectors, tiled_vectors, unit_shape):
    return pl.pallas_call(
        read_kernel,
        in_specs=[pl.BlockSpec(memory_space=pl.ANY)] * 2,
        out_specs=[ARRAY] * 2,
        out_shape=[jax.ShapeDtypeStruct(half_vectors.shape, HALF), unit_shape],
        scratch_shapes=[
            pltpu.SemaphoreType.DMA(((half_vectors.shape[0] + unit_shape.shape[0]) // LANES,))
        ],
        compiler_params=pltpu.CompilerParams(vmem_limit_bytes=READ_LIMIT),
        name="read",
    )(half_vectors, tiled_vectors)


def field_kernel(part, wanted, mine, *refs):
    refs = list(refs)
    left_refs = [refs.pop(0) for _ in range(3 if part == 0 else 1)]
    unit_refs, field_hbm, own_ref, sent_ref = refs[:2], refs[2], refs[3], refs[4]
    refs = refs[5:]
    spread_ref = refs.pop(0) if part == 0 else left_refs[0]
    values_ref = refs.pop() if part == 0 else None
    copies = []
    if wanted:
        semaphores = refs.pop()
        pairs = [unit_of(field_hbm, ref, unit) for ref, unit in zip(refs, wanted)]
        copies = start_reading(pairs, semaphores)
    if part == 0:
        fill_spread(*left_refs, spread_ref, values_ref)
    height, tiles, _, orbitals = unit_refs[0].shape
    count = spread_ref.shape[0] // TILE
    depth = height * TILE
    total = None
    for block, unit_ref in enumerate(unit_refs):
        right = jnp.concatenate(
            [unit_ref[:, t].reshape(depth, orbitals) for t in range(tiles)], 1
        )
        product = dot(spread_ref[:, block * depth : (block + 1) * depth], right)
        total = product if total is None else total + product
    for t in range(tiles):
        slab = total[:, t * orbitals : (t + 1) * orbitals].reshape(count, TILE, orbitals)
        own_ref[:, t * TILE : (t + 1) * TILE] = slab[:mine]
        sent_ref[:, t * TILE : (t + 1) * TILE] = slab[mine:].astype(HALF)
    for copy in copies:
        copy.wait()


def field_rows(left, units, tiled_vectors, part, wanted, count, mine):
    height, tiles, _, orbitals = units[0].shape
    vectors = 2 * height
    rows = tiles * TILE
    out_shape = [
        jax.ShapeDtypeStruct((mine, rows, orbitals), FULL),
        jax.ShapeDtypeStruct((count - mine, rows, orbitals), HALF),
    ]
    if part == 0:
        out_shape.append(jax.ShapeDtypeStruct((count * TILE, vectors * TILE), HALF))
    out_shape += [jax.ShapeDtypeStruct(units[0].shape, HALF) for _ in wanted]
    scratch = []
    if wanted:
        scratch.append(pltpu.SemaphoreType.DMA((len(wanted) * height // LANES,)))
    if part == 0:
        scratch.append(VMEM((count * TILE, vectors), HALF))
    left_specs = [SCALARS, ARRAY, ARRAY] if part == 0 else [ARRAY]
    own, sent, *rest = pl.pallas_call(
        functools.partial(field_kernel, part, wanted, mine),
        in_specs=left_specs + [ARRAY] * 2 + [pl.BlockSpec(memory_space=pltpu.HBM)],
        out_specs=[ARRAY] * len(out_shape),
        out_shape=out_shape,
        scratch_shapes=scratch,
        compiler_params=pltpu.CompilerParams(vmem_limit_bytes=SMALL),
        cost_estimate=pl.CostEstimate(
            flops=2 * count * TILE * vectors * rows * orbitals,
            bytes_accessed=2 * vectors * rows * orbitals,
            transcendentals=0,
        ),
        name="field",
    )(*left, *units, tiled_vectors)
    left = [rest.pop(0)] if part == 0 else left
    return own, sent, left, rest


def combine_kernel(chunks, *refs):
    own_refs, received_refs, out_ref = refs[:chunks], refs[chunks:-1], refs[-1]
    others = len(received_refs) // chunks
    rows = own_refs[0].shape[2]
    for c in range(chunks):
        total = own_refs[c][...]
        for received_ref in received_refs[c * others : (c + 1) * others]:
            total = total + received_ref[...].astype(FULL)
        out_ref[:, :, c * rows : (c + 1) * rows] = total.astype(HALF)


def combine(owns, received):
    chunks = len(owns)
    slots, parts, rows, orbitals = owns[0].shape
    return pl.pallas_call(
        functools.partial(combine_kernel, chunks),
        out_shape=jax.ShapeDtypeStruct((slots, parts, rows * chunks, orbitals), HALF),
        in_specs=[pl.BlockSpec(memory_space=VMEM)] * (chunks + len(received)),
        out_specs=pl.BlockSpec(memory_space=VMEM),
        compiler_params=pltpu.CompilerParams(vmem_limit_bytes=SMALL),
        name="combine",
    )(*owns, *received)


def walker_kernel(count, orbitals, electrons, rank_ref, field_piece_ref, *refs):
    start_refs = refs[:count]
    out_ref, field_ref, start_wide_ref = refs[count:]
    blocks, _, rows, _ = field_piece_ref.shape
    wide = start_wide_ref.shape[1] // 2
    start_wide_ref[...] = jnp.zeros_like(start_wide_ref)
    for r in range(blocks):
        for c in range(2):
            field_ref[pl.ds(c * orbitals + r * rows, rows)] = field_piece_ref[r, c]
    block = 0
    for start_ref in start_refs:
        for d in range(start_ref.shape[0]):
            at = pl.multiple_of((rank_ref[0] ^ block) * rows, 2 * TILE)
            for c in range(2):
                start_wide_ref[pl.ds(at, rows), pl.ds(c * wide, electrons)] = start_ref[d, c]
            block += 1
    current = start_wide_ref[...]
    summed = current.astype(FULL)
    for order in range(1, TERMS + 1):
        product = dot(field_ref[...], current)
        top, low = product[:orbitals], product[orbitals:]
        following = jnp.concatenate(
            [top[:, :wide] - low[:, wide:], top[:, wide:] + low[:, :wide]], 1
        )
        following = following * (1.0 / order)
        summed = summed + following
        current = following.astype(HALF)

    high, low = split_half(summed)
    rows_first = ((0,), (0,))
    gram = dot(high, high, rows_first) + dot(high, low, rows_first) + dot(low, high, rows_first)
    gram_real = (gram[:wide, :wide] + gram[wide:, wide:]) * (1.0 / orbitals)
    gram_imag = (gram[:wide, wide:] - gram[wide:, :wide]) * (1.0 / orbitals)
    row = lax.broadcasted_iota(jnp.int32, (wide, wide), 0)
    column = lax.broadcasted_iota(jnp.int32, (wide, wide), 1)
    identity = jnp.where((row == column) & (row < electrons), 1.0, 0.0)
    scale = jnp.sum(gram_real * identity, axis=0, keepdims=True)
    scale = jnp.sum(scale, axis=1, keepdims=True) * (1.0 / electrons)

    def times(left, right):
        product = fine_dot(jnp.concatenate(left, 0), jnp.concatenate(right, 1))
        real = product[:wide, :wide] - product[wide:, wide:]
        return real, product[:wide, wide:] + product[wide:, :wide]

    iterate = (gram_real / scale, gram_imag / scale)
    root = None
    for sweep in range(NS_STEPS):
        real, imag = iterate if root is None else times(root, iterate)
        step = (1.5 * identity - 0.5 * real, -0.5 * imag)
        if sweep + 1 < NS_STEPS:
            iterate = times(iterate, step)
        root = step if root is None else times(step, root)
    inverse = lax.rsqrt(scale)
    root = jnp.concatenate([root[0] * inverse, root[1] * inverse], 1)
    product = fine_dot(jnp.concatenate([summed[:, :wide], summed[:, wide:]], 0), root)
    top, low = product[:orbitals], product[orbitals:]
    real = (top[:, :wide] - low[:, wide:]).astype(HALF)
    imag = (top[:, wide:] + low[:, :wide]).astype(HALF)
    for r in range(blocks):
        out_ref[r, 0] = real[r * rows : (r + 1) * rows, :electrons]
        out_ref[r, 1] = imag[r * rows : (r + 1) * rows, :electrons]


def walker_step(rank, field, starts):
    blocks, parts, rows, orbitals = field.shape
    electrons = starts[0].shape[3]
    wide = -(-electrons // LANES) * LANES
    return local_kernel(
        functools.partial(walker_kernel, len(starts), orbitals, electrons),
        [SCALARS] + [ARRAY] * (1 + len(starts)),
        jax.ShapeDtypeStruct((blocks, parts, rows, electrons), HALF),
        [VMEM((2 * orbitals, orbitals), HALF), VMEM((orbitals, 2 * wide), HALF)],
        SMALL,
    )(rank, field, *starts)


def shift(value, axis, step):
    size = lax.axis_size(axis)
    return lax.ppermute(value, axis, [(i, (i + step) % size) for i in range(size)])


def scatter_sum(value, axis, dim):
    size = lax.axis_size(axis)
    here = lax.axis_index(axis)
    width = value.shape[dim] // size
    total = lax.dynamic_slice_in_dim(value, here * width, width, dim)
    for s in range(1, size):
        block = lax.dynamic_slice_in_dim(value, ((here + s) % size) * width, width, dim)
        total = total + shift(block, axis, s)
    return total


def gather_ordered(value, axis, dim):
    size = lax.axis_size(axis)
    here = lax.axis_index(axis)
    width = value.shape[dim]
    shape = list(value.shape)
    shape[dim] = width * size
    whole = jnp.zeros(shape, value.dtype)
    for s in range(size):
        block = value if s == 0 else shift(value, axis, s)
        whole = lax.dynamic_update_slice_in_dim(whole, block, ((here - s) % size) * width, dim)
    return whole


def exchange_sum(value, axis):
    size = lax.axis_size(axis)
    if size & (size - 1):
        return sum([shift(value, axis, s) for s in range(1, size)], value)
    step = 1
    while step < size:
        value = value + lax.ppermute(value, axis, [(i, i ^ step) for i in range(size)])
        step *= 2
    return value


def whole_step(walkers, correlation_inverse, half_vectors, field_vectors, samples, source):
    local = walkers.shape[0]
    vectors, row_block, orbitals = field_vectors.shape
    electrons = correlation_inverse.shape[2]
    planes = lax.axis_size("walk")
    population = local * planes
    count = population * 2
    devices_rows = lax.axis_size(ROWS)
    sharers = devices_rows // local
    first = lax.axis_index("walk") * local
    core = lax.axis_index("orb")
    chol = lax.axis_size("chol")
    half = vectors // 2
    fast = (
        row_block % (2 * TILE) == 0
        and vectors % (2 * LANES) == 0
        and lax.axis_size("orb") == 2
        and planes > 1
        and sharers == 1
        and chol & (chol - 1) == 0
    )

    def to_owners(value):
        value = jnp.broadcast_to(value[:, None], (local, sharers) + value.shape[1:])
        value = value.reshape((devices_rows,) + value.shape[2:])
        return lax.all_to_all(value, ROWS, split_axis=0, concat_axis=0, tiled=True)

    def others(value):
        return jnp.concatenate([shift(value, "walk", -s) for s in range(1, planes)], 0)

    def from_planes(sent):
        blocks = [sent[s * local : (s + 1) * local] for s in range(planes - 1)]
        return [shift(block, "walk", s + 1) for s, block in enumerate(blocks)]

    other_source = others(source)
    place = jnp.stack([first, core, lax.axis_index("chol")]).astype(jnp.int32)
    rank = lax.axis_index(ROWS).astype(jnp.int32).reshape(1)
    grid = walkers.reshape(local, 2, row_block, electrons)
    theta = local_kernel(
        theta_kernel, [ARRAY] * 2, jax.ShapeDtypeStruct(grid.shape, HALF), limit=SMALL
    )(grid, correlation_inverse)
    theta = theta.reshape(local * 2, row_block * electrons)
    other_theta = others(theta)
    start = grid.astype(HALF)
    other_start = others(start)

    if fast:
        tiled_vectors = field_vectors.reshape(vectors, row_block // TILE, TILE, orbitals)
        unit_shape = jax.ShapeDtypeStruct((half, 2, TILE, orbitals), HALF)
        half_vectors, unit = read_early(half_vectors, tiled_vectors, unit_shape)
        block = (2, row_block, electrons)
        slots = jax.ShapeDtypeStruct((local // 2, 1) + block, HALF)
        keep, sent = local_kernel(
            pick_kernel,
            [SCALARS] * 2 + [ARRAY] * 2,
            [slots] * 2,
            [VMEM((population,) + block, HALF)],
        )(place, source, start, other_start)
        passed = shift(sent, "orb", 1)
        part_shape = jax.ShapeDtypeStruct((count, half), FULL)
        bias, sent, other_unit = local_kernel(
            bias_kernel,
            [SCALARS] + [ARRAY] * 3 + [pl.BlockSpec(memory_space=pltpu.HBM)],
            [part_shape, part_shape, unit_shape],
            [pltpu.SemaphoreType.DMA((half // LANES,))],
            SMALL,
        )(place, theta, other_theta, half_vectors, tiled_vectors)
        units = [unit, other_unit]
        received = shift(sent, "orb", 1)
        rounded_shape = jax.ShapeDtypeStruct(part_shape.shape, HALF)
        add = local_kernel(add_kernel, [ARRAY] * 2, [part_shape, rounded_shape])
        step = 1
        while step < chol:
            pairs = [(i, i ^ step) for i in range(chol)]
            bias, rounded = add(bias, received)
            received = lax.ppermute(rounded, "chol", pairs)
            slots = jax.ShapeDtypeStruct((keep.shape[0] // 2, keep.shape[1] * 2) + block, HALF)
            keep, sent = local_kernel(
                functools.partial(split_kernel, step), [SCALARS] + [ARRAY] * 2, [slots] * 2
            )(place, keep, passed)
            passed = lax.ppermute(sent, "chol", pairs)
            step *= 2
        coefficient = local_kernel(
            coefficient_kernel,
            [SCALARS] * 3 + [ARRAY] * 3,
            jax.ShapeDtypeStruct((count, half), HALF),
            [VMEM((count, half), FULL)] * 2,
        )(place, source, other_source, bias, received, samples)
        other_half = shift(coefficient, "orb", 1)
        rows = 2 * TILE
        parts = row_block // rows
        owns, received = [], []
        left = [place, coefficient, other_half]
        for part in range(parts):
            have = 2 * part + len(units)
            wanted = range(have, max(have, min(2 * parts, 2 * part + 5)))
            own, sent, left, further = field_rows(
                left, units[:2], tiled_vectors, part, wanted, count, local * 2
            )
            units = units[2:] + further
            owns.append(own.reshape(local, 2, rows, orbitals))
            sent = sent.reshape(population - local, 2, rows, orbitals)
            received += from_planes(sent)
        field = to_owners(combine(owns, received))
        starts = [keep[0], passed[0]]
    else:
        wanted = jnp.concatenate([source, other_source], 0)
        relative = jnp.where(wanted < first, wanted - first + population, wanted - first)
        all_start = jnp.concatenate([start, other_start], 0)
        picked = all_start.at[relative[:local]].get(mode="promise_in_bounds")
        columns = to_owners(picked)
        angles = jnp.concatenate([theta, other_theta], 0)
        bias = jnp.einsum("ij,gj->ig", angles, half_vectors, preferred_element_type=FULL)
        bias = bias.reshape(population, 2, vectors)
        bias = exchange_sum(scatter_sum(bias, "orb", 2), "chol")
        bias = bias.at[relative].get(mode="promise_in_bounds")
        width = bias.shape[2]
        drawn = lax.dynamic_slice_in_dim(samples, core * width, width, 1)
        drawn = drawn.at[wanted].get(mode="promise_in_bounds")
        coefficient = jnp.stack([bias[:, 1], drawn - bias[:, 0]], 1).astype(HALF)
        coefficient = gather_ordered(coefficient, "orb", 2)
        field = jnp.einsum(
            "wcg,gab->wcab", coefficient, field_vectors, preferred_element_type=FULL
        )
        total = field[:local]
        for block in from_planes(field[local:].astype(HALF)):
            total = total + block
        field = to_owners(total.astype(HALF)).transpose(1, 0, 2, 3)
        field = field.reshape(1, 2, orbitals, orbitals)
        starts = [columns.transpose(1, 0, 2, 3).reshape(1, 2, orbitals, electrons)]
        rank = jnp.zeros((1,), jnp.int32)

    normalized = walker_step(rank, field, starts)
    if not fast:
        normalized = normalized.reshape(2, devices_rows, row_block, electrons)
        normalized = normalized.transpose(1, 0, 2, 3)
    if sharers > 1:
        share = lax.axis_index(ROWS) % sharers
        width = electrons // sharers
        normalized = lax.dynamic_slice_in_dim(normalized, share * width, width, 3)
    returned = lax.all_to_all(normalized, ROWS, split_axis=0, concat_axis=0, tiled=True)
    if sharers > 1:
        returned = returned.reshape(local, sharers, 2, row_block, width)
        returned = returned.transpose(0, 2, 3, 1, 4)
    return returned.reshape(local, 2, row_block * electrons).astype(FULL)


def solution(mesh):
    placed = (
        P(("groups", "walk"), None, ("chol", "orb")),
        P(("groups", "walk"), None, None, None),
        P(("groups", "walk"), ("chol", "orb")),
        P(("groups", "walk"), ("chol", "orb"), None),
        P("groups", "walk"),
        P(("groups", "walk")),
    )
    return jax.shard_map(
        whole_step,
        mesh=mesh,
        in_specs=placed,
        out_specs=P(("groups", "walk"), None, ("chol", "orb")),
        check_vma=False,
    )
```

```python
import functools

import jax
import jax.numpy as jnp
from jax import lax
from jax.experimental import pallas as pl
from jax.experimental.pallas import tpu as pltpu
from jax.sharding import PartitionSpec as P


TERMS = 4
NS_STEPS = 2
ROWS = ("chol", "orb")
HALF = jnp.bfloat16
FULL = jnp.float32
LANES = 128
TILE = 8
SMALL = 8 << 20
TINY = 2 << 20
READ_LIMIT = 36 << 20
VMEM = pltpu.VMEM


def split_half(value):
    high = value.astype(HALF)
    return high, (value - high.astype(FULL)).astype(HALF)


def dot(left, right, contract=((1,), (0,))):
    return lax.dot_general(left, right, (contract, ((), ())), preferred_element_type=FULL)


def fine_dot(left, right):
    left_high, left_low = split_half(left)
    right_high, right_low = split_half(right)
    height = left.shape[0]
    both = dot(jnp.concatenate([left_high, left_low], 0), right_high)
    return both[:height] + both[height:] + dot(left_high, right_low)


def theta_kernel(grid_ref, inverse_ref, theta_ref):
    rows = grid_ref.shape[2]
    for w in range(grid_ref.shape[0]):
        stacked = jnp.concatenate([grid_ref[w, 0], grid_ref[w, 1]], 0)
        by_real = fine_dot(stacked, inverse_ref[w, 0])
        by_imag = fine_dot(stacked, inverse_ref[w, 1])
        theta_ref[w, 0] = (by_real[:rows] - by_imag[rows:]).astype(HALF)
        theta_ref[w, 1] = (by_imag[:rows] + by_real[rows:]).astype(HALF)


def fill_spread(place_ref, own_ref, received_ref, spread_ref, values_ref):
    count, half = own_ref.shape
    height = count * TILE
    wide = LANES * TILE
    row = lax.broadcasted_iota(jnp.int32, (height, count), 0)
    column = lax.broadcasted_iota(jnp.int32, (height, count), 1)
    repeats = (row // TILE == column).astype(FULL).astype(HALF)
    low = place_ref[1] == 0
    own, received = own_ref[...].astype(FULL), received_ref[...].astype(FULL)
    values_ref[:, :half] = dot(repeats, jnp.where(low, own, received).astype(HALF)).astype(HALF)
    values_ref[:, half:] = dot(repeats, jnp.where(low, received, own).astype(HALF)).astype(HALF)
    row = lax.broadcasted_iota(jnp.int32, (LANES, wide), 0)
    column = lax.broadcasted_iota(jnp.int32, (LANES, wide), 1)
    copies = (column // TILE == row).astype(FULL).astype(HALF)
    a = lax.broadcasted_iota(jnp.int32, (TILE, wide), 0)
    b = lax.broadcasted_iota(jnp.int32, (TILE, wide), 1) % TILE
    keep = a == b

    @pl.loop(0, 2 * half // LANES)
    def _(block):
        values = values_ref[:, pl.ds(pl.multiple_of(block * LANES, LANES), LANES)]
        wider = dot(values, copies).reshape(count, TILE, wide)
        wider = jnp.where(keep[None], wider, 0.0).reshape(height, wide)
        spread_ref[:, pl.ds(pl.multiple_of(block * wide, wide), wide)] = wider.astype(HALF)


SCALARS = pl.BlockSpec(memory_space=pltpu.SMEM)
ARRAY = pl.BlockSpec(memory_space=VMEM)


def local_kernel(kernel, in_specs, out_shape, scratch_shapes=(), limit=TINY):
    return pl.pallas_call(
        kernel,
        in_specs=in_specs,
        out_specs=jax.tree.map(lambda _: ARRAY, out_shape),
        out_shape=out_shape,
        scratch_shapes=list(scratch_shapes),
        compiler_params=pltpu.CompilerParams(vmem_limit_bytes=limit),
    )


def wanted_walker(place_ref, source_ref, others_ref, i, population):
    local = source_ref.shape[0]
    walker = source_ref[i] if i < local else others_ref[i - local]
    relative = walker - place_ref[0]
    return walker, jnp.where(relative < 0, relative + population, relative)


def pick_kernel(place_ref, source_ref, own_ref, received_ref, keep_ref, send_ref, all_ref):
    local = own_ref.shape[0]
    population = all_ref.shape[0]
    all_ref[:local] = own_ref[...]
    all_ref[local:] = received_ref[...]
    for t in range(local // 2):
        for target_ref, core in ((keep_ref, place_ref[1]), (send_ref, 1 - place_ref[1])):
            relative = source_ref[2 * t + core] - place_ref[0]
            relative = jnp.where(relative < 0, relative + population, relative)
            target_ref[t, 0] = all_ref[relative]


def split_kernel(step, place_ref, own_ref, received_ref, keep_ref, send_ref):
    senders = own_ref.shape[1]
    bit = (place_ref[2] // step) % 2
    for t in range(own_ref.shape[0] // 2):
        for target_ref, side in ((keep_ref, bit), (send_ref, 1 - bit)):
            target_ref[t, :senders] = own_ref[2 * t + side]
            target_ref[t, senders:] = received_ref[2 * t + side]


def start_reading(pairs, semaphores):
    copies = []
    for source_ref, target_ref in pairs:
        for block in range(target_ref.shape[0] // LANES):
            group = pl.ds(block * LANES, LANES)
            semaphore = semaphores.at[len(copies)]
            copy = pltpu.make_async_copy(source_ref.at[group], target_ref.at[group], semaphore)
            copy.start()
            copies.append(copy)
    return copies


def unit_of(field_hbm, target_ref, unit):
    height, tiles = target_ref.shape[:2]
    rows = pl.ds(unit % 2 * height, height)
    return field_hbm.at[rows, pl.ds(unit // 2 * tiles, tiles)], target_ref


def bias_kernel(place_ref, own_ref, received_ref, vectors_ref, keep_ref, send_ref):
    angles = jnp.concatenate([own_ref[...], received_ref[...]], 0)
    bias = dot(vectors_ref[...], angles, ((1,), (1,))).T
    half = bias.shape[1] // 2
    first, second = bias[:, :half], bias[:, half:]
    low = place_ref[1] == 0
    keep_ref[...] = jnp.where(low, first, second)
    send_ref[...] = jnp.where(low, second, first)


def late_kernel(order_ref, field_hbm, unit_ref, semaphores):
    for copy in start_reading([unit_of(field_hbm, unit_ref, 1)], semaphores):
        copy.wait()


def add_kernel(left_ref, right_ref, out_ref, rounded_ref):
    total = left_ref[...] + right_ref[...].astype(FULL)
    out_ref[...] = total
    rounded_ref[...] = total.astype(HALF)


def coefficient_kernel(
    place_ref, source_ref, others_ref, left_ref, right_ref, samples_ref, out_ref, bias_ref, row_ref
):
    bias_ref[...] = left_ref[...] + right_ref[...].astype(FULL)
    count, half = bias_ref.shape
    lanes = pl.ds(pl.multiple_of(place_ref[1] * half, LANES), half)
    for i in range(count // 2):
        walker, relative = wanted_walker(place_ref, source_ref, others_ref, i, count // 2)
        row_ref[2 * i : 2 * i + 1] = bias_ref[pl.ds(2 * relative + 1, 1)]
        drawn = samples_ref[pl.ds(walker, 1), lanes]
        row_ref[2 * i + 1 : 2 * i + 2] = drawn - bias_ref[pl.ds(2 * relative, 1)]
    out_ref[...] = row_ref[...].astype(HALF)


def read_kernel(half_hbm, field_hbm, half_ref, unit_ref, semaphores):
    pairs = [(half_hbm, half_ref), unit_of(field_hbm, unit_ref, 0)]
    for copy in start_reading(pairs, semaphores):
        copy.wait()


def read_early(half_vectors, tiled_vectors, unit_shape):
    return pl.pallas_call(
        read_kernel,
        in_specs=[pl.BlockSpec(memory_space=pl.ANY)] * 2,
        out_specs=[ARRAY] * 2,
        out_shape=[jax.ShapeDtypeStruct(half_vectors.shape, HALF), unit_shape],
        scratch_shapes=[
            pltpu.SemaphoreType.DMA(((half_vectors.shape[0] + unit_shape.shape[0]) // LANES,))
        ],
        compiler_params=pltpu.CompilerParams(vmem_limit_bytes=READ_LIMIT),
        name="read",
    )(half_vectors, tiled_vectors)


def field_kernel(part, wanted, mine, *refs):
    refs = list(refs)
    left_refs = [refs.pop(0) for _ in range(3 if part == 0 else 1)]
    unit_refs, field_hbm, own_ref, sent_ref = refs[:2], refs[2], refs[3], refs[4]
    refs = refs[5:]
    spread_ref = refs.pop(0) if part == 0 else left_refs[0]
    values_ref = refs.pop() if part == 0 else None
    copies = []
    if wanted:
        semaphores = refs.pop()
        pairs = [unit_of(field_hbm, ref, unit) for ref, unit in zip(refs, wanted)]
        copies = start_reading(pairs, semaphores)
    if part == 0:
        fill_spread(*left_refs, spread_ref, values_ref)
    height, tiles, _, orbitals = unit_refs[0].shape
    count = spread_ref.shape[0] // TILE
    depth = height * TILE
    total = None
    for block, unit_ref in enumerate(unit_refs):
        right = jnp.concatenate(
            [unit_ref[:, t].reshape(depth, orbitals) for t in range(tiles)], 1
        )
        product = dot(spread_ref[:, block * depth : (block + 1) * depth], right)
        total = product if total is None else total + product
    for t in range(tiles):
        slab = total[:, t * orbitals : (t + 1) * orbitals].reshape(count, TILE, orbitals)
        own_ref[:, t * TILE : (t + 1) * TILE] = slab[:mine]
        sent_ref[:, t * TILE : (t + 1) * TILE] = slab[mine:].astype(HALF)
    for copy in copies:
        copy.wait()


def field_rows(left, units, tiled_vectors, part, wanted, count, mine):
    height, tiles, _, orbitals = units[0].shape
    vectors = 2 * height
    rows = tiles * TILE
    out_shape = [
        jax.ShapeDtypeStruct((mine, rows, orbitals), FULL),
        jax.ShapeDtypeStruct((count - mine, rows, orbitals), HALF),
    ]
    if part == 0:
        out_shape.append(jax.ShapeDtypeStruct((count * TILE, vectors * TILE), HALF))
    out_shape += [jax.ShapeDtypeStruct(units[0].shape, HALF) for _ in wanted]
    scratch = []
    if wanted:
        scratch.append(pltpu.SemaphoreType.DMA((len(wanted) * height // LANES,)))
    if part == 0:
        scratch.append(VMEM((count * TILE, vectors), HALF))
    left_specs = [SCALARS, ARRAY, ARRAY] if part == 0 else [ARRAY]
    own, sent, *rest = pl.pallas_call(
        functools.partial(field_kernel, part, wanted, mine),
        in_specs=left_specs + [ARRAY] * 2 + [pl.BlockSpec(memory_space=pltpu.HBM)],
        out_specs=[ARRAY] * len(out_shape),
        out_shape=out_shape,
        scratch_shapes=scratch,
        compiler_params=pltpu.CompilerParams(vmem_limit_bytes=SMALL),
        cost_estimate=pl.CostEstimate(
            flops=2 * count * TILE * vectors * rows * orbitals,
            bytes_accessed=2 * vectors * rows * orbitals,
            transcendentals=0,
        ),
        name="field",
    )(*left, *units, tiled_vectors)
    left = [rest.pop(0)] if part == 0 else left
    return own, sent, left, rest


def combine_kernel(chunks, *refs):
    own_refs, received_refs, out_ref = refs[:chunks], refs[chunks:-1], refs[-1]
    others = len(received_refs) // chunks
    rows = own_refs[0].shape[2]
    for c in range(chunks):
        total = own_refs[c][...]
        for received_ref in received_refs[c * others : (c + 1) * others]:
            total = total + received_ref[...].astype(FULL)
        out_ref[:, :, c * rows : (c + 1) * rows] = total.astype(HALF)


def combine(owns, received):
    chunks = len(owns)
    slots, parts, rows, orbitals = owns[0].shape
    return pl.pallas_call(
        functools.partial(combine_kernel, chunks),
        out_shape=jax.ShapeDtypeStruct((slots, parts, rows * chunks, orbitals), HALF),
        in_specs=[pl.BlockSpec(memory_space=VMEM)] * (chunks + len(received)),
        out_specs=pl.BlockSpec(memory_space=VMEM),
        compiler_params=pltpu.CompilerParams(vmem_limit_bytes=SMALL),
        name="combine",
    )(*owns, *received)


def walker_kernel(count, orbitals, electrons, rank_ref, field_ref, *refs):
    start_refs = refs[:count]
    out_ref, start_wide_ref = refs[count:]
    blocks, _, rows, _ = field_ref.shape
    wide = start_wide_ref.shape[1] // 2
    start_wide_ref[...] = jnp.zeros_like(start_wide_ref)
    block = 0
    for start_ref in start_refs:
        for d in range(start_ref.shape[0]):
            at = pl.multiple_of((rank_ref[0] ^ block) * rows, 2 * TILE)
            for c in range(2):
                start_wide_ref[pl.ds(at, rows), pl.ds(c * wide, electrons)] = start_ref[d, c]
            block += 1
    current = start_wide_ref[...]
    summed = current.astype(FULL)
    for order in range(1, TERMS + 1):
        product = dot(field_ref[...].reshape(2 * orbitals, orbitals), current)
        product = product.reshape(blocks, 2, rows, 2 * wide)
        top = product[:, 0].reshape(orbitals, 2 * wide)
        low = product[:, 1].reshape(orbitals, 2 * wide)
        following = jnp.concatenate(
            [top[:, :wide] - low[:, wide:], top[:, wide:] + low[:, :wide]], 1
        )
        following = following * (1.0 / order)
        summed = summed + following
        current = following.astype(HALF)

    rounded = summed.astype(HALF)
    gram = dot(rounded, rounded, ((0,), (0,)))
    gram_real = (gram[:wide, :wide] + gram[wide:, wide:]) * (1.0 / orbitals)
    gram_imag = (gram[:wide, wide:] - gram[wide:, :wide]) * (1.0 / orbitals)
    row = lax.broadcasted_iota(jnp.int32, (wide, wide), 0)
    column = lax.broadcasted_iota(jnp.int32, (wide, wide), 1)
    identity = jnp.where((row == column) & (row < electrons), 1.0, 0.0)
    scale = jnp.sum(gram_real * identity, axis=0, keepdims=True)
    scale = jnp.sum(scale, axis=1, keepdims=True) * (1.0 / electrons)

    def times(left, right):
        product = fine_dot(jnp.concatenate(left, 0), jnp.concatenate(right, 1))
        real = product[:wide, :wide] - product[wide:, wide:]
        return real, product[:wide, wide:] + product[wide:, :wide]

    iterate = (gram_real / scale, gram_imag / scale)
    root = None
    for sweep in range(NS_STEPS):
        real, imag = iterate if root is None else times(root, iterate)
        step = (1.5 * identity - 0.5 * real, -0.5 * imag)
        if sweep + 1 < NS_STEPS:
            iterate = times(iterate, step)
        root = step if root is None else times(step, root)
    inverse = lax.rsqrt(scale)
    root = jnp.concatenate([root[0] * inverse, root[1] * inverse], 1)
    product = dot(jnp.concatenate([rounded[:, :wide], rounded[:, wide:]], 0), root.astype(HALF))
    top, low = product[:orbitals], product[orbitals:]
    real = (top[:, :wide] - low[:, wide:]).astype(HALF)
    imag = (top[:, wide:] + low[:, :wide]).astype(HALF)
    for r in range(blocks):
        out_ref[r, 0] = real[r * rows : (r + 1) * rows, :electrons]
        out_ref[r, 1] = imag[r * rows : (r + 1) * rows, :electrons]


def walker_step(rank, field, starts):
    blocks, parts, rows, orbitals = field.shape
    electrons = starts[0].shape[3]
    wide = -(-electrons // LANES) * LANES
    return local_kernel(
        functools.partial(walker_kernel, len(starts), orbitals, electrons),
        [SCALARS] + [ARRAY] * (1 + len(starts)),
        jax.ShapeDtypeStruct((blocks, parts, rows, electrons), HALF),
        [VMEM((orbitals, 2 * wide), HALF)],
        SMALL,
    )(rank, field, *starts)


def shift(value, axis, step):
    size = lax.axis_size(axis)
    return lax.ppermute(value, axis, [(i, (i + step) % size) for i in range(size)])


def scatter_sum(value, axis, dim):
    size = lax.axis_size(axis)
    here = lax.axis_index(axis)
    width = value.shape[dim] // size
    total = lax.dynamic_slice_in_dim(value, here * width, width, dim)
    for s in range(1, size):
        block = lax.dynamic_slice_in_dim(value, ((here + s) % size) * width, width, dim)
        total = total + shift(block, axis, s)
    return total


def gather_ordered(value, axis, dim):
    size = lax.axis_size(axis)
    here = lax.axis_index(axis)
    width = value.shape[dim]
    shape = list(value.shape)
    shape[dim] = width * size
    whole = jnp.zeros(shape, value.dtype)
    for s in range(size):
        block = value if s == 0 else shift(value, axis, s)
        whole = lax.dynamic_update_slice_in_dim(whole, block, ((here - s) % size) * width, dim)
    return whole


def exchange_sum(value, axis):
    size = lax.axis_size(axis)
    if size & (size - 1):
        return sum([shift(value, axis, s) for s in range(1, size)], value)
    step = 1
    while step < size:
        value = value + lax.ppermute(value, axis, [(i, i ^ step) for i in range(size)])
        step *= 2
    return value


def whole_step(walkers, correlation_inverse, half_vectors, field_vectors, samples, source):
    local = walkers.shape[0]
    vectors, row_block, orbitals = field_vectors.shape
    electrons = correlation_inverse.shape[2]
    planes = lax.axis_size("walk")
    population = local * planes
    count = population * 2
    devices_rows = lax.axis_size(ROWS)
    sharers = devices_rows // local
    first = lax.axis_index("walk") * local
    core = lax.axis_index("orb")
    chol = lax.axis_size("chol")
    half = vectors // 2
    fast = (
        row_block % (2 * TILE) == 0
        and vectors % (2 * LANES) == 0
        and lax.axis_size("orb") == 2
        and planes > 1
        and sharers == 1
        and chol & (chol - 1) == 0
    )

    def to_owners(value):
        value = jnp.broadcast_to(value[:, None], (local, sharers) + value.shape[1:])
        value = value.reshape((devices_rows,) + value.shape[2:])
        return lax.all_to_all(value, ROWS, split_axis=0, concat_axis=0, tiled=True)

    def others(value):
        return jnp.concatenate([shift(value, "walk", -s) for s in range(1, planes)], 0)

    def from_planes(sent):
        blocks = [sent[s * local : (s + 1) * local] for s in range(planes - 1)]
        return [shift(block, "walk", s + 1) for s, block in enumerate(blocks)]

    other_source = others(source)
    place = jnp.stack([first, core, lax.axis_index("chol")]).astype(jnp.int32)
    rank = lax.axis_index(ROWS).astype(jnp.int32).reshape(1)
    grid = walkers.reshape(local, 2, row_block, electrons)
    theta = local_kernel(
        theta_kernel, [ARRAY] * 2, jax.ShapeDtypeStruct(grid.shape, HALF), limit=SMALL
    )(grid, correlation_inverse)
    theta = theta.reshape(local * 2, row_block * electrons)
    other_theta = others(theta)
    start = grid.astype(HALF)
    other_start = others(start)

    if fast:
        tiled_vectors = field_vectors.reshape(vectors, row_block // TILE, TILE, orbitals)
        unit_shape = jax.ShapeDtypeStruct((half, 2, TILE, orbitals), HALF)
        half_vectors, unit = read_early(half_vectors, tiled_vectors, unit_shape)
        block = (2, row_block, electrons)
        slots = jax.ShapeDtypeStruct((local // 2, 1) + block, HALF)
        keep, sent = local_kernel(
            pick_kernel,
            [SCALARS] * 2 + [ARRAY] * 2,
            [slots] * 2,
            [VMEM((population,) + block, HALF)],
        )(place, source, start, other_start)
        passed = shift(sent, "orb", 1)
        part_shape = jax.ShapeDtypeStruct((count, half), FULL)
        bias, sent = local_kernel(
            bias_kernel, [SCALARS] + [ARRAY] * 3, [part_shape, part_shape], limit=SMALL
        )(place, theta, other_theta, half_vectors)
        hbm = pl.BlockSpec(memory_space=pltpu.HBM)
        received = shift(sent, "orb", 1)
        rounded_shape = jax.ShapeDtypeStruct(part_shape.shape, HALF)
        add = local_kernel(add_kernel, [ARRAY] * 2, [part_shape, rounded_shape])
        step = 1
        while step < chol:
            pairs = [(i, i ^ step) for i in range(chol)]
            bias, rounded = add(bias, received)
            received = lax.ppermute(rounded, "chol", pairs)
            slots = jax.ShapeDtypeStruct((keep.shape[0] // 2, keep.shape[1] * 2) + block, HALF)
            keep, sent = local_kernel(
                functools.partial(split_kernel, step), [SCALARS] + [ARRAY] * 2, [slots] * 2
            )(place, keep, passed)
            passed = lax.ppermute(sent, "chol", pairs)
            step *= 2
        other_unit = local_kernel(
            late_kernel,
            [hbm, hbm],
            unit_shape,
            [pltpu.SemaphoreType.DMA((half // LANES,))],
            3 * SMALL,
        )(bias, tiled_vectors)
        units = [unit, other_unit]
        coefficient = local_kernel(
            coefficient_kernel,
            [SCALARS] * 3 + [ARRAY] * 3,
            jax.ShapeDtypeStruct((count, half), HALF),
            [VMEM((count, half), FULL)] * 2,
        )(place, source, other_source, bias, received, samples)
        other_half = shift(coefficient, "orb", 1)
        rows = 2 * TILE
        parts = row_block // rows
        owns, received = [], []
        left = [place, coefficient, other_half]
        for part in range(parts):
            have = 2 * part + len(units)
            wanted = range(have, max(have, min(2 * parts, 2 * part + 5)))
            own, sent, left, further = field_rows(
                left, units[:2], tiled_vectors, part, wanted, count, local * 2
            )
            units = units[2:] + further
            owns.append(own.reshape(local, 2, rows, orbitals))
            sent = sent.reshape(population - local, 2, rows, orbitals)
            received += from_planes(sent)
        field = to_owners(combine(owns, received))
        starts = [keep[0], passed[0]]
    else:
        wanted = jnp.concatenate([source, other_source], 0)
        relative = jnp.where(wanted < first, wanted - first + population, wanted - first)
        all_start = jnp.concatenate([start, other_start], 0)
        picked = all_start.at[relative[:local]].get(mode="promise_in_bounds")
        columns = to_owners(picked)
        angles = jnp.concatenate([theta, other_theta], 0)
        bias = jnp.einsum("ij,gj->ig", angles, half_vectors, preferred_element_type=FULL)
        bias = bias.reshape(population, 2, vectors)
        bias = exchange_sum(scatter_sum(bias, "orb", 2), "chol")
        bias = bias.at[relative].get(mode="promise_in_bounds")
        width = bias.shape[2]
        drawn = lax.dynamic_slice_in_dim(samples, core * width, width, 1)
        drawn = drawn.at[wanted].get(mode="promise_in_bounds")
        coefficient = jnp.stack([bias[:, 1], drawn - bias[:, 0]], 1).astype(HALF)
        coefficient = gather_ordered(coefficient, "orb", 2)
        field = jnp.einsum(
            "wcg,gab->wcab", coefficient, field_vectors, preferred_element_type=FULL
        )
        total = field[:local]
        for block in from_planes(field[local:].astype(HALF)):
            total = total + block
        field = to_owners(total.astype(HALF)).transpose(1, 0, 2, 3)
        field = field.reshape(1, 2, orbitals, orbitals)
        starts = [columns.transpose(1, 0, 2, 3).reshape(1, 2, orbitals, electrons)]
        rank = jnp.zeros((1,), jnp.int32)

    normalized = walker_step(rank, field, starts)
    if not fast:
        normalized = normalized.reshape(2, devices_rows, row_block, electrons)
        normalized = normalized.transpose(1, 0, 2, 3)
    if sharers > 1:
        share = lax.axis_index(ROWS) % sharers
        width = electrons // sharers
        normalized = lax.dynamic_slice_in_dim(normalized, share * width, width, 3)
    returned = lax.all_to_all(normalized, ROWS, split_axis=0, concat_axis=0, tiled=True)
    if sharers > 1:
        returned = returned.reshape(local, sharers, 2, row_block, width)
        returned = returned.transpose(0, 2, 3, 1, 4)
    return returned.reshape(local, 2, row_block * electrons).astype(FULL)


def solution(mesh):
    placed = (
        P(("groups", "walk"), None, ("chol", "orb")),
        P(("groups", "walk"), None, None, None),
        P(("groups", "walk"), ("chol", "orb")),
        P(("groups", "walk"), ("chol", "orb"), None),
        P("groups", "walk"),
        P(("groups", "walk")),
    )
    return jax.shard_map(
        whole_step,
        mesh=mesh,
        in_specs=placed,
        out_specs=P(("groups", "walk"), None, ("chol", "orb")),
        check_vma=False,
    )
```

```python
import functools

import jax
import jax.numpy as jnp
from jax import lax
from jax.experimental import pallas as pl
from jax.experimental.pallas import tpu as pltpu
from jax.sharding import PartitionSpec as P


TERMS = 4
NS_STEPS = 2
ROWS = ("chol", "orb")
HALF = jnp.bfloat16
FULL = jnp.float32
LANES = 128
TILE = 8
SMALL = 8 << 20
TINY = 2 << 20
LINES_LIMIT = 56250000
READ_LIMIT = 36 << 20
VMEM = pltpu.VMEM


def split_half(value):
    high = value.astype(HALF)
    return high, (value - high.astype(FULL)).astype(HALF)


def dot(left, right, contract=((1,), (0,))):
    return lax.dot_general(left, right, (contract, ((), ())), preferred_element_type=FULL)


def fine_dot(left, right):
    left_high, left_low = split_half(left)
    right_high, right_low = split_half(right)
    height = left.shape[0]
    both = dot(jnp.concatenate([left_high, left_low], 0), right_high)
    return both[:height] + both[height:] + dot(left_high, right_low)


def theta_kernel(grid_ref, inverse_ref, theta_ref):
    rows = grid_ref.shape[2]
    for w in range(grid_ref.shape[0]):
        stacked = jnp.concatenate([grid_ref[w, 0], grid_ref[w, 1]], 0)
        by_real = fine_dot(stacked, inverse_ref[w, 0])
        by_imag = fine_dot(stacked, inverse_ref[w, 1])
        theta_ref[w, 0] = (by_real[:rows] - by_imag[rows:]).astype(HALF)
        theta_ref[w, 1] = (by_imag[:rows] + by_real[rows:]).astype(HALF)


def narrow_rows(first, second, third):
    lane = lax.broadcasted_iota(jnp.int32, first.shape, 1)
    part = LANES // 4
    return (
        first,
        jnp.where(lane < part, pltpu.roll(first, part, 1), pltpu.roll(second, part, 1)),
        jnp.where(lane < 2 * part, pltpu.roll(second, 2 * part, 1), pltpu.roll(third, 2 * part, 1)),
        pltpu.roll(third, 3 * part, 1),
    )


def lines_kernel(
    walkers_hbm, inverse_hbm, theta_ref, start_ref, walkers_ref, inverse_ref, rows_ref, semaphores
):
    first = pltpu.make_async_copy(walkers_hbm, walkers_ref, semaphores.at[0])
    first.start()
    copy = pltpu.make_async_copy(inverse_hbm, inverse_ref, semaphores.at[1])
    copy.start()
    first.wait()
    count, _, rows, electrons = theta_ref.shape
    for c in range(2):
        for k in range(rows // 4):
            lines = [
                walkers_ref[:, c, (3 * k + t) * LANES : (3 * k + t + 1) * LANES] for t in range(3)
            ]
            for s, narrow in enumerate(narrow_rows(*lines)):
                rows_ref[c, pl.ds(4 * k + s, count, stride=rows)] = narrow
    for w in range(count):
        for c in range(2):
            start_ref[w, c] = rows_ref[c, w * rows : (w + 1) * rows, :electrons].astype(HALF)
    copy.wait()
    for w in range(count):
        stacked = jnp.concatenate(
            [rows_ref[c, w * rows : (w + 1) * rows, :electrons] for c in range(2)], 0
        )
        by_real = fine_dot(stacked, inverse_ref[w, 0])
        by_imag = fine_dot(stacked, inverse_ref[w, 1])
        theta_ref[w, 0] = (by_real[:rows] - by_imag[rows:]).astype(HALF)
        theta_ref[w, 1] = (by_imag[:rows] + by_real[rows:]).astype(HALF)


def fill_spread(place_ref, own_ref, received_ref, spread_ref, values_ref):
    count, half = own_ref.shape
    height = count * TILE
    wide = LANES * TILE
    row = lax.broadcasted_iota(jnp.int32, (height, count), 0)
    column = lax.broadcasted_iota(jnp.int32, (height, count), 1)
    repeats = (row // TILE == column).astype(FULL).astype(HALF)
    low = place_ref[1] == 0
    own, received = own_ref[...].astype(FULL), received_ref[...].astype(FULL)
    values_ref[:, :half] = dot(repeats, jnp.where(low, own, received).astype(HALF)).astype(HALF)
    values_ref[:, half:] = dot(repeats, jnp.where(low, received, own).astype(HALF)).astype(HALF)
    row = lax.broadcasted_iota(jnp.int32, (LANES, wide), 0)
    column = lax.broadcasted_iota(jnp.int32, (LANES, wide), 1)
    copies = (column // TILE == row).astype(FULL).astype(HALF)
    a = lax.broadcasted_iota(jnp.int32, (TILE, wide), 0)
    b = lax.broadcasted_iota(jnp.int32, (TILE, wide), 1) % TILE
    keep = a == b

    @pl.loop(0, 2 * half // LANES)
    def _(block):
        values = values_ref[:, pl.ds(pl.multiple_of(block * LANES, LANES), LANES)]
        wider = dot(values, copies).reshape(count, TILE, wide)
        wider = jnp.where(keep[None], wider, 0.0).reshape(height, wide)
        spread_ref[:, pl.ds(pl.multiple_of(block * wide, wide), wide)] = wider.astype(HALF)


SCALARS = pl.BlockSpec(memory_space=pltpu.SMEM)
ARRAY = pl.BlockSpec(memory_space=VMEM)


def local_kernel(kernel, in_specs, out_shape, scratch_shapes=(), limit=TINY):
    return pl.pallas_call(
        kernel,
        in_specs=in_specs,
        out_specs=jax.tree.map(lambda _: ARRAY, out_shape),
        out_shape=out_shape,
        scratch_shapes=list(scratch_shapes),
        compiler_params=pltpu.CompilerParams(vmem_limit_bytes=limit),
    )


def wanted_walker(place_ref, source_ref, others_ref, i, population):
    local = source_ref.shape[0]
    walker = source_ref[i] if i < local else others_ref[i - local]
    relative = walker - place_ref[0]
    return walker, jnp.where(relative < 0, relative + population, relative)


def pick_kernel(place_ref, source_ref, own_ref, received_ref, keep_ref, send_ref, all_ref):
    local = own_ref.shape[0]
    population = all_ref.shape[0]
    all_ref[:local] = own_ref[...]
    all_ref[local:] = received_ref[...]
    for t in range(local // 2):
        for target_ref, core in ((keep_ref, place_ref[1]), (send_ref, 1 - place_ref[1])):
            relative = source_ref[2 * t + core] - place_ref[0]
            relative = jnp.where(relative < 0, relative + population, relative)
            target_ref[t, 0] = all_ref[relative]


def split_kernel(step, place_ref, own_ref, received_ref, keep_ref, send_ref):
    senders = own_ref.shape[1]
    bit = (place_ref[2] // step) % 2
    for t in range(own_ref.shape[0] // 2):
        for target_ref, side in ((keep_ref, bit), (send_ref, 1 - bit)):
            target_ref[t, :senders] = own_ref[2 * t + side]
            target_ref[t, senders:] = received_ref[2 * t + side]


def start_reading(pairs, semaphores):
    copies = []
    for source_ref, target_ref in pairs:
        for block in range(target_ref.shape[0] // LANES):
            group = pl.ds(block * LANES, LANES)
            semaphore = semaphores.at[len(copies)]
            copy = pltpu.make_async_copy(source_ref.at[group], target_ref.at[group], semaphore)
            copy.start()
            copies.append(copy)
    return copies


def unit_of(field_hbm, target_ref, unit):
    height, tiles = target_ref.shape[:2]
    rows = pl.ds(unit % 2 * height, height)
    return field_hbm.at[rows, pl.ds(unit // 2 * tiles, tiles)], target_ref


def bias_kernel(place_ref, own_ref, received_ref, vectors_ref, keep_ref, send_ref):
    angles = jnp.concatenate([own_ref[...], received_ref[...]], 0)
    bias = dot(vectors_ref[...], angles, ((1,), (1,))).T
    half = bias.shape[1] // 2
    first, second = bias[:, :half], bias[:, half:]
    low = place_ref[1] == 0
    keep_ref[...] = jnp.where(low, first, second)
    send_ref[...] = jnp.where(low, second, first)


def late_kernel(order_ref, field_hbm, unit_ref, semaphores):
    for copy in start_reading([unit_of(field_hbm, unit_ref, 1)], semaphores):
        copy.wait()


def add_kernel(left_ref, right_ref, out_ref, rounded_ref):
    total = left_ref[...] + right_ref[...].astype(FULL)
    out_ref[...] = total
    rounded_ref[...] = total.astype(HALF)


def coefficient_kernel(
    place_ref, source_ref, others_ref, left_ref, right_ref, samples_ref, out_ref, bias_ref, row_ref
):
    bias_ref[...] = left_ref[...] + right_ref[...].astype(FULL)
    count, half = bias_ref.shape
    lanes = pl.ds(pl.multiple_of(place_ref[1] * half, LANES), half)
    for i in range(count // 2):
        walker, relative = wanted_walker(place_ref, source_ref, others_ref, i, count // 2)
        row_ref[2 * i : 2 * i + 1] = bias_ref[pl.ds(2 * relative + 1, 1)]
        drawn = samples_ref[pl.ds(walker, 1), lanes]
        row_ref[2 * i + 1 : 2 * i + 2] = drawn - bias_ref[pl.ds(2 * relative, 1)]
    out_ref[...] = row_ref[...].astype(HALF)


def read_kernel(half_hbm, field_hbm, half_ref, unit_ref, semaphores):
    pairs = [(half_hbm, half_ref), unit_of(field_hbm, unit_ref, 0)]
    for copy in start_reading(pairs, semaphores):
        copy.wait()


def read_early(half_vectors, tiled_vectors, unit_shape):
    return pl.pallas_call(
        read_kernel,
        in_specs=[pl.BlockSpec(memory_space=pl.ANY)] * 2,
        out_specs=[ARRAY] * 2,
        out_shape=[jax.ShapeDtypeStruct(half_vectors.shape, HALF), unit_shape],
        scratch_shapes=[
            pltpu.SemaphoreType.DMA(((half_vectors.shape[0] + unit_shape.shape[0]) // LANES,))
        ],
        compiler_params=pltpu.CompilerParams(vmem_limit_bytes=READ_LIMIT),
        name="read",
    )(half_vectors, tiled_vectors)


def field_kernel(part, wanted, mine, *refs):
    refs = list(refs)
    left_refs = [refs.pop(0) for _ in range(3 if part == 0 else 1)]
    unit_refs, field_hbm, own_ref, sent_ref = refs[:2], refs[2], refs[3], refs[4]
    refs = refs[5:]
    spread_ref = refs.pop(0) if part == 0 else left_refs[0]
    values_ref = refs.pop() if part == 0 else None
    copies = []
    if wanted:
        semaphores = refs.pop()
        pairs = [unit_of(field_hbm, ref, unit) for ref, unit in zip(refs, wanted)]
        copies = start_reading(pairs, semaphores)
    if part == 0:
        fill_spread(*left_refs, spread_ref, values_ref)
    height, tiles, _, orbitals = unit_refs[0].shape
    count = spread_ref.shape[0] // TILE
    depth = height * TILE
    total = None
    for block, unit_ref in enumerate(unit_refs):
        right = jnp.concatenate(
            [unit_ref[:, t].reshape(depth, orbitals) for t in range(tiles)], 1
        )
        product = dot(spread_ref[:, block * depth : (block + 1) * depth], right)
        total = product if total is None else total + product
    for t in range(tiles):
        slab = total[:, t * orbitals : (t + 1) * orbitals].reshape(count, TILE, orbitals)
        own_ref[:, t * TILE : (t + 1) * TILE] = slab[:mine]
        sent_ref[:, t * TILE : (t + 1) * TILE] = slab[mine:].astype(HALF)
    for copy in copies:
        copy.wait()


def field_rows(left, units, tiled_vectors, part, wanted, count, mine):
    height, tiles, _, orbitals = units[0].shape
    vectors = 2 * height
    rows = tiles * TILE
    out_shape = [
        jax.ShapeDtypeStruct((mine, rows, orbitals), FULL),
        jax.ShapeDtypeStruct((count - mine, rows, orbitals), HALF),
    ]
    if part == 0:
        out_shape.append(jax.ShapeDtypeStruct((count * TILE, vectors * TILE), HALF))
    out_shape += [jax.ShapeDtypeStruct(units[0].shape, HALF) for _ in wanted]
    scratch = []
    if wanted:
        scratch.append(pltpu.SemaphoreType.DMA((len(wanted) * height // LANES,)))
    if part == 0:
        scratch.append(VMEM((count * TILE, vectors), HALF))
    left_specs = [SCALARS, ARRAY, ARRAY] if part == 0 else [ARRAY]
    own, sent, *rest = pl.pallas_call(
        functools.partial(field_kernel, part, wanted, mine),
        in_specs=left_specs + [ARRAY] * 2 + [pl.BlockSpec(memory_space=pltpu.HBM)],
        out_specs=[ARRAY] * len(out_shape),
        out_shape=out_shape,
        scratch_shapes=scratch,
        compiler_params=pltpu.CompilerParams(vmem_limit_bytes=SMALL),
        cost_estimate=pl.CostEstimate(
            flops=2 * count * TILE * vectors * rows * orbitals,
            bytes_accessed=2 * vectors * rows * orbitals,
            transcendentals=0,
        ),
        name="field",
    )(*left, *units, tiled_vectors)
    left = [rest.pop(0)] if part == 0 else left
    return own, sent, left, rest


def combine_kernel(chunks, *refs):
    own_refs, received_refs, out_ref = refs[:chunks], refs[chunks:-1], refs[-1]
    others = len(received_refs) // chunks
    rows = own_refs[0].shape[2]
    for c in range(chunks):
        total = own_refs[c][...]
        for received_ref in received_refs[c * others : (c + 1) * others]:
            total = total + received_ref[...].astype(FULL)
        out_ref[:, :, c * rows : (c + 1) * rows] = total.astype(HALF)


def combine(owns, received):
    chunks = len(owns)
    slots, parts, rows, orbitals = owns[0].shape
    return pl.pallas_call(
        functools.partial(combine_kernel, chunks),
        out_shape=jax.ShapeDtypeStruct((slots, parts, rows * chunks, orbitals), HALF),
        in_specs=[pl.BlockSpec(memory_space=VMEM)] * (chunks + len(received)),
        out_specs=pl.BlockSpec(memory_space=VMEM),
        compiler_params=pltpu.CompilerParams(vmem_limit_bytes=SMALL),
        name="combine",
    )(*owns, *received)


def walker_kernel(count, orbitals, electrons, rank_ref, field_ref, *refs):
    start_refs = refs[:count]
    out_ref, start_wide_ref = refs[count:]
    blocks, _, rows, _ = field_ref.shape
    wide = start_wide_ref.shape[1] // 2
    start_wide_ref[...] = jnp.zeros_like(start_wide_ref)
    block = 0
    for start_ref in start_refs:
        for d in range(start_ref.shape[0]):
            at = pl.multiple_of((rank_ref[0] ^ block) * rows, 2 * TILE)
            for c in range(2):
                start_wide_ref[pl.ds(at, rows), pl.ds(c * wide, electrons)] = start_ref[d, c]
            block += 1
    current = start_wide_ref[...]
    summed = current.astype(FULL)
    for order in range(1, TERMS + 1):
        product = dot(field_ref[...].reshape(2 * orbitals, orbitals), current)
        product = product.reshape(blocks, 2, rows, 2 * wide)
        top = product[:, 0].reshape(orbitals, 2 * wide)
        low = product[:, 1].reshape(orbitals, 2 * wide)
        following = jnp.concatenate(
            [top[:, :wide] - low[:, wide:], top[:, wide:] + low[:, :wide]], 1
        )
        following = following * (1.0 / order)
        summed = summed + following
        current = following.astype(HALF)

    rounded = summed.astype(HALF)
    gram = dot(rounded, rounded, ((0,), (0,)))
    gram_real = (gram[:wide, :wide] + gram[wide:, wide:]) * (1.0 / orbitals)
    gram_imag = (gram[:wide, wide:] - gram[wide:, :wide]) * (1.0 / orbitals)
    row = lax.broadcasted_iota(jnp.int32, (wide, wide), 0)
    column = lax.broadcasted_iota(jnp.int32, (wide, wide), 1)
    identity = jnp.where((row == column) & (row < electrons), 1.0, 0.0)
    scale = jnp.sum(gram_real * identity, axis=0, keepdims=True)
    scale = jnp.sum(scale, axis=1, keepdims=True) * (1.0 / electrons)

    def times(left, right):
        product = fine_dot(jnp.concatenate(left, 0), jnp.concatenate(right, 1))
        real = product[:wide, :wide] - product[wide:, wide:]
        return real, product[:wide, wide:] + product[wide:, :wide]

    iterate = (gram_real / scale, gram_imag / scale)
    root = None
    for sweep in range(NS_STEPS):
        real, imag = iterate if root is None else times(root, iterate)
        step = (1.5 * identity - 0.5 * real, -0.5 * imag)
        if sweep + 1 < NS_STEPS:
            iterate = times(iterate, step)
        root = step if root is None else times(step, root)
    inverse = lax.rsqrt(scale)
    root = jnp.concatenate([root[0] * inverse, root[1] * inverse], 1)
    product = dot(jnp.concatenate([rounded[:, :wide], rounded[:, wide:]], 0), root.astype(HALF))
    top, low = product[:orbitals], product[orbitals:]
    real = (top[:, :wide] - low[:, wide:]).astype(HALF)
    imag = (top[:, wide:] + low[:, :wide]).astype(HALF)
    for r in range(blocks):
        out_ref[r, 0] = real[r * rows : (r + 1) * rows, :electrons]
        out_ref[r, 1] = imag[r * rows : (r + 1) * rows, :electrons]


def walker_step(rank, field, starts):
    blocks, parts, rows, orbitals = field.shape
    electrons = starts[0].shape[3]
    wide = -(-electrons // LANES) * LANES
    return local_kernel(
        functools.partial(walker_kernel, len(starts), orbitals, electrons),
        [SCALARS] + [ARRAY] * (1 + len(starts)),
        jax.ShapeDtypeStruct((blocks, parts, rows, electrons), HALF),
        [VMEM((orbitals, 2 * wide), HALF)],
        SMALL,
    )(rank, field, *starts)


def shift(value, axis, step):
    size = lax.axis_size(axis)
    return lax.ppermute(value, axis, [(i, (i + step) % size) for i in range(size)])


def scatter_sum(value, axis, dim):
    size = lax.axis_size(axis)
    here = lax.axis_index(axis)
    width = value.shape[dim] // size
    total = lax.dynamic_slice_in_dim(value, here * width, width, dim)
    for s in range(1, size):
        block = lax.dynamic_slice_in_dim(value, ((here + s) % size) * width, width, dim)
        total = total + shift(block, axis, s)
    return total


def gather_ordered(value, axis, dim):
    size = lax.axis_size(axis)
    here = lax.axis_index(axis)
    width = value.shape[dim]
    shape = list(value.shape)
    shape[dim] = width * size
    whole = jnp.zeros(shape, value.dtype)
    for s in range(size):
        block = value if s == 0 else shift(value, axis, s)
        whole = lax.dynamic_update_slice_in_dim(whole, block, ((here - s) % size) * width, dim)
    return whole


def exchange_sum(value, axis):
    size = lax.axis_size(axis)
    if size & (size - 1):
        return sum([shift(value, axis, s) for s in range(1, size)], value)
    step = 1
    while step < size:
        value = value + lax.ppermute(value, axis, [(i, i ^ step) for i in range(size)])
        step *= 2
    return value


def whole_step(walkers, correlation_inverse, half_vectors, field_vectors, samples, source):
    local = walkers.shape[0]
    vectors, row_block, orbitals = field_vectors.shape
    electrons = correlation_inverse.shape[2]
    planes = lax.axis_size("walk")
    population = local * planes
    count = population * 2
    devices_rows = lax.axis_size(ROWS)
    sharers = devices_rows // local
    first = lax.axis_index("walk") * local
    core = lax.axis_index("orb")
    chol = lax.axis_size("chol")
    half = vectors // 2
    fast = (
        row_block % (2 * TILE) == 0
        and vectors % (2 * LANES) == 0
        and lax.axis_size("orb") == 2
        and planes > 1
        and sharers == 1
        and chol & (chol - 1) == 0
    )

    def to_owners(value):
        value = jnp.broadcast_to(value[:, None], (local, sharers) + value.shape[1:])
        value = value.reshape((devices_rows,) + value.shape[2:])
        return lax.all_to_all(value, ROWS, split_axis=0, concat_axis=0, tiled=True)

    def others(value):
        return jnp.concatenate([shift(value, "walk", -s) for s in range(1, planes)], 0)

    def from_planes(sent):
        blocks = [sent[s * local : (s + 1) * local] for s in range(planes - 1)]
        return [shift(block, "walk", s + 1) for s, block in enumerate(blocks)]

    other_source = others(source)
    place = jnp.stack([first, core, lax.axis_index("chol")]).astype(jnp.int32)
    rank = lax.axis_index(ROWS).astype(jnp.int32).reshape(1)
    grid_shape = (local, 2, row_block, electrons)
    half_grid = jax.ShapeDtypeStruct(grid_shape, HALF)
    if fast and 4 * electrons == 3 * LANES and row_block % TILE == 0:
        theta, start = local_kernel(
            lines_kernel,
            [pl.BlockSpec(memory_space=pltpu.HBM)] * 2,
            [half_grid] * 2,
            [
                VMEM(walkers.shape, FULL),
                VMEM(correlation_inverse.shape, FULL),
                VMEM((2, local * row_block, LANES), FULL),
                pltpu.SemaphoreType.DMA((2,)),
            ],
            LINES_LIMIT,
        )(walkers, correlation_inverse)
    else:
        grid = walkers.reshape(grid_shape)
        start = grid.astype(HALF)
        theta = local_kernel(theta_kernel, [ARRAY] * 2, half_grid, limit=SMALL)(
            grid, correlation_inverse
        )
    theta = theta.reshape(local * 2, row_block * electrons)
    other_theta = others(theta)
    other_start = others(start)

    if fast:
        tiled_vectors = field_vectors.reshape(vectors, row_block // TILE, TILE, orbitals)
        unit_shape = jax.ShapeDtypeStruct((half, 2, TILE, orbitals), HALF)
        half_vectors, unit = read_early(half_vectors, tiled_vectors, unit_shape)
        block = (2, row_block, electrons)
        slots = jax.ShapeDtypeStruct((local // 2, 1) + block, HALF)
        keep, sent = local_kernel(
            pick_kernel,
            [SCALARS] * 2 + [ARRAY] * 2,
            [slots] * 2,
            [VMEM((population,) + block, HALF)],
        )(place, source, start, other_start)
        passed = shift(sent, "orb", 1)
        part_shape = jax.ShapeDtypeStruct((count, half), FULL)
        bias, sent = local_kernel(
            bias_kernel, [SCALARS] + [ARRAY] * 3, [part_shape, part_shape], limit=SMALL
        )(place, theta, other_theta, half_vectors)
        hbm = pl.BlockSpec(memory_space=pltpu.HBM)
        received = shift(sent, "orb", 1)
        rounded_shape = jax.ShapeDtypeStruct(part_shape.shape, HALF)
        add = local_kernel(add_kernel, [ARRAY] * 2, [part_shape, rounded_shape])
        step = 1
        while step < chol:
            pairs = [(i, i ^ step) for i in range(chol)]
            bias, rounded = add(bias, received)
            received = lax.ppermute(rounded, "chol", pairs)
            slots = jax.ShapeDtypeStruct((keep.shape[0] // 2, keep.shape[1] * 2) + block, HALF)
            keep, sent = local_kernel(
                functools.partial(split_kernel, step), [SCALARS] + [ARRAY] * 2, [slots] * 2
            )(place, keep, passed)
            passed = lax.ppermute(sent, "chol", pairs)
            step *= 2
        other_unit = local_kernel(
            late_kernel,
            [hbm, hbm],
            unit_shape,
            [pltpu.SemaphoreType.DMA((half // LANES,))],
            3 * SMALL,
        )(bias, tiled_vectors)
        units = [unit, other_unit]
        coefficient = local_kernel(
            coefficient_kernel,
            [SCALARS] * 3 + [ARRAY] * 3,
            jax.ShapeDtypeStruct((count, half), HALF),
            [VMEM((count, half), FULL)] * 2,
        )(place, source, other_source, bias, received, samples)
        other_half = shift(coefficient, "orb", 1)
        rows = 2 * TILE
        parts = row_block // rows
        owns, received = [], []
        left = [place, coefficient, other_half]
        for part in range(parts):
            have = 2 * part + len(units)
            wanted = range(have, max(have, min(2 * parts, 2 * part + 5)))
            own, sent, left, further = field_rows(
                left, units[:2], tiled_vectors, part, wanted, count, local * 2
            )
            units = units[2:] + further
            owns.append(own.reshape(local, 2, rows, orbitals))
            sent = sent.reshape(population - local, 2, rows, orbitals)
            received += from_planes(sent)
        field = to_owners(combine(owns, received))
        starts = [keep[0], passed[0]]
    else:
        wanted = jnp.concatenate([source, other_source], 0)
        relative = jnp.where(wanted < first, wanted - first + population, wanted - first)
        all_start = jnp.concatenate([start, other_start], 0)
        picked = all_start.at[relative[:local]].get(mode="promise_in_bounds")
        columns = to_owners(picked)
        angles = jnp.concatenate([theta, other_theta], 0)
        bias = jnp.einsum("ij,gj->ig", angles, half_vectors, preferred_element_type=FULL)
        bias = bias.reshape(population, 2, vectors)
        bias = exchange_sum(scatter_sum(bias, "orb", 2), "chol")
        bias = bias.at[relative].get(mode="promise_in_bounds")
        width = bias.shape[2]
        drawn = lax.dynamic_slice_in_dim(samples, core * width, width, 1)
        drawn = drawn.at[wanted].get(mode="promise_in_bounds")
        coefficient = jnp.stack([bias[:, 1], drawn - bias[:, 0]], 1).astype(HALF)
        coefficient = gather_ordered(coefficient, "orb", 2)
        field = jnp.einsum(
            "wcg,gab->wcab", coefficient, field_vectors, preferred_element_type=FULL
        )
        total = field[:local]
        for block in from_planes(field[local:].astype(HALF)):
            total = total + block
        field = to_owners(total.astype(HALF)).transpose(1, 0, 2, 3)
        field = field.reshape(1, 2, orbitals, orbitals)
        starts = [columns.transpose(1, 0, 2, 3).reshape(1, 2, orbitals, electrons)]
        rank = jnp.zeros((1,), jnp.int32)

    normalized = walker_step(rank, field, starts)
    if not fast:
        normalized = normalized.reshape(2, devices_rows, row_block, electrons)
        normalized = normalized.transpose(1, 0, 2, 3)
    if sharers > 1:
        share = lax.axis_index(ROWS) % sharers
        width = electrons // sharers
        normalized = lax.dynamic_slice_in_dim(normalized, share * width, width, 3)
    returned = lax.all_to_all(normalized, ROWS, split_axis=0, concat_axis=0, tiled=True)
    if sharers > 1:
        returned = returned.reshape(local, sharers, 2, row_block, width)
        returned = returned.transpose(0, 2, 3, 1, 4)
    return returned.reshape(local, 2, row_block * electrons).astype(FULL)


def solution(mesh):
    placed = (
        P(("groups", "walk"), None, ("chol", "orb")),
        P(("groups", "walk"), None, None, None),
        P(("groups", "walk"), ("chol", "orb")),
        P(("groups", "walk"), ("chol", "orb"), None),
        P("groups", "walk"),
        P(("groups", "walk")),
    )
    return jax.shard_map(
        whole_step,
        mesh=mesh,
        in_specs=placed,
        out_specs=P(("groups", "walk"), None, ("chol", "orb")),
        check_vma=False,
    )
```

```python
import functools

import jax
import jax.numpy as jnp
from jax import lax
from jax.experimental import pallas as pl
from jax.experimental.pallas import tpu as pltpu
from jax.sharding import PartitionSpec as P


TERMS = 4
NS_STEPS = 2
ROWS = ("chol", "orb")
HALF = jnp.bfloat16
FULL = jnp.float32
LANES = 128
TILE = 8
SMALL = 8 << 20
TINY = 2 << 20
LINES_LIMIT = 56250000
READ_LIMIT = 36 << 20
VMEM = pltpu.VMEM


def split_half(value):
    high = value.astype(HALF)
    return high, (value - high.astype(FULL)).astype(HALF)


def dot(left, right, contract=((1,), (0,))):
    return lax.dot_general(left, right, (contract, ((), ())), preferred_element_type=FULL)


def fine_dot(left, right):
    left_high, left_low = split_half(left)
    right_high, right_low = split_half(right)
    height = left.shape[0]
    both = dot(jnp.concatenate([left_high, left_low], 0), right_high)
    return both[:height] + both[height:] + dot(left_high, right_low)


def theta_kernel(grid_ref, inverse_ref, theta_ref):
    rows = grid_ref.shape[2]
    for w in range(grid_ref.shape[0]):
        stacked = jnp.concatenate([grid_ref[w, 0], grid_ref[w, 1]], 0)
        by_real = fine_dot(stacked, inverse_ref[w, 0])
        by_imag = fine_dot(stacked, inverse_ref[w, 1])
        theta_ref[w, 0] = (by_real[:rows] - by_imag[rows:]).astype(HALF)
        theta_ref[w, 1] = (by_imag[:rows] + by_real[rows:]).astype(HALF)


def narrow_rows(first, second, third):
    lane = lax.broadcasted_iota(jnp.int32, first.shape, 1)
    part = LANES // 4
    return (
        first,
        jnp.where(lane < part, pltpu.roll(first, part, 1), pltpu.roll(second, part, 1)),
        jnp.where(lane < 2 * part, pltpu.roll(second, 2 * part, 1), pltpu.roll(third, 2 * part, 1)),
        pltpu.roll(third, 3 * part, 1),
    )


def wide_lines(first, second, third, fourth):
    lane = lax.broadcasted_iota(jnp.int32, first.shape, 1)
    part = LANES // 4
    second, third = pltpu.roll(second, 3 * part, 1), pltpu.roll(third, 2 * part, 1)
    return (
        jnp.where(lane < 3 * part, first, second),
        jnp.where(lane < 2 * part, second, third),
        jnp.where(lane < part, third, pltpu.roll(fourth, part, 1)),
    )


def flatten_kernel(grid_ref, out_ref, rows_ref):
    count, _, rows, electrons = grid_ref.shape
    for w in range(count):
        for c in range(2):
            rows_ref[c, w * rows : (w + 1) * rows, :electrons] = grid_ref[w, c].astype(FULL)
    for c in range(2):
        for k in range(rows // 4):
            narrow = [rows_ref[c, pl.ds(4 * k + s, count, stride=rows)] for s in range(4)]
            for t, line in enumerate(wide_lines(*narrow)):
                out_ref[:, c, (3 * k + t) * LANES : (3 * k + t + 1) * LANES] = line


def lines_kernel(
    walkers_hbm, inverse_hbm, theta_ref, start_ref, walkers_ref, inverse_ref, rows_ref, semaphores
):
    first = pltpu.make_async_copy(walkers_hbm, walkers_ref, semaphores.at[0])
    first.start()
    copy = pltpu.make_async_copy(inverse_hbm, inverse_ref, semaphores.at[1])
    copy.start()
    first.wait()
    count, _, rows, electrons = theta_ref.shape
    for c in range(2):
        for k in range(rows // 4):
            lines = [
                walkers_ref[:, c, (3 * k + t) * LANES : (3 * k + t + 1) * LANES] for t in range(3)
            ]
            for s, narrow in enumerate(narrow_rows(*lines)):
                rows_ref[c, pl.ds(4 * k + s, count, stride=rows)] = narrow
    for w in range(count):
        for c in range(2):
            start_ref[w, c] = rows_ref[c, w * rows : (w + 1) * rows, :electrons].astype(HALF)
    copy.wait()
    for w in range(count):
        stacked = jnp.concatenate(
            [rows_ref[c, w * rows : (w + 1) * rows, :electrons] for c in range(2)], 0
        )
        by_real = fine_dot(stacked, inverse_ref[w, 0])
        by_imag = fine_dot(stacked, inverse_ref[w, 1])
        theta_ref[w, 0] = (by_real[:rows] - by_imag[rows:]).astype(HALF)
        theta_ref[w, 1] = (by_imag[:rows] + by_real[rows:]).astype(HALF)


def fill_spread(place_ref, own_ref, received_ref, spread_ref, values_ref):
    count, half = own_ref.shape
    height = count * TILE
    wide = LANES * TILE
    row = lax.broadcasted_iota(jnp.int32, (height, count), 0)
    column = lax.broadcasted_iota(jnp.int32, (height, count), 1)
    repeats = (row // TILE == column).astype(FULL).astype(HALF)
    low = place_ref[1] == 0
    own, received = own_ref[...].astype(FULL), received_ref[...].astype(FULL)
    values_ref[:, :half] = dot(repeats, jnp.where(low, own, received).astype(HALF)).astype(HALF)
    values_ref[:, half:] = dot(repeats, jnp.where(low, received, own).astype(HALF)).astype(HALF)
    row = lax.broadcasted_iota(jnp.int32, (LANES, wide), 0)
    column = lax.broadcasted_iota(jnp.int32, (LANES, wide), 1)
    copies = (column // TILE == row).astype(FULL).astype(HALF)
    a = lax.broadcasted_iota(jnp.int32, (TILE, wide), 0)
    b = lax.broadcasted_iota(jnp.int32, (TILE, wide), 1) % TILE
    keep = a == b

    @pl.loop(0, 2 * half // LANES)
    def _(block):
        values = values_ref[:, pl.ds(pl.multiple_of(block * LANES, LANES), LANES)]
        wider = dot(values, copies).reshape(count, TILE, wide)
        wider = jnp.where(keep[None], wider, 0.0).reshape(height, wide)
        spread_ref[:, pl.ds(pl.multiple_of(block * wide, wide), wide)] = wider.astype(HALF)


SCALARS = pl.BlockSpec(memory_space=pltpu.SMEM)
ARRAY = pl.BlockSpec(memory_space=VMEM)


def local_kernel(kernel, in_specs, out_shape, scratch_shapes=(), limit=TINY):
    return pl.pallas_call(
        kernel,
        in_specs=in_specs,
        out_specs=jax.tree.map(lambda _: ARRAY, out_shape),
        out_shape=out_shape,
        scratch_shapes=list(scratch_shapes),
        compiler_params=pltpu.CompilerParams(vmem_limit_bytes=limit),
    )


def wanted_walker(place_ref, source_ref, others_ref, i, population):
    local = source_ref.shape[0]
    walker = source_ref[i] if i < local else others_ref[i - local]
    relative = walker - place_ref[0]
    return walker, jnp.where(relative < 0, relative + population, relative)


def pick_kernel(place_ref, source_ref, own_ref, received_ref, keep_ref, send_ref, all_ref):
    local = own_ref.shape[0]
    population = all_ref.shape[0]
    all_ref[:local] = own_ref[...]
    all_ref[local:] = received_ref[...]
    for t in range(local // 2):
        for target_ref, core in ((keep_ref, place_ref[1]), (send_ref, 1 - place_ref[1])):
            relative = source_ref[2 * t + core] - place_ref[0]
            relative = jnp.where(relative < 0, relative + population, relative)
            target_ref[t, 0] = all_ref[relative]


def split_kernel(step, place_ref, own_ref, received_ref, keep_ref, send_ref):
    senders = own_ref.shape[1]
    bit = (place_ref[2] // step) % 2
    for t in range(own_ref.shape[0] // 2):
        for target_ref, side in ((keep_ref, bit), (send_ref, 1 - bit)):
            target_ref[t, :senders] = own_ref[2 * t + side]
            target_ref[t, senders:] = received_ref[2 * t + side]


def start_reading(pairs, semaphores):
    copies = []
    for source_ref, target_ref in pairs:
        for block in range(target_ref.shape[0] // LANES):
            group = pl.ds(block * LANES, LANES)
            semaphore = semaphores.at[len(copies)]
            copy = pltpu.make_async_copy(source_ref.at[group], target_ref.at[group], semaphore)
            copy.start()
            copies.append(copy)
    return copies


def unit_of(field_hbm, target_ref, unit):
    height, tiles = target_ref.shape[:2]
    rows = pl.ds(unit % 2 * height, height)
    return field_hbm.at[rows, pl.ds(unit // 2 * tiles, tiles)], target_ref


def bias_kernel(place_ref, own_ref, received_ref, vectors_ref, keep_ref, send_ref):
    angles = jnp.concatenate([own_ref[...], received_ref[...]], 0)
    bias = dot(vectors_ref[...], angles, ((1,), (1,))).T
    half = bias.shape[1] // 2
    first, second = bias[:, :half], bias[:, half:]
    low = place_ref[1] == 0
    keep_ref[...] = jnp.where(low, first, second)
    send_ref[...] = jnp.where(low, second, first)


def late_kernel(order_ref, field_hbm, unit_ref, semaphores):
    for copy in start_reading([unit_of(field_hbm, unit_ref, 1)], semaphores):
        copy.wait()


def add_kernel(left_ref, right_ref, out_ref, rounded_ref):
    total = left_ref[...] + right_ref[...].astype(FULL)
    out_ref[...] = total
    rounded_ref[...] = total.astype(HALF)


def coefficient_kernel(
    place_ref, source_ref, others_ref, left_ref, right_ref, samples_ref, out_ref, bias_ref, row_ref
):
    bias_ref[...] = left_ref[...] + right_ref[...].astype(FULL)
    count, half = bias_ref.shape
    lanes = pl.ds(pl.multiple_of(place_ref[1] * half, LANES), half)
    for i in range(count // 2):
        walker, relative = wanted_walker(place_ref, source_ref, others_ref, i, count // 2)
        row_ref[2 * i : 2 * i + 1] = bias_ref[pl.ds(2 * relative + 1, 1)]
        drawn = samples_ref[pl.ds(walker, 1), lanes]
        row_ref[2 * i + 1 : 2 * i + 2] = drawn - bias_ref[pl.ds(2 * relative, 1)]
    out_ref[...] = row_ref[...].astype(HALF)


def read_kernel(half_hbm, field_hbm, half_ref, unit_ref, semaphores):
    pairs = [(half_hbm, half_ref), unit_of(field_hbm, unit_ref, 0)]
    for copy in start_reading(pairs, semaphores):
        copy.wait()


def read_early(half_vectors, tiled_vectors, unit_shape):
    return pl.pallas_call(
        read_kernel,
        in_specs=[pl.BlockSpec(memory_space=pl.ANY)] * 2,
        out_specs=[ARRAY] * 2,
        out_shape=[jax.ShapeDtypeStruct(half_vectors.shape, HALF), unit_shape],
        scratch_shapes=[
            pltpu.SemaphoreType.DMA(((half_vectors.shape[0] + unit_shape.shape[0]) // LANES,))
        ],
        compiler_params=pltpu.CompilerParams(vmem_limit_bytes=READ_LIMIT),
        name="read",
    )(half_vectors, tiled_vectors)


def field_kernel(part, wanted, mine, *refs):
    refs = list(refs)
    left_refs = [refs.pop(0) for _ in range(3 if part == 0 else 1)]
    unit_refs, field_hbm, own_ref, sent_ref = refs[:2], refs[2], refs[3], refs[4]
    refs = refs[5:]
    spread_ref = refs.pop(0) if part == 0 else left_refs[0]
    values_ref = refs.pop() if part == 0 else None
    copies = []
    if wanted:
        semaphores = refs.pop()
        pairs = [unit_of(field_hbm, ref, unit) for ref, unit in zip(refs, wanted)]
        copies = start_reading(pairs, semaphores)
    if part == 0:
        fill_spread(*left_refs, spread_ref, values_ref)
    height, tiles, _, orbitals = unit_refs[0].shape
    count = spread_ref.shape[0] // TILE
    depth = height * TILE
    total = None
    for block, unit_ref in enumerate(unit_refs):
        right = jnp.concatenate(
            [unit_ref[:, t].reshape(depth, orbitals) for t in range(tiles)], 1
        )
        product = dot(spread_ref[:, block * depth : (block + 1) * depth], right)
        total = product if total is None else total + product
    for t in range(tiles):
        slab = total[:, t * orbitals : (t + 1) * orbitals].reshape(count, TILE, orbitals)
        own_ref[:, t * TILE : (t + 1) * TILE] = slab[:mine]
        sent_ref[:, t * TILE : (t + 1) * TILE] = slab[mine:].astype(HALF)
    for copy in copies:
        copy.wait()


def field_rows(left, units, tiled_vectors, part, wanted, count, mine):
    height, tiles, _, orbitals = units[0].shape
    vectors = 2 * height
    rows = tiles * TILE
    out_shape = [
        jax.ShapeDtypeStruct((mine, rows, orbitals), FULL),
        jax.ShapeDtypeStruct((count - mine, rows, orbitals), HALF),
    ]
    if part == 0:
        out_shape.append(jax.ShapeDtypeStruct((count * TILE, vectors * TILE), HALF))
    out_shape += [jax.ShapeDtypeStruct(units[0].shape, HALF) for _ in wanted]
    scratch = []
    if wanted:
        scratch.append(pltpu.SemaphoreType.DMA((len(wanted) * height // LANES,)))
    if part == 0:
        scratch.append(VMEM((count * TILE, vectors), HALF))
    left_specs = [SCALARS, ARRAY, ARRAY] if part == 0 else [ARRAY]
    own, sent, *rest = pl.pallas_call(
        functools.partial(field_kernel, part, wanted, mine),
        in_specs=left_specs + [ARRAY] * 2 + [pl.BlockSpec(memory_space=pltpu.HBM)],
        out_specs=[ARRAY] * len(out_shape),
        out_shape=out_shape,
        scratch_shapes=scratch,
        compiler_params=pltpu.CompilerParams(vmem_limit_bytes=SMALL),
        cost_estimate=pl.CostEstimate(
            flops=2 * count * TILE * vectors * rows * orbitals,
            bytes_accessed=2 * vectors * rows * orbitals,
            transcendentals=0,
        ),
        name="field",
    )(*left, *units, tiled_vectors)
    left = [rest.pop(0)] if part == 0 else left
    return own, sent, left, rest


def combine_kernel(chunks, *refs):
    own_refs, received_refs, out_ref = refs[:chunks], refs[chunks:-1], refs[-1]
    others = len(received_refs) // chunks
    rows = own_refs[0].shape[2]
    for c in range(chunks):
        total = own_refs[c][...]
        for received_ref in received_refs[c * others : (c + 1) * others]:
            total = total + received_ref[...].astype(FULL)
        out_ref[:, :, c * rows : (c + 1) * rows] = total.astype(HALF)


def combine(owns, received):
    chunks = len(owns)
    slots, parts, rows, orbitals = owns[0].shape
    return pl.pallas_call(
        functools.partial(combine_kernel, chunks),
        out_shape=jax.ShapeDtypeStruct((slots, parts, rows * chunks, orbitals), HALF),
        in_specs=[pl.BlockSpec(memory_space=VMEM)] * (chunks + len(received)),
        out_specs=pl.BlockSpec(memory_space=VMEM),
        compiler_params=pltpu.CompilerParams(vmem_limit_bytes=SMALL),
        name="combine",
    )(*owns, *received)


def walker_kernel(count, orbitals, electrons, rank_ref, field_ref, *refs):
    start_refs = refs[:count]
    out_ref, start_wide_ref = refs[count:]
    blocks, _, rows, _ = field_ref.shape
    wide = start_wide_ref.shape[1] // 2
    start_wide_ref[...] = jnp.zeros_like(start_wide_ref)
    block = 0
    for start_ref in start_refs:
        for d in range(start_ref.shape[0]):
            at = pl.multiple_of((rank_ref[0] ^ block) * rows, 2 * TILE)
            for c in range(2):
                start_wide_ref[pl.ds(at, rows), pl.ds(c * wide, electrons)] = start_ref[d, c]
            block += 1
    current = start_wide_ref[...]
    summed = current.astype(FULL)
    for order in range(1, TERMS + 1):
        product = dot(field_ref[...].reshape(2 * orbitals, orbitals), current)
        product = product.reshape(blocks, 2, rows, 2 * wide)
        top = product[:, 0].reshape(orbitals, 2 * wide)
        low = product[:, 1].reshape(orbitals, 2 * wide)
        following = jnp.concatenate(
            [top[:, :wide] - low[:, wide:], top[:, wide:] + low[:, :wide]], 1
        )
        following = following * (1.0 / order)
        summed = summed + following
        current = following.astype(HALF)

    rounded = summed.astype(HALF)
    gram = dot(rounded, rounded, ((0,), (0,)))
    gram_real = (gram[:wide, :wide] + gram[wide:, wide:]) * (1.0 / orbitals)
    gram_imag = (gram[:wide, wide:] - gram[wide:, :wide]) * (1.0 / orbitals)
    row = lax.broadcasted_iota(jnp.int32, (wide, wide), 0)
    column = lax.broadcasted_iota(jnp.int32, (wide, wide), 1)
    identity = jnp.where((row == column) & (row < electrons), 1.0, 0.0)
    scale = jnp.sum(gram_real * identity, axis=0, keepdims=True)
    scale = jnp.sum(scale, axis=1, keepdims=True) * (1.0 / electrons)

    def times(left, right):
        product = fine_dot(jnp.concatenate(left, 0), jnp.concatenate(right, 1))
        real = product[:wide, :wide] - product[wide:, wide:]
        return real, product[:wide, wide:] + product[wide:, :wide]

    iterate = (gram_real / scale, gram_imag / scale)
    root = None
    for sweep in range(NS_STEPS):
        real, imag = iterate if root is None else times(root, iterate)
        step = (1.5 * identity - 0.5 * real, -0.5 * imag)
        if sweep + 1 < NS_STEPS:
            iterate = times(iterate, step)
        root = step if root is None else times(step, root)
    inverse = lax.rsqrt(scale)
    root = jnp.concatenate([root[0] * inverse, root[1] * inverse], 1)
    product = dot(jnp.concatenate([rounded[:, :wide], rounded[:, wide:]], 0), root.astype(HALF))
    top, low = product[:orbitals], product[orbitals:]
    real = (top[:, :wide] - low[:, wide:]).astype(HALF)
    imag = (top[:, wide:] + low[:, :wide]).astype(HALF)
    for r in range(blocks):
        out_ref[r, 0] = real[r * rows : (r + 1) * rows, :electrons]
        out_ref[r, 1] = imag[r * rows : (r + 1) * rows, :electrons]


def walker_step(rank, field, starts):
    blocks, parts, rows, orbitals = field.shape
    electrons = starts[0].shape[3]
    wide = -(-electrons // LANES) * LANES
    return local_kernel(
        functools.partial(walker_kernel, len(starts), orbitals, electrons),
        [SCALARS] + [ARRAY] * (1 + len(starts)),
        jax.ShapeDtypeStruct((blocks, parts, rows, electrons), HALF),
        [VMEM((orbitals, 2 * wide), HALF)],
        SMALL,
    )(rank, field, *starts)


def shift(value, axis, step):
    size = lax.axis_size(axis)
    return lax.ppermute(value, axis, [(i, (i + step) % size) for i in range(size)])


def scatter_sum(value, axis, dim):
    size = lax.axis_size(axis)
    here = lax.axis_index(axis)
    width = value.shape[dim] // size
    total = lax.dynamic_slice_in_dim(value, here * width, width, dim)
    for s in range(1, size):
        block = lax.dynamic_slice_in_dim(value, ((here + s) % size) * width, width, dim)
        total = total + shift(block, axis, s)
    return total


def gather_ordered(value, axis, dim):
    size = lax.axis_size(axis)
    here = lax.axis_index(axis)
    width = value.shape[dim]
    shape = list(value.shape)
    shape[dim] = width * size
    whole = jnp.zeros(shape, value.dtype)
    for s in range(size):
        block = value if s == 0 else shift(value, axis, s)
        whole = lax.dynamic_update_slice_in_dim(whole, block, ((here - s) % size) * width, dim)
    return whole


def exchange_sum(value, axis):
    size = lax.axis_size(axis)
    if size & (size - 1):
        return sum([shift(value, axis, s) for s in range(1, size)], value)
    step = 1
    while step < size:
        value = value + lax.ppermute(value, axis, [(i, i ^ step) for i in range(size)])
        step *= 2
    return value


def whole_step(walkers, correlation_inverse, half_vectors, field_vectors, samples, source):
    local = walkers.shape[0]
    vectors, row_block, orbitals = field_vectors.shape
    electrons = correlation_inverse.shape[2]
    planes = lax.axis_size("walk")
    population = local * planes
    count = population * 2
    devices_rows = lax.axis_size(ROWS)
    sharers = devices_rows // local
    first = lax.axis_index("walk") * local
    core = lax.axis_index("orb")
    chol = lax.axis_size("chol")
    half = vectors // 2
    fast = (
        row_block % (2 * TILE) == 0
        and vectors % (2 * LANES) == 0
        and lax.axis_size("orb") == 2
        and planes > 1
        and sharers == 1
        and chol & (chol - 1) == 0
    )

    def to_owners(value):
        value = jnp.broadcast_to(value[:, None], (local, sharers) + value.shape[1:])
        value = value.reshape((devices_rows,) + value.shape[2:])
        return lax.all_to_all(value, ROWS, split_axis=0, concat_axis=0, tiled=True)

    def others(value):
        return jnp.concatenate([shift(value, "walk", -s) for s in range(1, planes)], 0)

    def from_planes(sent):
        blocks = [sent[s * local : (s + 1) * local] for s in range(planes - 1)]
        return [shift(block, "walk", s + 1) for s, block in enumerate(blocks)]

    other_source = others(source)
    place = jnp.stack([first, core, lax.axis_index("chol")]).astype(jnp.int32)
    rank = lax.axis_index(ROWS).astype(jnp.int32).reshape(1)
    grid_shape = (local, 2, row_block, electrons)
    half_grid = jax.ShapeDtypeStruct(grid_shape, HALF)
    if fast and 4 * electrons == 3 * LANES and row_block % TILE == 0:
        theta, start = local_kernel(
            lines_kernel,
            [pl.BlockSpec(memory_space=pltpu.HBM)] * 2,
            [half_grid] * 2,
            [
                VMEM(walkers.shape, FULL),
                VMEM(correlation_inverse.shape, FULL),
                VMEM((2, local * row_block, LANES), FULL),
                pltpu.SemaphoreType.DMA((2,)),
            ],
            LINES_LIMIT,
        )(walkers, correlation_inverse)
    else:
        grid = walkers.reshape(grid_shape)
        start = grid.astype(HALF)
        theta = local_kernel(theta_kernel, [ARRAY] * 2, half_grid, limit=SMALL)(
            grid, correlation_inverse
        )
    theta = theta.reshape(local * 2, row_block * electrons)
    other_theta = others(theta)
    other_start = others(start)

    if fast:
        tiled_vectors = field_vectors.reshape(vectors, row_block // TILE, TILE, orbitals)
        unit_shape = jax.ShapeDtypeStruct((half, 2, TILE, orbitals), HALF)
        half_vectors, unit = read_early(half_vectors, tiled_vectors, unit_shape)
        block = (2, row_block, electrons)
        slots = jax.ShapeDtypeStruct((local // 2, 1) + block, HALF)
        keep, sent = local_kernel(
            pick_kernel,
            [SCALARS] * 2 + [ARRAY] * 2,
            [slots] * 2,
            [VMEM((population,) + block, HALF)],
        )(place, source, start, other_start)
        passed = shift(sent, "orb", 1)
        part_shape = jax.ShapeDtypeStruct((count, half), FULL)
        bias, sent = local_kernel(
            bias_kernel, [SCALARS] + [ARRAY] * 3, [part_shape, part_shape], limit=SMALL
        )(place, theta, other_theta, half_vectors)
        hbm = pl.BlockSpec(memory_space=pltpu.HBM)
        received = shift(sent, "orb", 1)
        rounded_shape = jax.ShapeDtypeStruct(part_shape.shape, HALF)
        add = local_kernel(add_kernel, [ARRAY] * 2, [part_shape, rounded_shape])
        step = 1
        while step < chol:
            pairs = [(i, i ^ step) for i in range(chol)]
            bias, rounded = add(bias, received)
            received = lax.ppermute(rounded, "chol", pairs)
            slots = jax.ShapeDtypeStruct((keep.shape[0] // 2, keep.shape[1] * 2) + block, HALF)
            keep, sent = local_kernel(
                functools.partial(split_kernel, step), [SCALARS] + [ARRAY] * 2, [slots] * 2
            )(place, keep, passed)
            passed = lax.ppermute(sent, "chol", pairs)
            step *= 2
        other_unit = local_kernel(
            late_kernel,
            [hbm, hbm],
            unit_shape,
            [pltpu.SemaphoreType.DMA((half // LANES,))],
            3 * SMALL,
        )(bias, tiled_vectors)
        units = [unit, other_unit]
        coefficient = local_kernel(
            coefficient_kernel,
            [SCALARS] * 3 + [ARRAY] * 3,
            jax.ShapeDtypeStruct((count, half), HALF),
            [VMEM((count, half), FULL)] * 2,
        )(place, source, other_source, bias, received, samples)
        other_half = shift(coefficient, "orb", 1)
        rows = 2 * TILE
        parts = row_block // rows
        owns, received = [], []
        left = [place, coefficient, other_half]
        for part in range(parts):
            have = 2 * part + len(units)
            wanted = range(have, max(have, min(2 * parts, 2 * part + 5)))
            own, sent, left, further = field_rows(
                left, units[:2], tiled_vectors, part, wanted, count, local * 2
            )
            units = units[2:] + further
            owns.append(own.reshape(local, 2, rows, orbitals))
            sent = sent.reshape(population - local, 2, rows, orbitals)
            received += from_planes(sent)
        field = to_owners(combine(owns, received))
        starts = [keep[0], passed[0]]
    else:
        wanted = jnp.concatenate([source, other_source], 0)
        relative = jnp.where(wanted < first, wanted - first + population, wanted - first)
        all_start = jnp.concatenate([start, other_start], 0)
        picked = all_start.at[relative[:local]].get(mode="promise_in_bounds")
        columns = to_owners(picked)
        angles = jnp.concatenate([theta, other_theta], 0)
        bias = jnp.einsum("ij,gj->ig", angles, half_vectors, preferred_element_type=FULL)
        bias = bias.reshape(population, 2, vectors)
        bias = exchange_sum(scatter_sum(bias, "orb", 2), "chol")
        bias = bias.at[relative].get(mode="promise_in_bounds")
        width = bias.shape[2]
        drawn = lax.dynamic_slice_in_dim(samples, core * width, width, 1)
        drawn = drawn.at[wanted].get(mode="promise_in_bounds")
        coefficient = jnp.stack([bias[:, 1], drawn - bias[:, 0]], 1).astype(HALF)
        coefficient = gather_ordered(coefficient, "orb", 2)
        field = jnp.einsum(
            "wcg,gab->wcab", coefficient, field_vectors, preferred_element_type=FULL
        )
        total = field[:local]
        for block in from_planes(field[local:].astype(HALF)):
            total = total + block
        field = to_owners(total.astype(HALF)).transpose(1, 0, 2, 3)
        field = field.reshape(1, 2, orbitals, orbitals)
        starts = [columns.transpose(1, 0, 2, 3).reshape(1, 2, orbitals, electrons)]
        rank = jnp.zeros((1,), jnp.int32)

    normalized = walker_step(rank, field, starts)
    if not fast:
        normalized = normalized.reshape(2, devices_rows, row_block, electrons)
        normalized = normalized.transpose(1, 0, 2, 3)
    if sharers > 1:
        share = lax.axis_index(ROWS) % sharers
        width = electrons // sharers
        normalized = lax.dynamic_slice_in_dim(normalized, share * width, width, 3)
    returned = lax.all_to_all(normalized, ROWS, split_axis=0, concat_axis=0, tiled=True)
    if fast and 4 * electrons == 3 * LANES and row_block % TILE == 0:
        return local_kernel(
            flatten_kernel,
            [ARRAY],
            jax.ShapeDtypeStruct(walkers.shape, FULL),
            [VMEM((2, local * row_block, LANES), FULL)],
        )(returned)
    if sharers > 1:
        returned = returned.reshape(local, sharers, 2, row_block, width)
        returned = returned.transpose(0, 2, 3, 1, 4)
    return returned.reshape(local, 2, row_block * electrons).astype(FULL)


def solution(mesh):
    placed = (
        P(("groups", "walk"), None, ("chol", "orb")),
        P(("groups", "walk"), None, None, None),
        P(("groups", "walk"), ("chol", "orb")),
        P(("groups", "walk"), ("chol", "orb"), None),
        P("groups", "walk"),
        P(("groups", "walk")),
    )
    return jax.shard_map(
        whole_step,
        mesh=mesh,
        in_specs=placed,
        out_specs=P(("groups", "walk"), None, ("chol", "orb")),
        check_vma=False,
    )
```

```python
import functools

import jax
import jax.numpy as jnp
from jax import lax
from jax.experimental import pallas as pl
from jax.experimental.pallas import tpu as pltpu
from jax.sharding import PartitionSpec as P


TERMS = 4
NS_STEPS = 2
ROWS = ("chol", "orb")
HALF = jnp.bfloat16
FULL = jnp.float32
LANES = 128
TILE = 8
SMALL = 8 << 20
TINY = 2 << 20
LINES_LIMIT = 56250000
READ_LIMIT = 36 << 20
VMEM = pltpu.VMEM


def split_half(value):
    high = value.astype(HALF)
    return high, (value - high.astype(FULL)).astype(HALF)


def dot(left, right, contract=((1,), (0,))):
    return lax.dot_general(left, right, (contract, ((), ())), preferred_element_type=FULL)


def fine_dot(left, right):
    left_high, left_low = split_half(left)
    right_high, right_low = split_half(right)
    height = left.shape[0]
    both = dot(jnp.concatenate([left_high, left_low], 0), right_high)
    return both[:height] + both[height:] + dot(left_high, right_low)


def theta_kernel(grid_ref, inverse_ref, theta_ref):
    rows = grid_ref.shape[2]
    for w in range(grid_ref.shape[0]):
        stacked = jnp.concatenate([grid_ref[w, 0], grid_ref[w, 1]], 0)
        by_real = fine_dot(stacked, inverse_ref[w, 0])
        by_imag = fine_dot(stacked, inverse_ref[w, 1])
        theta_ref[w, 0] = (by_real[:rows] - by_imag[rows:]).astype(HALF)
        theta_ref[w, 1] = (by_imag[:rows] + by_real[rows:]).astype(HALF)


def narrow_rows(first, second, third):
    lane = lax.broadcasted_iota(jnp.int32, first.shape, 1)
    part = LANES // 4
    return (
        first,
        jnp.where(lane < part, pltpu.roll(first, part, 1), pltpu.roll(second, part, 1)),
        jnp.where(lane < 2 * part, pltpu.roll(second, 2 * part, 1), pltpu.roll(third, 2 * part, 1)),
        pltpu.roll(third, 3 * part, 1),
    )


def wide_lines(first, second, third, fourth):
    lane = lax.broadcasted_iota(jnp.int32, first.shape, 1)
    part = LANES // 4
    second, third = pltpu.roll(second, 3 * part, 1), pltpu.roll(third, 2 * part, 1)
    return (
        jnp.where(lane < 3 * part, first, second),
        jnp.where(lane < 2 * part, second, third),
        jnp.where(lane < part, third, pltpu.roll(fourth, part, 1)),
    )


def flatten_kernel(grid_ref, out_ref, rows_ref):
    count, _, rows, electrons = grid_ref.shape
    for w in range(count):
        for c in range(2):
            rows_ref[c, w * rows : (w + 1) * rows, :electrons] = grid_ref[w, c].astype(FULL)
    for c in range(2):
        for k in range(rows // 4):
            narrow = [rows_ref[c, pl.ds(4 * k + s, count, stride=rows)] for s in range(4)]
            for t, line in enumerate(wide_lines(*narrow)):
                out_ref[:, c, (3 * k + t) * LANES : (3 * k + t + 1) * LANES] = line


def lines_kernel(
    walkers_hbm, inverse_hbm, theta_ref, start_ref, walkers_ref, inverse_ref, rows_ref, semaphores
):
    first = pltpu.make_async_copy(walkers_hbm, walkers_ref, semaphores.at[0])
    first.start()
    copy = pltpu.make_async_copy(inverse_hbm, inverse_ref, semaphores.at[1])
    copy.start()
    first.wait()
    count, _, rows, electrons = theta_ref.shape
    for c in range(2):
        for k in range(rows // 4):
            lines = [
                walkers_ref[:, c, (3 * k + t) * LANES : (3 * k + t + 1) * LANES] for t in range(3)
            ]
            for s, narrow in enumerate(narrow_rows(*lines)):
                rows_ref[c, pl.ds(4 * k + s, count, stride=rows)] = narrow
    for w in range(count):
        for c in range(2):
            start_ref[w, c] = rows_ref[c, w * rows : (w + 1) * rows, :electrons].astype(HALF)
    copy.wait()
    for w in range(count):
        stacked = jnp.concatenate(
            [rows_ref[c, w * rows : (w + 1) * rows, :electrons] for c in range(2)], 0
        )
        by_real = fine_dot(stacked, inverse_ref[w, 0])
        by_imag = fine_dot(stacked, inverse_ref[w, 1])
        theta_ref[w, 0] = (by_real[:rows] - by_imag[rows:]).astype(HALF)
        theta_ref[w, 1] = (by_imag[:rows] + by_real[rows:]).astype(HALF)


def fill_spread(place_ref, own_ref, received_ref, spread_ref, values_ref):
    count, half = own_ref.shape
    height = count * TILE
    wide = LANES * TILE
    row = lax.broadcasted_iota(jnp.int32, (height, count), 0)
    column = lax.broadcasted_iota(jnp.int32, (height, count), 1)
    repeats = (row // TILE == column).astype(FULL).astype(HALF)
    low = place_ref[1] == 0
    own, received = own_ref[...].astype(FULL), received_ref[...].astype(FULL)
    values_ref[:, :half] = dot(repeats, jnp.where(low, own, received).astype(HALF)).astype(HALF)
    values_ref[:, half:] = dot(repeats, jnp.where(low, received, own).astype(HALF)).astype(HALF)
    row = lax.broadcasted_iota(jnp.int32, (LANES, wide), 0)
    column = lax.broadcasted_iota(jnp.int32, (LANES, wide), 1)
    copies = (column // TILE == row).astype(FULL).astype(HALF)
    a = lax.broadcasted_iota(jnp.int32, (TILE, wide), 0)
    b = lax.broadcasted_iota(jnp.int32, (TILE, wide), 1) % TILE
    keep = a == b

    @pl.loop(0, 2 * half // LANES)
    def _(block):
        values = values_ref[:, pl.ds(pl.multiple_of(block * LANES, LANES), LANES)]
        wider = dot(values, copies).reshape(count, TILE, wide)
        wider = jnp.where(keep[None], wider, 0.0).reshape(height, wide)
        spread_ref[:, pl.ds(pl.multiple_of(block * wide, wide), wide)] = wider.astype(HALF)


SCALARS = pl.BlockSpec(memory_space=pltpu.SMEM)
ARRAY = pl.BlockSpec(memory_space=VMEM)


def local_kernel(kernel, in_specs, out_shape, scratch_shapes=(), limit=TINY):
    return pl.pallas_call(
        kernel,
        in_specs=in_specs,
        out_specs=jax.tree.map(lambda _: ARRAY, out_shape),
        out_shape=out_shape,
        scratch_shapes=list(scratch_shapes),
        compiler_params=pltpu.CompilerParams(vmem_limit_bytes=limit),
    )


def wanted_walker(place_ref, source_ref, others_ref, i, population):
    local = source_ref.shape[0]
    walker = source_ref[i] if i < local else others_ref[i - local]
    relative = walker - place_ref[0]
    return walker, jnp.where(relative < 0, relative + population, relative)


def pick_kernel(place_ref, source_ref, own_ref, received_ref, keep_ref, send_ref, all_ref):
    local = own_ref.shape[0]
    population = all_ref.shape[0]
    all_ref[:local] = own_ref[...]
    all_ref[local:] = received_ref[...]
    for t in range(local // 2):
        for target_ref, core in ((keep_ref, place_ref[1]), (send_ref, 1 - place_ref[1])):
            relative = source_ref[2 * t + core] - place_ref[0]
            relative = jnp.where(relative < 0, relative + population, relative)
            target_ref[t, 0] = all_ref[relative]


def split_kernel(step, place_ref, own_ref, received_ref, keep_ref, send_ref):
    senders = own_ref.shape[1]
    bit = (place_ref[2] // step) % 2
    for t in range(own_ref.shape[0] // 2):
        for target_ref, side in ((keep_ref, bit), (send_ref, 1 - bit)):
            target_ref[t, :senders] = own_ref[2 * t + side]
            target_ref[t, senders:] = received_ref[2 * t + side]


def start_reading(pairs, semaphores):
    copies = []
    for source_ref, target_ref in pairs:
        for block in range(target_ref.shape[0] // LANES):
            group = pl.ds(block * LANES, LANES)
            semaphore = semaphores.at[len(copies)]
            copy = pltpu.make_async_copy(source_ref.at[group], target_ref.at[group], semaphore)
            copy.start()
            copies.append(copy)
    return copies


def unit_of(field_hbm, target_ref, unit):
    height, tiles = target_ref.shape[:2]
    rows = pl.ds(unit % 2 * height, height)
    return field_hbm.at[rows, pl.ds(unit // 2 * tiles, tiles)], target_ref


def bias_kernel(place_ref, own_ref, received_ref, vectors_ref, keep_ref, send_ref):
    angles = jnp.concatenate([own_ref[...], received_ref[...]], 0)
    bias = dot(vectors_ref[...], angles, ((1,), (1,))).T
    half = bias.shape[1] // 2
    first, second = bias[:, :half], bias[:, half:]
    low = place_ref[1] == 0
    keep_ref[...] = jnp.where(low, first, second)
    send_ref[...] = jnp.where(low, second, first)


def late_kernel(order_ref, field_hbm, unit_ref, semaphores):
    for copy in start_reading([unit_of(field_hbm, unit_ref, 1)], semaphores):
        copy.wait()


def add_kernel(left_ref, right_ref, out_ref, rounded_ref):
    total = left_ref[...] + right_ref[...].astype(FULL)
    out_ref[...] = total
    rounded_ref[...] = total.astype(HALF)


def coefficient_kernel(
    place_ref, source_ref, others_ref, left_ref, right_ref, samples_ref, out_ref, bias_ref, row_ref
):
    bias_ref[...] = left_ref[...] + right_ref[...].astype(FULL)
    count, half = bias_ref.shape
    lanes = pl.ds(pl.multiple_of(place_ref[1] * half, LANES), half)
    for i in range(count // 2):
        walker, relative = wanted_walker(place_ref, source_ref, others_ref, i, count // 2)
        row_ref[2 * i : 2 * i + 1] = bias_ref[pl.ds(2 * relative + 1, 1)]
        drawn = samples_ref[pl.ds(walker, 1), lanes]
        row_ref[2 * i + 1 : 2 * i + 2] = drawn - bias_ref[pl.ds(2 * relative, 1)]
    out_ref[...] = row_ref[...].astype(HALF)


def read_kernel(half_hbm, field_hbm, half_ref, unit_ref, semaphores):
    pairs = [(half_hbm, half_ref), unit_of(field_hbm, unit_ref, 0)]
    for copy in start_reading(pairs, semaphores):
        copy.wait()


def read_early(half_vectors, tiled_vectors, unit_shape):
    return pl.pallas_call(
        read_kernel,
        in_specs=[pl.BlockSpec(memory_space=pl.ANY)] * 2,
        out_specs=[ARRAY] * 2,
        out_shape=[jax.ShapeDtypeStruct(half_vectors.shape, HALF), unit_shape],
        scratch_shapes=[
            pltpu.SemaphoreType.DMA(((half_vectors.shape[0] + unit_shape.shape[0]) // LANES,))
        ],
        compiler_params=pltpu.CompilerParams(vmem_limit_bytes=READ_LIMIT),
        name="read",
    )(half_vectors, tiled_vectors)


def field_kernel(part, wanted, mine, *refs):
    refs = list(refs)
    left_refs = [refs.pop(0) for _ in range(3 if part == 0 else 1)]
    unit_refs, field_hbm, own_ref, sent_ref = refs[:2], refs[2], refs[3], refs[4]
    refs = refs[5:]
    spread_ref = refs.pop(0) if part == 0 else left_refs[0]
    values_ref = refs.pop() if part == 0 else None
    copies = []
    if wanted:
        semaphores = refs.pop()
        pairs = [unit_of(field_hbm, ref, unit) for ref, unit in zip(refs, wanted)]
        copies = start_reading(pairs, semaphores)
    if part == 0:
        fill_spread(*left_refs, spread_ref, values_ref)
    height, tiles, _, orbitals = unit_refs[0].shape
    count = spread_ref.shape[0] // TILE
    depth = height * TILE
    total = None
    for block, unit_ref in enumerate(unit_refs):
        right = jnp.concatenate(
            [unit_ref[:, t].reshape(depth, orbitals) for t in range(tiles)], 1
        )
        product = dot(spread_ref[:, block * depth : (block + 1) * depth], right)
        total = product if total is None else total + product
    for t in range(tiles):
        slab = total[:, t * orbitals : (t + 1) * orbitals].reshape(count, TILE, orbitals)
        own_ref[:, t * TILE : (t + 1) * TILE] = slab[:mine].astype(HALF)
        sent_ref[:, t * TILE : (t + 1) * TILE] = slab[mine:].astype(HALF)
    for copy in copies:
        copy.wait()


def field_rows(left, units, tiled_vectors, part, wanted, count, mine):
    height, tiles, _, orbitals = units[0].shape
    vectors = 2 * height
    rows = tiles * TILE
    out_shape = [
        jax.ShapeDtypeStruct((mine, rows, orbitals), HALF),
        jax.ShapeDtypeStruct((count - mine, rows, orbitals), HALF),
    ]
    if part == 0:
        out_shape.append(jax.ShapeDtypeStruct((count * TILE, vectors * TILE), HALF))
    out_shape += [jax.ShapeDtypeStruct(units[0].shape, HALF) for _ in wanted]
    scratch = []
    if wanted:
        scratch.append(pltpu.SemaphoreType.DMA((len(wanted) * height // LANES,)))
    if part == 0:
        scratch.append(VMEM((count * TILE, vectors), HALF))
    left_specs = [SCALARS, ARRAY, ARRAY] if part == 0 else [ARRAY]
    own, sent, *rest = pl.pallas_call(
        functools.partial(field_kernel, part, wanted, mine),
        in_specs=left_specs + [ARRAY] * 2 + [pl.BlockSpec(memory_space=pltpu.HBM)],
        out_specs=[ARRAY] * len(out_shape),
        out_shape=out_shape,
        scratch_shapes=scratch,
        compiler_params=pltpu.CompilerParams(vmem_limit_bytes=SMALL),
        cost_estimate=pl.CostEstimate(
            flops=2 * count * TILE * vectors * rows * orbitals,
            bytes_accessed=2 * vectors * rows * orbitals,
            transcendentals=0,
        ),
        name="field",
    )(*left, *units, tiled_vectors)
    left = [rest.pop(0)] if part == 0 else left
    return own, sent, left, rest


def combine_kernel(chunks, *refs):
    own_refs, received_refs, out_ref = refs[:chunks], refs[chunks:-1], refs[-1]
    others = len(received_refs) // chunks
    rows = own_refs[0].shape[2]
    for c in range(chunks):
        total = own_refs[c][...].astype(FULL)
        for received_ref in received_refs[c * others : (c + 1) * others]:
            total = total + received_ref[...].astype(FULL)
        out_ref[:, :, c * rows : (c + 1) * rows] = total.astype(HALF)


def combine(owns, received):
    chunks = len(owns)
    slots, parts, rows, orbitals = owns[0].shape
    return pl.pallas_call(
        functools.partial(combine_kernel, chunks),
        out_shape=jax.ShapeDtypeStruct((slots, parts, rows * chunks, orbitals), HALF),
        in_specs=[pl.BlockSpec(memory_space=VMEM)] * (chunks + len(received)),
        out_specs=pl.BlockSpec(memory_space=VMEM),
        compiler_params=pltpu.CompilerParams(vmem_limit_bytes=SMALL),
        name="combine",
    )(*owns, *received)


def walker_kernel(count, orbitals, electrons, rank_ref, field_ref, *refs):
    start_refs = refs[:count]
    out_ref, start_wide_ref = refs[count:]
    blocks, _, rows, _ = field_ref.shape
    wide = start_wide_ref.shape[1] // 2
    start_wide_ref[...] = jnp.zeros_like(start_wide_ref)
    block = 0
    for start_ref in start_refs:
        for d in range(start_ref.shape[0]):
            at = pl.multiple_of((rank_ref[0] ^ block) * rows, 2 * TILE)
            for c in range(2):
                start_wide_ref[pl.ds(at, rows), pl.ds(c * wide, electrons)] = start_ref[d, c]
            block += 1
    current = start_wide_ref[...]
    summed = current.astype(FULL)
    for order in range(1, TERMS + 1):
        product = dot(field_ref[...].reshape(2 * orbitals, orbitals), current)
        product = product.reshape(blocks, 2, rows, 2 * wide)
        top = product[:, 0].reshape(orbitals, 2 * wide)
        low = product[:, 1].reshape(orbitals, 2 * wide)
        following = jnp.concatenate(
            [top[:, :wide] - low[:, wide:], top[:, wide:] + low[:, :wide]], 1
        )
        following = following * (1.0 / order)
        summed = summed + following
        current = following.astype(HALF)

    rounded = summed.astype(HALF)
    gram = dot(rounded, rounded, ((0,), (0,)))
    gram_real = (gram[:wide, :wide] + gram[wide:, wide:]) * (1.0 / orbitals)
    gram_imag = (gram[:wide, wide:] - gram[wide:, :wide]) * (1.0 / orbitals)
    row = lax.broadcasted_iota(jnp.int32, (wide, wide), 0)
    column = lax.broadcasted_iota(jnp.int32, (wide, wide), 1)
    identity = jnp.where((row == column) & (row < electrons), 1.0, 0.0)
    scale = jnp.sum(gram_real * identity, axis=0, keepdims=True)
    scale = jnp.sum(scale, axis=1, keepdims=True) * (1.0 / electrons)

    def times(left, right):
        product = fine_dot(jnp.concatenate(left, 0), jnp.concatenate(right, 1))
        real = product[:wide, :wide] - product[wide:, wide:]
        return real, product[:wide, wide:] + product[wide:, :wide]

    iterate = (gram_real / scale, gram_imag / scale)
    root = None
    for sweep in range(NS_STEPS):
        real, imag = iterate if root is None else times(root, iterate)
        step = (1.5 * identity - 0.5 * real, -0.5 * imag)
        if sweep + 1 < NS_STEPS:
            iterate = times(iterate, step)
        root = step if root is None else times(step, root)
    inverse = lax.rsqrt(scale)
    root = jnp.concatenate([root[0] * inverse, root[1] * inverse], 1)
    product = dot(jnp.concatenate([rounded[:, :wide], rounded[:, wide:]], 0), root.astype(HALF))
    top, low = product[:orbitals], product[orbitals:]
    real = (top[:, :wide] - low[:, wide:]).astype(HALF)
    imag = (top[:, wide:] + low[:, :wide]).astype(HALF)
    for r in range(blocks):
        out_ref[r, 0] = real[r * rows : (r + 1) * rows, :electrons]
        out_ref[r, 1] = imag[r * rows : (r + 1) * rows, :electrons]


def walker_step(rank, field, starts):
    blocks, parts, rows, orbitals = field.shape
    electrons = starts[0].shape[3]
    wide = -(-electrons // LANES) * LANES
    return local_kernel(
        functools.partial(walker_kernel, len(starts), orbitals, electrons),
        [SCALARS] + [ARRAY] * (1 + len(starts)),
        jax.ShapeDtypeStruct((blocks, parts, rows, electrons), HALF),
        [VMEM((orbitals, 2 * wide), HALF)],
        SMALL,
    )(rank, field, *starts)


def shift(value, axis, step):
    size = lax.axis_size(axis)
    return lax.ppermute(value, axis, [(i, (i + step) % size) for i in range(size)])


def scatter_sum(value, axis, dim):
    size = lax.axis_size(axis)
    here = lax.axis_index(axis)
    width = value.shape[dim] // size
    total = lax.dynamic_slice_in_dim(value, here * width, width, dim)
    for s in range(1, size):
        block = lax.dynamic_slice_in_dim(value, ((here + s) % size) * width, width, dim)
        total = total + shift(block, axis, s)
    return total


def gather_ordered(value, axis, dim):
    size = lax.axis_size(axis)
    here = lax.axis_index(axis)
    width = value.shape[dim]
    shape = list(value.shape)
    shape[dim] = width * size
    whole = jnp.zeros(shape, value.dtype)
    for s in range(size):
        block = value if s == 0 else shift(value, axis, s)
        whole = lax.dynamic_update_slice_in_dim(whole, block, ((here - s) % size) * width, dim)
    return whole


def exchange_sum(value, axis):
    size = lax.axis_size(axis)
    if size & (size - 1):
        return sum([shift(value, axis, s) for s in range(1, size)], value)
    step = 1
    while step < size:
        value = value + lax.ppermute(value, axis, [(i, i ^ step) for i in range(size)])
        step *= 2
    return value


def whole_step(walkers, correlation_inverse, half_vectors, field_vectors, samples, source):
    local = walkers.shape[0]
    vectors, row_block, orbitals = field_vectors.shape
    electrons = correlation_inverse.shape[2]
    planes = lax.axis_size("walk")
    population = local * planes
    count = population * 2
    devices_rows = lax.axis_size(ROWS)
    sharers = devices_rows // local
    first = lax.axis_index("walk") * local
    core = lax.axis_index("orb")
    chol = lax.axis_size("chol")
    half = vectors // 2
    fast = (
        row_block % (2 * TILE) == 0
        and vectors % (2 * LANES) == 0
        and lax.axis_size("orb") == 2
        and planes > 1
        and sharers == 1
        and chol & (chol - 1) == 0
    )

    def to_owners(value):
        value = jnp.broadcast_to(value[:, None], (local, sharers) + value.shape[1:])
        value = value.reshape((devices_rows,) + value.shape[2:])
        return lax.all_to_all(value, ROWS, split_axis=0, concat_axis=0, tiled=True)

    def others(value):
        return jnp.concatenate([shift(value, "walk", -s) for s in range(1, planes)], 0)

    def from_planes(sent):
        blocks = [sent[s * local : (s + 1) * local] for s in range(planes - 1)]
        return [shift(block, "walk", s + 1) for s, block in enumerate(blocks)]

    other_source = others(source)
    place = jnp.stack([first, core, lax.axis_index("chol")]).astype(jnp.int32)
    rank = lax.axis_index(ROWS).astype(jnp.int32).reshape(1)
    grid_shape = (local, 2, row_block, electrons)
    half_grid = jax.ShapeDtypeStruct(grid_shape, HALF)
    if fast and 4 * electrons == 3 * LANES and row_block % TILE == 0:
        theta, start = local_kernel(
            lines_kernel,
            [pl.BlockSpec(memory_space=pltpu.HBM)] * 2,
            [half_grid] * 2,
            [
                VMEM(walkers.shape, FULL),
                VMEM(correlation_inverse.shape, FULL),
                VMEM((2, local * row_block, LANES), FULL),
                pltpu.SemaphoreType.DMA((2,)),
            ],
            LINES_LIMIT,
        )(walkers, correlation_inverse)
    else:
        grid = walkers.reshape(grid_shape)
        start = grid.astype(HALF)
        theta = local_kernel(theta_kernel, [ARRAY] * 2, half_grid, limit=SMALL)(
            grid, correlation_inverse
        )
    theta = theta.reshape(local * 2, row_block * electrons)
    other_theta = others(theta)
    other_start = others(start)

    if fast:
        tiled_vectors = field_vectors.reshape(vectors, row_block // TILE, TILE, orbitals)
        unit_shape = jax.ShapeDtypeStruct((half, 2, TILE, orbitals), HALF)
        half_vectors, unit = read_early(half_vectors, tiled_vectors, unit_shape)
        block = (2, row_block, electrons)
        slots = jax.ShapeDtypeStruct((local // 2, 1) + block, HALF)
        keep, sent = local_kernel(
            pick_kernel,
            [SCALARS] * 2 + [ARRAY] * 2,
            [slots] * 2,
            [VMEM((population,) + block, HALF)],
        )(place, source, start, other_start)
        passed = shift(sent, "orb", 1)
        part_shape = jax.ShapeDtypeStruct((count, half), FULL)
        bias, sent = local_kernel(
            bias_kernel, [SCALARS] + [ARRAY] * 3, [part_shape, part_shape], limit=SMALL
        )(place, theta, other_theta, half_vectors)
        hbm = pl.BlockSpec(memory_space=pltpu.HBM)
        received = shift(sent, "orb", 1)
        rounded_shape = jax.ShapeDtypeStruct(part_shape.shape, HALF)
        add = local_kernel(add_kernel, [ARRAY] * 2, [part_shape, rounded_shape])
        step = 1
        while step < chol:
            pairs = [(i, i ^ step) for i in range(chol)]
            bias, rounded = add(bias, received)
            received = lax.ppermute(rounded, "chol", pairs)
            slots = jax.ShapeDtypeStruct((keep.shape[0] // 2, keep.shape[1] * 2) + block, HALF)
            keep, sent = local_kernel(
                functools.partial(split_kernel, step), [SCALARS] + [ARRAY] * 2, [slots] * 2
            )(place, keep, passed)
            passed = lax.ppermute(sent, "chol", pairs)
            step *= 2
        other_unit = local_kernel(
            late_kernel,
            [hbm, hbm],
            unit_shape,
            [pltpu.SemaphoreType.DMA((half // LANES,))],
            3 * SMALL,
        )(bias, tiled_vectors)
        units = [unit, other_unit]
        coefficient = local_kernel(
            coefficient_kernel,
            [SCALARS] * 3 + [ARRAY] * 3,
            jax.ShapeDtypeStruct((count, half), HALF),
            [VMEM((count, half), FULL)] * 2,
        )(place, source, other_source, bias, received, samples)
        other_half = shift(coefficient, "orb", 1)
        rows = 2 * TILE
        parts = row_block // rows
        owns, received = [], []
        left = [place, coefficient, other_half]
        for part in range(parts):
            have = 2 * part + len(units)
            wanted = range(have, max(have, min(2 * parts, 2 * part + 5)))
            own, sent, left, further = field_rows(
                left, units[:2], tiled_vectors, part, wanted, count, local * 2
            )
            units = units[2:] + further
            owns.append(own.reshape(local, 2, rows, orbitals))
            sent = sent.reshape(population - local, 2, rows, orbitals)
            received += from_planes(sent)
        field = to_owners(combine(owns, received))
        starts = [keep[0], passed[0]]
    else:
        wanted = jnp.concatenate([source, other_source], 0)
        relative = jnp.where(wanted < first, wanted - first + population, wanted - first)
        all_start = jnp.concatenate([start, other_start], 0)
        picked = all_start.at[relative[:local]].get(mode="promise_in_bounds")
        columns = to_owners(picked)
        angles = jnp.concatenate([theta, other_theta], 0)
        bias = jnp.einsum("ij,gj->ig", angles, half_vectors, preferred_element_type=FULL)
        bias = bias.reshape(population, 2, vectors)
        bias = exchange_sum(scatter_sum(bias, "orb", 2), "chol")
        bias = bias.at[relative].get(mode="promise_in_bounds")
        width = bias.shape[2]
        drawn = lax.dynamic_slice_in_dim(samples, core * width, width, 1)
        drawn = drawn.at[wanted].get(mode="promise_in_bounds")
        coefficient = jnp.stack([bias[:, 1], drawn - bias[:, 0]], 1).astype(HALF)
        coefficient = gather_ordered(coefficient, "orb", 2)
        field = jnp.einsum(
            "wcg,gab->wcab", coefficient, field_vectors, preferred_element_type=FULL
        )
        total = field[:local]
        for block in from_planes(field[local:].astype(HALF)):
            total = total + block
        field = to_owners(total.astype(HALF)).transpose(1, 0, 2, 3)
        field = field.reshape(1, 2, orbitals, orbitals)
        starts = [columns.transpose(1, 0, 2, 3).reshape(1, 2, orbitals, electrons)]
        rank = jnp.zeros((1,), jnp.int32)

    normalized = walker_step(rank, field, starts)
    if not fast:
        normalized = normalized.reshape(2, devices_rows, row_block, electrons)
        normalized = normalized.transpose(1, 0, 2, 3)
    if sharers > 1:
        share = lax.axis_index(ROWS) % sharers
        width = electrons // sharers
        normalized = lax.dynamic_slice_in_dim(normalized, share * width, width, 3)
    returned = lax.all_to_all(normalized, ROWS, split_axis=0, concat_axis=0, tiled=True)
    if fast and 4 * electrons == 3 * LANES and row_block % TILE == 0:
        return local_kernel(
            flatten_kernel,
            [ARRAY],
            jax.ShapeDtypeStruct(walkers.shape, FULL),
            [VMEM((2, local * row_block, LANES), FULL)],
        )(returned)
    if sharers > 1:
        returned = returned.reshape(local, sharers, 2, row_block, width)
        returned = returned.transpose(0, 2, 3, 1, 4)
    return returned.reshape(local, 2, row_block * electrons).astype(FULL)


def solution(mesh):
    placed = (
        P(("groups", "walk"), None, ("chol", "orb")),
        P(("groups", "walk"), None, None, None),
        P(("groups", "walk"), ("chol", "orb")),
        P(("groups", "walk"), ("chol", "orb"), None),
        P("groups", "walk"),
        P(("groups", "walk")),
    )
    return jax.shard_map(
        whole_step,
        mesh=mesh,
        in_specs=placed,
        out_specs=P(("groups", "walk"), None, ("chol", "orb")),
        check_vma=False,
    )
```

```python
import functools

import jax
import jax.numpy as jnp
from jax import lax
from jax.experimental import pallas as pl
from jax.experimental.pallas import tpu as pltpu
from jax.sharding import PartitionSpec as P


TERMS = 4
NS_STEPS = 2
ROWS = ("chol", "orb")
HALF = jnp.bfloat16
FULL = jnp.float32
LANES = 128
TILE = 8
SMALL = 8 << 20
TINY = 2 << 20
LINES_LIMIT = 56250000
READ_LIMIT = 36 << 20
VMEM = pltpu.VMEM


def split_half(value):
    high = value.astype(HALF)
    return high, (value - high.astype(FULL)).astype(HALF)


def dot(left, right, contract=((1,), (0,))):
    return lax.dot_general(left, right, (contract, ((), ())), preferred_element_type=FULL)


def fine_dot(left, right):
    left_high, left_low = split_half(left)
    right_high, right_low = split_half(right)
    height = left.shape[0]
    both = dot(jnp.concatenate([left_high, left_low], 0), right_high)
    return both[:height] + both[height:] + dot(left_high, right_low)


def theta_kernel(grid_ref, inverse_ref, theta_ref):
    rows = grid_ref.shape[2]
    for w in range(grid_ref.shape[0]):
        stacked = jnp.concatenate([grid_ref[w, 0], grid_ref[w, 1]], 0)
        by_real = fine_dot(stacked, inverse_ref[w, 0])
        by_imag = fine_dot(stacked, inverse_ref[w, 1])
        theta_ref[w, 0] = (by_real[:rows] - by_imag[rows:]).astype(HALF)
        theta_ref[w, 1] = (by_imag[:rows] + by_real[rows:]).astype(HALF)


def narrow_rows(first, second, third):
    lane = lax.broadcasted_iota(jnp.int32, first.shape, 1)
    part = LANES // 4
    return (
        first,
        jnp.where(lane < part, pltpu.roll(first, part, 1), pltpu.roll(second, part, 1)),
        jnp.where(lane < 2 * part, pltpu.roll(second, 2 * part, 1), pltpu.roll(third, 2 * part, 1)),
        pltpu.roll(third, 3 * part, 1),
    )


def wide_lines(first, second, third, fourth):
    lane = lax.broadcasted_iota(jnp.int32, first.shape, 1)
    part = LANES // 4
    second, third = pltpu.roll(second, 3 * part, 1), pltpu.roll(third, 2 * part, 1)
    return (
        jnp.where(lane < 3 * part, first, second),
        jnp.where(lane < 2 * part, second, third),
        jnp.where(lane < part, third, pltpu.roll(fourth, part, 1)),
    )


def flatten_kernel(grid_ref, out_ref, rows_ref):
    count, _, rows, electrons = grid_ref.shape
    for w in range(count):
        for c in range(2):
            rows_ref[c, w * rows : (w + 1) * rows, :electrons] = grid_ref[w, c].astype(FULL)
    for c in range(2):
        for k in range(rows // 4):
            narrow = [rows_ref[c, pl.ds(4 * k + s, count, stride=rows)] for s in range(4)]
            for t, line in enumerate(wide_lines(*narrow)):
                out_ref[:, c, (3 * k + t) * LANES : (3 * k + t + 1) * LANES] = line


def lines_kernel(
    walkers_hbm, inverse_hbm, theta_ref, start_ref, walkers_ref, inverse_ref, rows_ref, semaphores
):
    first = pltpu.make_async_copy(walkers_hbm, walkers_ref, semaphores.at[0])
    first.start()
    copy = pltpu.make_async_copy(inverse_hbm, inverse_ref, semaphores.at[1])
    copy.start()
    first.wait()
    count, _, rows, electrons = theta_ref.shape
    for c in range(2):
        for k in range(rows // 4):
            lines = [
                walkers_ref[:, c, (3 * k + t) * LANES : (3 * k + t + 1) * LANES] for t in range(3)
            ]
            for s, narrow in enumerate(narrow_rows(*lines)):
                rows_ref[c, pl.ds(4 * k + s, count, stride=rows)] = narrow
    for w in range(count):
        for c in range(2):
            start_ref[w, c] = rows_ref[c, w * rows : (w + 1) * rows, :electrons].astype(HALF)
    copy.wait()
    for w in range(count):
        stacked = jnp.concatenate(
            [rows_ref[c, w * rows : (w + 1) * rows, :electrons] for c in range(2)], 0
        )
        by_real = fine_dot(stacked, inverse_ref[w, 0])
        by_imag = fine_dot(stacked, inverse_ref[w, 1])
        theta_ref[w, 0] = (by_real[:rows] - by_imag[rows:]).astype(HALF)
        theta_ref[w, 1] = (by_imag[:rows] + by_real[rows:]).astype(HALF)


def fill_spread(place_ref, own_ref, received_ref, spread_ref, values_ref):
    count, half = own_ref.shape
    height = count * TILE
    wide = LANES * TILE
    row = lax.broadcasted_iota(jnp.int32, (height, count), 0)
    column = lax.broadcasted_iota(jnp.int32, (height, count), 1)
    repeats = (row // TILE == column).astype(FULL).astype(HALF)
    low = place_ref[1] == 0
    own, received = own_ref[...].astype(FULL), received_ref[...].astype(FULL)
    values_ref[:, :half] = dot(repeats, jnp.where(low, own, received).astype(HALF)).astype(HALF)
    values_ref[:, half:] = dot(repeats, jnp.where(low, received, own).astype(HALF)).astype(HALF)
    row = lax.broadcasted_iota(jnp.int32, (LANES, wide), 0)
    column = lax.broadcasted_iota(jnp.int32, (LANES, wide), 1)
    copies = (column // TILE == row).astype(FULL).astype(HALF)
    a = lax.broadcasted_iota(jnp.int32, (TILE, wide), 0)
    b = lax.broadcasted_iota(jnp.int32, (TILE, wide), 1) % TILE
    keep = a == b

    @pl.loop(0, 2 * half // LANES)
    def _(block):
        values = values_ref[:, pl.ds(pl.multiple_of(block * LANES, LANES), LANES)]
        wider = dot(values, copies).reshape(count, TILE, wide)
        wider = jnp.where(keep[None], wider, 0.0).reshape(height, wide)
        spread_ref[:, pl.ds(pl.multiple_of(block * wide, wide), wide)] = wider.astype(HALF)


SCALARS = pl.BlockSpec(memory_space=pltpu.SMEM)
ARRAY = pl.BlockSpec(memory_space=VMEM)


def local_kernel(kernel, in_specs, out_shape, scratch_shapes=(), limit=TINY):
    return pl.pallas_call(
        kernel,
        in_specs=in_specs,
        out_specs=jax.tree.map(lambda _: ARRAY, out_shape),
        out_shape=out_shape,
        scratch_shapes=list(scratch_shapes),
        compiler_params=pltpu.CompilerParams(vmem_limit_bytes=limit),
    )


def wanted_walker(place_ref, source_ref, others_ref, i, population):
    local = source_ref.shape[0]
    walker = source_ref[i] if i < local else others_ref[i - local]
    relative = walker - place_ref[0]
    return walker, jnp.where(relative < 0, relative + population, relative)


def pick_kernel(place_ref, source_ref, own_ref, received_ref, keep_ref, send_ref, all_ref):
    local = own_ref.shape[0]
    population = all_ref.shape[0]
    all_ref[:local] = own_ref[...]
    all_ref[local:] = received_ref[...]
    for t in range(local // 2):
        for target_ref, core in ((keep_ref, place_ref[1]), (send_ref, 1 - place_ref[1])):
            relative = source_ref[2 * t + core] - place_ref[0]
            relative = jnp.where(relative < 0, relative + population, relative)
            target_ref[t, 0] = all_ref[relative]


def split_kernel(step, place_ref, own_ref, received_ref, keep_ref, send_ref):
    senders = own_ref.shape[1]
    bit = (place_ref[2] // step) % 2
    for t in range(own_ref.shape[0] // 2):
        for target_ref, side in ((keep_ref, bit), (send_ref, 1 - bit)):
            target_ref[t, :senders] = own_ref[2 * t + side]
            target_ref[t, senders:] = received_ref[2 * t + side]


def start_reading(pairs, semaphores):
    copies = []
    for source_ref, target_ref in pairs:
        height = target_ref.shape[0]
        size = 2 * LANES if height % (2 * LANES) == 0 else LANES
        for block in range(height // size):
            group = pl.ds(block * size, size)
            semaphore = semaphores.at[len(copies)]
            copy = pltpu.make_async_copy(source_ref.at[group], target_ref.at[group], semaphore)
            copy.start()
            copies.append(copy)
    return copies


def unit_of(field_hbm, target_ref, unit):
    height, tiles = target_ref.shape[:2]
    rows = pl.ds(unit % 2 * height, height)
    return field_hbm.at[rows, pl.ds(unit // 2 * tiles, tiles)], target_ref


def bias_kernel(place_ref, own_ref, received_ref, vectors_ref, keep_ref, send_ref):
    angles = jnp.concatenate([own_ref[...], received_ref[...]], 0)
    bias = dot(vectors_ref[...], angles, ((1,), (1,))).T
    half = bias.shape[1] // 2
    first, second = bias[:, :half], bias[:, half:]
    low = place_ref[1] == 0
    keep_ref[...] = jnp.where(low, first, second)
    send_ref[...] = jnp.where(low, second, first)


def late_kernel(order_ref, field_hbm, unit_ref, semaphores):
    for copy in start_reading([unit_of(field_hbm, unit_ref, 1)], semaphores):
        copy.wait()


def add_kernel(left_ref, right_ref, out_ref, rounded_ref):
    total = left_ref[...] + right_ref[...].astype(FULL)
    out_ref[...] = total
    rounded_ref[...] = total.astype(HALF)


def coefficient_kernel(
    place_ref, source_ref, others_ref, left_ref, right_ref, samples_ref, out_ref, bias_ref, row_ref
):
    bias_ref[...] = left_ref[...] + right_ref[...].astype(FULL)
    count, half = bias_ref.shape
    lanes = pl.ds(pl.multiple_of(place_ref[1] * half, LANES), half)
    for i in range(count // 2):
        walker, relative = wanted_walker(place_ref, source_ref, others_ref, i, count // 2)
        row_ref[2 * i : 2 * i + 1] = bias_ref[pl.ds(2 * relative + 1, 1)]
        drawn = samples_ref[pl.ds(walker, 1), lanes]
        row_ref[2 * i + 1 : 2 * i + 2] = drawn - bias_ref[pl.ds(2 * relative, 1)]
    out_ref[...] = row_ref[...].astype(HALF)


def read_kernel(half_hbm, field_hbm, half_ref, unit_ref, semaphores):
    pairs = [(half_hbm, half_ref), unit_of(field_hbm, unit_ref, 0)]
    for copy in start_reading(pairs, semaphores):
        copy.wait()


def read_early(half_vectors, tiled_vectors, unit_shape):
    return pl.pallas_call(
        read_kernel,
        in_specs=[pl.BlockSpec(memory_space=pl.ANY)] * 2,
        out_specs=[ARRAY] * 2,
        out_shape=[jax.ShapeDtypeStruct(half_vectors.shape, HALF), unit_shape],
        scratch_shapes=[
            pltpu.SemaphoreType.DMA(((half_vectors.shape[0] + unit_shape.shape[0]) // LANES,))
        ],
        compiler_params=pltpu.CompilerParams(vmem_limit_bytes=READ_LIMIT),
        name="read",
    )(half_vectors, tiled_vectors)


def field_kernel(part, wanted, mine, *refs):
    refs = list(refs)
    left_refs = [refs.pop(0) for _ in range(3 if part == 0 else 1)]
    unit_refs, field_hbm, own_ref, sent_ref = refs[:2], refs[2], refs[3], refs[4]
    refs = refs[5:]
    spread_ref = refs.pop(0) if part == 0 else left_refs[0]
    values_ref = refs.pop() if part == 0 else None
    copies = []
    if wanted:
        semaphores = refs.pop()
        pairs = [unit_of(field_hbm, ref, unit) for ref, unit in zip(refs, wanted)]
        copies = start_reading(pairs, semaphores)
    if part == 0:
        fill_spread(*left_refs, spread_ref, values_ref)
    height, tiles, _, orbitals = unit_refs[0].shape
    count = spread_ref.shape[0] // TILE
    depth = height * TILE
    total = None
    for block, unit_ref in enumerate(unit_refs):
        right = jnp.concatenate(
            [unit_ref[:, t].reshape(depth, orbitals) for t in range(tiles)], 1
        )
        product = dot(spread_ref[:, block * depth : (block + 1) * depth], right)
        total = product if total is None else total + product
    for t in range(tiles):
        slab = total[:, t * orbitals : (t + 1) * orbitals].reshape(count, TILE, orbitals)
        own_ref[:, t * TILE : (t + 1) * TILE] = slab[:mine].astype(HALF)
        sent_ref[:, t * TILE : (t + 1) * TILE] = slab[mine:].astype(HALF)
    for copy in copies:
        copy.wait()


def field_rows(left, units, tiled_vectors, part, wanted, count, mine):
    height, tiles, _, orbitals = units[0].shape
    vectors = 2 * height
    rows = tiles * TILE
    out_shape = [
        jax.ShapeDtypeStruct((mine, rows, orbitals), HALF),
        jax.ShapeDtypeStruct((count - mine, rows, orbitals), HALF),
    ]
    if part == 0:
        out_shape.append(jax.ShapeDtypeStruct((count * TILE, vectors * TILE), HALF))
    out_shape += [jax.ShapeDtypeStruct(units[0].shape, HALF) for _ in wanted]
    scratch = []
    if wanted:
        scratch.append(pltpu.SemaphoreType.DMA((len(wanted) * height // LANES,)))
    if part == 0:
        scratch.append(VMEM((count * TILE, vectors), HALF))
    left_specs = [SCALARS, ARRAY, ARRAY] if part == 0 else [ARRAY]
    own, sent, *rest = pl.pallas_call(
        functools.partial(field_kernel, part, wanted, mine),
        in_specs=left_specs + [ARRAY] * 2 + [pl.BlockSpec(memory_space=pltpu.HBM)],
        out_specs=[ARRAY] * len(out_shape),
        out_shape=out_shape,
        scratch_shapes=scratch,
        compiler_params=pltpu.CompilerParams(vmem_limit_bytes=SMALL),
        cost_estimate=pl.CostEstimate(
            flops=2 * count * TILE * vectors * rows * orbitals,
            bytes_accessed=2 * vectors * rows * orbitals,
            transcendentals=0,
        ),
        name="field",
    )(*left, *units, tiled_vectors)
    left = [rest.pop(0)] if part == 0 else left
    return own, sent, left, rest


def combine_kernel(chunks, *refs):
    own_refs, received_refs, out_ref = refs[:chunks], refs[chunks:-1], refs[-1]
    others = len(received_refs) // chunks
    rows = own_refs[0].shape[2]
    for c in range(chunks):
        total = own_refs[c][...].astype(FULL)
        for received_ref in received_refs[c * others : (c + 1) * others]:
            total = total + received_ref[...].astype(FULL)
        out_ref[:, :, c * rows : (c + 1) * rows] = total.astype(HALF)


def combine(owns, received):
    chunks = len(owns)
    slots, parts, rows, orbitals = owns[0].shape
    return pl.pallas_call(
        functools.partial(combine_kernel, chunks),
        out_shape=jax.ShapeDtypeStruct((slots, parts, rows * chunks, orbitals), HALF),
        in_specs=[pl.BlockSpec(memory_space=VMEM)] * (chunks + len(received)),
        out_specs=pl.BlockSpec(memory_space=VMEM),
        compiler_params=pltpu.CompilerParams(vmem_limit_bytes=SMALL),
        name="combine",
    )(*owns, *received)


def walker_kernel(count, orbitals, electrons, rank_ref, field_ref, *refs):
    start_refs = refs[:count]
    out_ref, start_wide_ref = refs[count:]
    blocks, _, rows, _ = field_ref.shape
    wide = start_wide_ref.shape[1] // 2
    start_wide_ref[...] = jnp.zeros_like(start_wide_ref)
    block = 0
    for start_ref in start_refs:
        for d in range(start_ref.shape[0]):
            at = pl.multiple_of((rank_ref[0] ^ block) * rows, 2 * TILE)
            for c in range(2):
                start_wide_ref[pl.ds(at, rows), pl.ds(c * wide, electrons)] = start_ref[d, c]
            block += 1
    current = start_wide_ref[...]
    summed = current.astype(FULL)
    for order in range(1, TERMS + 1):
        product = dot(field_ref[...].reshape(2 * orbitals, orbitals), current)
        product = product.reshape(blocks, 2, rows, 2 * wide)
        top = product[:, 0].reshape(orbitals, 2 * wide)
        low = product[:, 1].reshape(orbitals, 2 * wide)
        following = jnp.concatenate(
            [top[:, :wide] - low[:, wide:], top[:, wide:] + low[:, :wide]], 1
        )
        following = following * (1.0 / order)
        summed = summed + following
        current = following.astype(HALF)

    rounded = summed.astype(HALF)
    gram = dot(rounded, rounded, ((0,), (0,)))
    gram_real = (gram[:wide, :wide] + gram[wide:, wide:]) * (1.0 / orbitals)
    gram_imag = (gram[:wide, wide:] - gram[wide:, :wide]) * (1.0 / orbitals)
    row = lax.broadcasted_iota(jnp.int32, (wide, wide), 0)
    column = lax.broadcasted_iota(jnp.int32, (wide, wide), 1)
    identity = jnp.where((row == column) & (row < electrons), 1.0, 0.0)
    scale = jnp.sum(gram_real * identity, axis=0, keepdims=True)
    scale = jnp.sum(scale, axis=1, keepdims=True) * (1.0 / electrons)

    def times(left, right):
        product = fine_dot(jnp.concatenate(left, 0), jnp.concatenate(right, 1))
        real = product[:wide, :wide] - product[wide:, wide:]
        return real, product[:wide, wide:] + product[wide:, :wide]

    iterate = (gram_real / scale, gram_imag / scale)
    root = None
    for sweep in range(NS_STEPS):
        real, imag = iterate if root is None else times(root, iterate)
        step = (1.5 * identity - 0.5 * real, -0.5 * imag)
        if sweep + 1 < NS_STEPS:
            iterate = times(iterate, step)
        root = step if root is None else times(step, root)
    inverse = lax.rsqrt(scale)
    root = jnp.concatenate([root[0] * inverse, root[1] * inverse], 1)
    product = dot(jnp.concatenate([rounded[:, :wide], rounded[:, wide:]], 0), root.astype(HALF))
    top, low = product[:orbitals], product[orbitals:]
    real = (top[:, :wide] - low[:, wide:]).astype(HALF)
    imag = (top[:, wide:] + low[:, :wide]).astype(HALF)
    for r in range(blocks):
        out_ref[r, 0] = real[r * rows : (r + 1) * rows, :electrons]
        out_ref[r, 1] = imag[r * rows : (r + 1) * rows, :electrons]


def walker_step(rank, field, starts):
    blocks, parts, rows, orbitals = field.shape
    electrons = starts[0].shape[3]
    wide = -(-electrons // LANES) * LANES
    return local_kernel(
        functools.partial(walker_kernel, len(starts), orbitals, electrons),
        [SCALARS] + [ARRAY] * (1 + len(starts)),
        jax.ShapeDtypeStruct((blocks, parts, rows, electrons), HALF),
        [VMEM((orbitals, 2 * wide), HALF)],
        SMALL,
    )(rank, field, *starts)


def shift(value, axis, step):
    size = lax.axis_size(axis)
    return lax.ppermute(value, axis, [(i, (i + step) % size) for i in range(size)])


def scatter_sum(value, axis, dim):
    size = lax.axis_size(axis)
    here = lax.axis_index(axis)
    width = value.shape[dim] // size
    total = lax.dynamic_slice_in_dim(value, here * width, width, dim)
    for s in range(1, size):
        block = lax.dynamic_slice_in_dim(value, ((here + s) % size) * width, width, dim)
        total = total + shift(block, axis, s)
    return total


def gather_ordered(value, axis, dim):
    size = lax.axis_size(axis)
    here = lax.axis_index(axis)
    width = value.shape[dim]
    shape = list(value.shape)
    shape[dim] = width * size
    whole = jnp.zeros(shape, value.dtype)
    for s in range(size):
        block = value if s == 0 else shift(value, axis, s)
        whole = lax.dynamic_update_slice_in_dim(whole, block, ((here - s) % size) * width, dim)
    return whole


def exchange_sum(value, axis):
    size = lax.axis_size(axis)
    if size & (size - 1):
        return sum([shift(value, axis, s) for s in range(1, size)], value)
    step = 1
    while step < size:
        value = value + lax.ppermute(value, axis, [(i, i ^ step) for i in range(size)])
        step *= 2
    return value


def whole_step(walkers, correlation_inverse, half_vectors, field_vectors, samples, source):
    local = walkers.shape[0]
    vectors, row_block, orbitals = field_vectors.shape
    electrons = correlation_inverse.shape[2]
    planes = lax.axis_size("walk")
    population = local * planes
    count = population * 2
    devices_rows = lax.axis_size(ROWS)
    sharers = devices_rows // local
    first = lax.axis_index("walk") * local
    core = lax.axis_index("orb")
    chol = lax.axis_size("chol")
    half = vectors // 2
    fast = (
        row_block % (2 * TILE) == 0
        and vectors % (2 * LANES) == 0
        and lax.axis_size("orb") == 2
        and planes > 1
        and sharers == 1
        and chol & (chol - 1) == 0
    )

    def to_owners(value):
        value = jnp.broadcast_to(value[:, None], (local, sharers) + value.shape[1:])
        value = value.reshape((devices_rows,) + value.shape[2:])
        return lax.all_to_all(value, ROWS, split_axis=0, concat_axis=0, tiled=True)

    def others(value):
        return jnp.concatenate([shift(value, "walk", -s) for s in range(1, planes)], 0)

    def from_planes(sent):
        blocks = [sent[s * local : (s + 1) * local] for s in range(planes - 1)]
        return [shift(block, "walk", s + 1) for s, block in enumerate(blocks)]

    other_source = others(source)
    place = jnp.stack([first, core, lax.axis_index("chol")]).astype(jnp.int32)
    rank = lax.axis_index(ROWS).astype(jnp.int32).reshape(1)
    grid_shape = (local, 2, row_block, electrons)
    half_grid = jax.ShapeDtypeStruct(grid_shape, HALF)
    if fast and 4 * electrons == 3 * LANES and row_block % TILE == 0:
        theta, start = local_kernel(
            lines_kernel,
            [pl.BlockSpec(memory_space=pltpu.HBM)] * 2,
            [half_grid] * 2,
            [
                VMEM(walkers.shape, FULL),
                VMEM(correlation_inverse.shape, FULL),
                VMEM((2, local * row_block, LANES), FULL),
                pltpu.SemaphoreType.DMA((2,)),
            ],
            LINES_LIMIT,
        )(walkers, correlation_inverse)
    else:
        grid = walkers.reshape(grid_shape)
        start = grid.astype(HALF)
        theta = local_kernel(theta_kernel, [ARRAY] * 2, half_grid, limit=SMALL)(
            grid, correlation_inverse
        )
    theta = theta.reshape(local * 2, row_block * electrons)
    other_theta = others(theta)
    other_start = others(start)

    if fast:
        tiled_vectors = field_vectors.reshape(vectors, row_block // TILE, TILE, orbitals)
        unit_shape = jax.ShapeDtypeStruct((half, 2, TILE, orbitals), HALF)
        half_vectors, unit = read_early(half_vectors, tiled_vectors, unit_shape)
        block = (2, row_block, electrons)
        slots = jax.ShapeDtypeStruct((local // 2, 1) + block, HALF)
        keep, sent = local_kernel(
            pick_kernel,
            [SCALARS] * 2 + [ARRAY] * 2,
            [slots] * 2,
            [VMEM((population,) + block, HALF)],
        )(place, source, start, other_start)
        passed = shift(sent, "orb", 1)
        part_shape = jax.ShapeDtypeStruct((count, half), FULL)
        bias, sent = local_kernel(
            bias_kernel, [SCALARS] + [ARRAY] * 3, [part_shape, part_shape], limit=SMALL
        )(place, theta, other_theta, half_vectors)
        hbm = pl.BlockSpec(memory_space=pltpu.HBM)
        received = shift(sent, "orb", 1)
        rounded_shape = jax.ShapeDtypeStruct(part_shape.shape, HALF)
        add = local_kernel(add_kernel, [ARRAY] * 2, [part_shape, rounded_shape])
        step = 1
        while step < chol:
            pairs = [(i, i ^ step) for i in range(chol)]
            bias, rounded = add(bias, received)
            received = lax.ppermute(rounded, "chol", pairs)
            slots = jax.ShapeDtypeStruct((keep.shape[0] // 2, keep.shape[1] * 2) + block, HALF)
            keep, sent = local_kernel(
                functools.partial(split_kernel, step), [SCALARS] + [ARRAY] * 2, [slots] * 2
            )(place, keep, passed)
            passed = lax.ppermute(sent, "chol", pairs)
            step *= 2
        other_unit = local_kernel(
            late_kernel,
            [hbm, hbm],
            unit_shape,
            [pltpu.SemaphoreType.DMA((half // LANES,))],
            3 * SMALL,
        )(bias, tiled_vectors)
        units = [unit, other_unit]
        coefficient = local_kernel(
            coefficient_kernel,
            [SCALARS] * 3 + [ARRAY] * 3,
            jax.ShapeDtypeStruct((count, half), HALF),
            [VMEM((count, half), FULL)] * 2,
        )(place, source, other_source, bias, received, samples)
        other_half = shift(coefficient, "orb", 1)
        rows = 2 * TILE
        parts = row_block // rows
        owns, received = [], []
        left = [place, coefficient, other_half]
        for part in range(parts):
            have = 2 * part + len(units)
            wanted = range(have, max(have, min(2 * parts, 2 * part + 5)))
            own, sent, left, further = field_rows(
                left, units[:2], tiled_vectors, part, wanted, count, local * 2
            )
            units = units[2:] + further
            owns.append(own.reshape(local, 2, rows, orbitals))
            sent = sent.reshape(population - local, 2, rows, orbitals)
            received += from_planes(sent)
        field = to_owners(combine(owns, received))
        starts = [keep[0], passed[0]]
    else:
        wanted = jnp.concatenate([source, other_source], 0)
        relative = jnp.where(wanted < first, wanted - first + population, wanted - first)
        all_start = jnp.concatenate([start, other_start], 0)
        picked = all_start.at[relative[:local]].get(mode="promise_in_bounds")
        columns = to_owners(picked)
        angles = jnp.concatenate([theta, other_theta], 0)
        bias = jnp.einsum("ij,gj->ig", angles, half_vectors, preferred_element_type=FULL)
        bias = bias.reshape(population, 2, vectors)
        bias = exchange_sum(scatter_sum(bias, "orb", 2), "chol")
        bias = bias.at[relative].get(mode="promise_in_bounds")
        width = bias.shape[2]
        drawn = lax.dynamic_slice_in_dim(samples, core * width, width, 1)
        drawn = drawn.at[wanted].get(mode="promise_in_bounds")
        coefficient = jnp.stack([bias[:, 1], drawn - bias[:, 0]], 1).astype(HALF)
        coefficient = gather_ordered(coefficient, "orb", 2)
        field = jnp.einsum(
            "wcg,gab->wcab", coefficient, field_vectors, preferred_element_type=FULL
        )
        total = field[:local]
        for block in from_planes(field[local:].astype(HALF)):
            total = total + block
        field = to_owners(total.astype(HALF)).transpose(1, 0, 2, 3)
        field = field.reshape(1, 2, orbitals, orbitals)
        starts = [columns.transpose(1, 0, 2, 3).reshape(1, 2, orbitals, electrons)]
        rank = jnp.zeros((1,), jnp.int32)

    normalized = walker_step(rank, field, starts)
    if not fast:
        normalized = normalized.reshape(2, devices_rows, row_block, electrons)
        normalized = normalized.transpose(1, 0, 2, 3)
    if sharers > 1:
        share = lax.axis_index(ROWS) % sharers
        width = electrons // sharers
        normalized = lax.dynamic_slice_in_dim(normalized, share * width, width, 3)
    returned = lax.all_to_all(normalized, ROWS, split_axis=0, concat_axis=0, tiled=True)
    if fast and 4 * electrons == 3 * LANES and row_block % TILE == 0:
        return local_kernel(
            flatten_kernel,
            [ARRAY],
            jax.ShapeDtypeStruct(walkers.shape, FULL),
            [VMEM((2, local * row_block, LANES), FULL)],
        )(returned)
    if sharers > 1:
        returned = returned.reshape(local, sharers, 2, row_block, width)
        returned = returned.transpose(0, 2, 3, 1, 4)
    return returned.reshape(local, 2, row_block * electrons).astype(FULL)


def solution(mesh):
    placed = (
        P(("groups", "walk"), None, ("chol", "orb")),
        P(("groups", "walk"), None, None, None),
        P(("groups", "walk"), ("chol", "orb")),
        P(("groups", "walk"), ("chol", "orb"), None),
        P("groups", "walk"),
        P(("groups", "walk")),
    )
    return jax.shard_map(
        whole_step,
        mesh=mesh,
        in_specs=placed,
        out_specs=P(("groups", "walk"), None, ("chol", "orb")),
        check_vma=False,
    )
```
